32 devices in a mesh: dp: 16 (over z, x, core), tensor: 2 (over y).
Axes of the slice: x: 2, y: 2, z: 4, core: 2. Of those that a mesh axis runs over, the one named last changes fastest.
Arguments:
- tokens: bfloat16 [10240, 2048], P(('dp', 'tensor')), may hold values from -6 to 6
- cotangent: bfloat16 [10240, 2048], P(('dp', 'tensor')), may hold values from -6 to 6
- cont_ids: int32 [16, 512], P('dp'), may hold values from 0 to 3, never falling along the last dimension, each value on 1 to 256 neighbouring positions
- q_weight: bfloat16 [2048, 2048], P('dp', 'tensor'), may hold values from -0.125 to 0.125
- k_weight: bfloat16 [2048, 2048], P('dp', 'tensor'), may hold values from -0.125 to 0.125
- v_weight: bfloat16 [2048, 2048], P('dp', 'tensor'), may hold values from -0.125 to 0.125
- out_weight: bfloat16 [2048, 2048], P('dp', 'tensor'), may hold values from -0.125 to 0.125
- attn_gain: bfloat16 [2048], P('dp'), may hold values from 0.25 to 1.75
- head_gain: bfloat16 [256, 8], P('dp', 'tensor'), may hold values from 0.25 to 1.75
- lam_q1: bfloat16 [128, 8], P('dp', 'tensor'), may hold values from -1 to 1
- lam_k1: bfloat16 [128, 8], P('dp', 'tensor'), may hold values from -1 to 1
- lam_q2: bfloat16 [128, 8], P('dp', 'tensor'), may hold values from -1 to 1
- lam_k2: bfloat16 [128, 8], P('dp', 'tensor'), may hold values from -1 to 1
- gate_weight: bfloat16 [2048, 5632], P('dp', 'tensor'), may hold values from -0.125 to 0.125
- up_weight: bfloat16 [2048, 5632], P('dp', 'tensor'), may hold values from -0.125 to 0.125
- down_weight: bfloat16 [2048, 5632], P('dp', 'tensor'), may hold values from -0.078125 to 0.078125
- ffn_gain: bfloat16 [2048], P('dp'), may hold values from 0.25 to 1.75
Outputs:
- output: bfloat16 [10240, 2048], P(('dp', 'tensor'))
- tokens_grad: bfloat16 [10240, 2048], P(('dp', 'tensor'))
- grad_q: float32 [2048, 2048], P('dp', 'tensor')
- grad_k: float32 [2048, 2048], P('dp', 'tensor')
- grad_v: float32 [2048, 2048], P('dp', 'tensor')
- grad_out: float32 [2048, 2048], P('dp', 'tensor')
- grad_attn_gain: float32 [2048], P('dp')
- grad_head_gain: float32 [256, 8], P('dp', 'tensor')
- grad_lam_q1: float32 [128, 8], P('dp', 'tensor')
- grad_lam_k1: float32 [128, 8], P('dp', 'tensor')
- grad_lam_q2: float32 [128, 8], P('dp', 'tensor')
- grad_lam_k2: float32 [128, 8], P('dp', 'tensor')
- grad_gate: float32 [2048, 5632], P('dp', 'tensor')
- grad_up: float32 [2048, 5632], P('dp', 'tensor')
- grad_down: float32 [2048, 5632], P('dp', 'tensor')
- grad_ffn_gain: float32 [2048], P('dp')
The draws below stay inside these ranges and needn't reach their ends.
Inputs may be any that keep to these rules, and one draw needn't show every extreme that they name: `cont_ids`: in each row the ids never fall; each of the 4 continuations holds 1 to 256 tokens, and one continuation of each row holds exactly 256.
All inputs are finite; a program needn't handle non-finite values.
Results may differ from the reference program's by a relative error of at most 0.01345.
The reference program's roundings to bfloat16 on the way count: a program that leaves them out, or rounds other values in their place, can miss the bound.
Values may be sent and summed in bfloat16 or wider, within the bound.
No kernel may reach another device: no remote copies, remote signals or barrier semaphores. Data moves between devices by JAX's collectives and lax.ppermute only.
A program may use at most 320 MiB of HBM per device.

```python
import math
import jax
import jax.numpy as jnp
import numpy as np
from jax import lax

D = 2048
H = 8
DK = 128
DV = 256
FF = 5632
PROMPT = 2048
CONT_DEV = 512
SEGS = 4
CMAX = 256
TOKENS = 10240
N_DP = 16


def raised(result, stream_key, source, target, shards_of, factor):
    def block_of(axis_at):
        return (jnp.arange(result.shape[axis_at]) // (result.shape[axis_at] // shards_of)).reshape((-1,) + (1,) * (result.ndim - 1 - axis_at))

    one_side = jax.random.permutation(stream_key, shards_of)[block_of(target)]
    far = (block_of(target) + shards_of // 2) % shards_of
    return jnp.where((block_of(source) == one_side) | (block_of(source) == far), factor * result, result)


def levels(own_key, dims, cuts, smallest, high):
    def one(dim, blocks):
        draws = jax.random.uniform(jax.random.fold_in(jax.random.fold_in(own_key, 6), dim), (blocks,), jnp.float32, smallest / len(cuts), high / len(cuts))
        return jnp.repeat(jnp.exp(draws), dims[dim] // blocks).reshape((-1,) + (1,) * (len(dims) - dim - 1))

    gain = one(*cuts[0])
    for cut in cuts[1:]:
        gain = gain * one(*cut)
    return gain


def length_profile(number_of, total, limit, lean):
    portions = [(1 << 20) // math.isqrt(rank ** lean) + 1 for rank in range(2, number_of + 1)]
    surplus, given = total - limit - (number_of - 1), [1] * (number_of - 1)
    while surplus > 0:
        free = [i for i in range(number_of - 1) if given[i] < limit]
        pool, remaining = sum([portions[i] for i in free]), surplus
        for i in free:
            addition = min(limit - given[i], max(1, remaining * portions[i] // pool), surplus)
            given[i] = given[i] + addition
            surplus = surplus - addition
    return np.array([limit] + given)


def ragged(stream_key, count, total, bound, slope):
    if count == 2:
        one = jax.random.randint(stream_key, (), max(1, total - bound), min(bound, total - 1) + 1)
        return jnp.stack([one, total - one])
    tallies = jnp.asarray(length_profile(count, total, bound, slope), jnp.int32)
    twos = (count - 1) // 2
    giver, sink = tallies[1:1 + 2 * twos:2], tallies[2:2 + 2 * twos:2]
    slack = jnp.minimum(giver - 1, bound - sink)
    shifted = jax.random.randint(jax.random.fold_in(stream_key, 1), (twos,), 0, 1 << 20) % (slack + 1)
    tallies = tallies.at[1:1 + 2 * twos:2].set(giver - shifted).at[2:2 + 2 * twos:2].set(sink + shifted)
    return tallies[jax.random.permutation(jax.random.fold_in(stream_key, 2), count)]


def noise(own_key, shape, deviation, limit, split=(), kind=jnp.bfloat16):
    result = jax.random.normal(own_key, shape, jnp.float32) * deviation
    if len(split) > 0:
        result = levels(own_key, shape, split, -0.22, 0.18) * result
    return jnp.clip(result, min=-limit, max=limit).astype(kind)


def heavy_noise(rng, shape, width, most, split, heavy, kind=jnp.bfloat16):
    result = width * jax.random.normal(rng, shape, jnp.float32)
    if split:
        result = result * levels(rng, shape, split, -0.22, 0.18)
    return jnp.clip(raised(result, jax.random.fold_in(rng, 3), *heavy), -most, most).astype(kind)


def setup_inputs(seed: int = 0) -> dict:
    key_of = jax.random.split(jax.random.key(seed), 18)
    return {
        "tokens": heavy_noise(key_of[0], (TOKENS, D), 1.0, 6.0, ((0, 32),), (0, 1, 32, 2.75)),
        "cotangent": heavy_noise(key_of[1], (TOKENS, D), 1.0, 6.0, ((0, 32),), (0, 1, 32, 2.75)),
        "cont_ids": jax.vmap(lambda own: jnp.searchsorted(jnp.cumsum(ragged(own, SEGS, CONT_DEV, CMAX, 1)), jnp.arange(CONT_DEV), side="right"))(jax.random.split(key_of[2], N_DP)).reshape((N_DP, CONT_DEV)).astype(jnp.int32),
        "q_weight": noise(key_of[3], (D, H * 2 * DK), D ** -0.5, 0.125, ((0, 16), (1, 2))),
        "k_weight": noise(key_of[4], (D, H * 2 * DK), D ** -0.5, 0.125, ((0, 16), (1, 2))),
        "v_weight": noise(key_of[5], (D, H * DV), D ** -0.5, 0.125, ((0, 16), (1, 2))),
        "out_weight": noise(key_of[6], (D, H * DV), (H * DV) ** -0.5, 0.125, ((0, 16), (1, 2))),
        "attn_gain": jnp.clip(1.0 + 0.15 * jax.random.normal(key_of[7], (D,), jnp.float32), 0.25, 1.75).astype(jnp.bfloat16),
        "head_gain": jnp.clip(1.0 + 0.15 * jax.random.normal(key_of[8], (DV, H), jnp.float32), 0.25, 1.75).astype(jnp.bfloat16),
        "lam_q1": noise(key_of[9], (DK, H), 0.2, 1.0, ((0, 16), (1, 2))),
        "lam_k1": noise(key_of[10], (DK, H), 0.2, 1.0, ((0, 16), (1, 2))),
        "lam_q2": noise(key_of[11], (DK, H), 0.2, 1.0, ((0, 16), (1, 2))),
        "lam_k2": noise(key_of[12], (DK, H), 0.2, 1.0, ((0, 16), (1, 2))),
        "gate_weight": noise(key_of[13], (D, FF), D ** -0.5, 0.125, ((0, 16), (1, 2))),
        "up_weight": noise(key_of[14], (D, FF), D ** -0.5, 0.125, ((0, 16), (1, 2))),
        "down_weight": noise(key_of[15], (D, FF), FF ** -0.5, 0.078125, ((0, 16), (1, 2))),
        "ffn_gain": jnp.clip(1.0 + 0.15 * jax.random.normal(key_of[16], (D,), jnp.float32), 0.25, 1.75).astype(jnp.bfloat16),
    }


@jax.custom_vjp
def low(v):
    return lax.optimization_barrier(v.astype(jnp.bfloat16)).astype(jnp.float32)

@jax.custom_vjp
def low_back(v):
    return v

def low_keep(v):
    return (low(v), None)

def low_pass(kept, grad):
    return (grad,)

def back_keep(v):
    return (v, None)

def back_low(kept, grad):
    return (low(grad),)
low.defvjp(low_keep, low_pass)
low_back.defvjp(back_keep, back_low)
norm_eps = 1e-06
head_eps = 1e-05
lambda_init = 0.2
masked_value = -1e+30

def inv_rms(entries, eps_value):
    return lax.rsqrt(lax.optimization_barrier(jnp.mean(entries * entries, axis=-1, keepdims=True)) + eps_value)

def wide_dot(first_arg, second_arg):
    return jnp.dot(first_arg, second_arg, precision=lax.Precision.HIGHEST)

def both_ways(entries):
    return low_back(low(entries))

def key_mask(block_rows, prompt_part, prompt_len, cont_row_ids, block_index):
    row_index = lax.broadcasted_iota(jnp.int32, (block_rows, 1), 0)
    prompt_key = lax.broadcasted_iota(jnp.int32, (1, prompt_len), 1)
    position = block_index * prompt_part + row_index
    prompt_cols = jnp.where(row_index < prompt_part, prompt_key <= position, True)
    cont_len = cont_row_ids.shape[0]
    cont_key = lax.broadcasted_iota(jnp.int32, (1, cont_len), 1)
    row_ids = jnp.concatenate([jnp.full((prompt_part,), -1, jnp.int32), cont_row_ids.astype(jnp.int32)])[:, None]
    cont_cols = (row_ids == cont_row_ids.astype(jnp.int32)[None, :]) & (cont_key <= row_index - prompt_part)
    return jnp.concatenate([prompt_cols, cont_cols], axis=1)

def layer_forward(param_list, cont_ids):
    tokens, q_weight, k_weight, v_weight, out_weight, attn_gain, head_gain, lam_q1, lam_k1, lam_q2, lam_k2, gate_weight, up_weight, down_weight, ffn_gain = param_list
    prompt_part = PROMPT // N_DP
    block_rows = prompt_part + CONT_DEV
    score_scale = DK ** (-0.5)
    normed = low(tokens * inv_rms(tokens, norm_eps) * attn_gain)
    queries = both_ways(wide_dot(normed, q_weight)).reshape(N_DP, block_rows, H, 2, DK)
    keys_all = both_ways(wide_dot(normed, k_weight)).reshape(N_DP, block_rows, H, 2, DK)
    values_all = both_ways(wide_dot(normed, v_weight)).reshape(N_DP, block_rows, H, DV)
    prompt_keys = keys_all[:, :prompt_part].reshape(PROMPT, H, 2, DK)
    prompt_values = values_all[:, :prompt_part].reshape(PROMPT, H, DV)
    lam_vec = jnp.exp(lax.optimization_barrier(jnp.sum(lam_q1 * lam_k1, axis=0))) - jnp.exp(lax.optimization_barrier(jnp.sum(lam_q2 * lam_k2, axis=0))) + lambda_init

    def attend(pieces):
        query_block, cont_keys, cont_values, row_ids, block_index = pieces
        key_block = jnp.concatenate([prompt_keys, cont_keys], axis=0)
        value_block = jnp.concatenate([prompt_values, cont_values], axis=0)
        allowed = key_mask(block_rows, prompt_part, PROMPT, row_ids, block_index)
        scores = jnp.einsum('qhcd,khcd->hcqk', query_block, key_block, precision=lax.Precision.HIGHEST) * score_scale
        scores = low_back(scores)
        scores = jnp.where(allowed[None, None], scores, masked_value)
        row_top = lax.optimization_barrier(jnp.max(scores, axis=-1, keepdims=True))
        exp_terms = jnp.exp(scores - row_top)
        weights = exp_terms / lax.optimization_barrier(jnp.sum(exp_terms, axis=-1, keepdims=True))
        mixed_map = low(weights[:, 0] - lam_vec[:, None, None] * weights[:, 1])
        heads_out = low_back(jnp.einsum('hqk,khd->qhd', mixed_map, value_block, precision=lax.Precision.HIGHEST))
        return heads_out * inv_rms(heads_out, head_eps) * head_gain.T[None] * (1.0 - lambda_init)
    per_block = lax.map(jax.checkpoint(attend), (queries, keys_all[:, prompt_part:], values_all[:, prompt_part:], cont_ids, jnp.arange(N_DP, dtype=jnp.int32)))
    attn_vec = low(per_block.reshape(TOKENS, H * DV))
    residual = tokens + low_back(wide_dot(attn_vec, out_weight.T))
    ffn_in = low(residual * inv_rms(residual, norm_eps) * ffn_gain)
    gate_proj = low_back(wide_dot(ffn_in, gate_weight))
    up_proj = low_back(wide_dot(ffn_in, up_weight))
    hidden = low(jax.nn.silu(gate_proj) * up_proj)
    return residual + low_back(wide_dot(hidden, down_weight.T))

def reference(tokens, cotangent, cont_ids, q_weight, k_weight, v_weight, out_weight, attn_gain, head_gain, lam_q1, lam_k1, lam_q2, lam_k2, gate_weight, up_weight, down_weight, ffn_gain):
    param_list = (tokens, q_weight, k_weight, v_weight, out_weight, attn_gain, head_gain, lam_q1, lam_k1, lam_q2, lam_k2, gate_weight, up_weight, down_weight, ffn_gain)
    floats = tuple((entry.astype(jnp.float32) for entry in param_list))

    def forward(float_list):
        return layer_forward(float_list, cont_ids)
    output, pull_back = jax.vjp(forward, floats)
    grad_list = pull_back(cotangent.astype(jnp.float32))[0]
    return (output.astype(jnp.bfloat16), grad_list[0].astype(jnp.bfloat16), grad_list[1], grad_list[2], grad_list[3], grad_list[4], grad_list[5], grad_list[6], grad_list[7], grad_list[8], grad_list[9], grad_list[10], grad_list[11], grad_list[12], grad_list[13], grad_list[14])
```

```python
import jax
import jax.numpy as jnp
from jax import lax
from jax.sharding import PartitionSpec as P

D = 2048
DK = 128
DV = 256

norm_eps = 1e-06
head_eps = 1e-05
lambda_init = 0.2
masked_value = -1e30
f32 = jnp.float32
bf16 = jnp.bfloat16


def inv_rms(entries, eps_value):
    return lax.rsqrt(jnp.mean(entries * entries, axis=-1, keepdims=True) + eps_value)


def norm_back(entries, inverse, gain_row, incoming):
    scaled = gain_row * incoming
    return inverse * scaled - entries * inverse**3 * jnp.mean(
        entries * scaled, axis=-1, keepdims=True
    )


def plain_product(first_arg, second_arg):
    return jnp.dot(first_arg, second_arg, preferred_element_type=f32)


def rows_product(first_arg, second_arg):
    return lax.dot_general(
        first_arg, second_arg, (((0,), (0,)), ((), ())), preferred_element_type=f32
    )


def cols_product(first_arg, second_arg):
    return lax.dot_general(
        first_arg, second_arg, (((1,), (1,)), ((), ())), preferred_element_type=f32
    )


class Places:
    def __init__(self):
        self.count = lax.axis_size("dp")
        self.upper = self.count // 4
        index = lax.axis_index("dp")
        self.index = index
        self.core = index % 2
        self.side = (index // 2) % 2
        self.tensor = lax.axis_index("tensor")
        self.upper_groups = [
            [low + 4 * high for high in range(self.upper)] for low in range(4)
        ]
        self.core_pairs = [(k, k ^ 1) for k in range(self.count)]
        self.side_pairs = [(k, k ^ 2) for k in range(self.count)]

    def swap_core(self, value):
        return lax.ppermute(value, "dp", self.core_pairs)

    def swap_side(self, value):
        return lax.ppermute(value, "dp", self.side_pairs)

    def swap_tensor(self, value):
        return lax.ppermute(value, "tensor", [(0, 1), (1, 0)])

    def gather(self, shard):
        here = lax.all_gather(
            shard, "dp", axis=0, tiled=True, axis_index_groups=self.upper_groups
        )
        aside = self.swap_side(here)
        return jnp.concatenate(
            [here, aside, self.swap_core(here), self.swap_core(aside)], axis=0
        )

    def scatter_upper(self, value):
        return lax.psum_scatter(
            value, "dp", scatter_dimension=0, tiled=True, axis_index_groups=self.upper_groups
        )

    def scatter_product(self, first_arg, second_arg):
        width = first_arg.shape[1]
        half, quarter = width // 2, width // 4
        far = self.swap_core(rows_product(first_arg[:, half:], second_arg).astype(bf16))
        aside = rows_product(first_arg[:, quarter:half], second_arg) + far[quarter:].astype(f32)
        aside = self.swap_side(aside.astype(bf16))
        near = rows_product(first_arg[:, :quarter], second_arg) + far[:quarter].astype(f32)
        near = (near + aside.astype(f32)).astype(bf16)
        return self.scatter_upper(near)

    def scatter_rows(self, value):
        half, quarter = value.shape[0] // 2, value.shape[0] // 4
        far = self.swap_core(value[half:])
        near = (value[:half].astype(f32) + far.astype(f32)).astype(bf16)
        aside = self.swap_side(near[quarter:])
        near = (near[:quarter].astype(f32) + aside.astype(f32)).astype(bf16)
        return self.scatter_upper(near)

    def flip(self, value, axis, bit):
        return jnp.where(bit == 1, jnp.flip(value, axis), value)

    def to_relative(self, value):
        lead = value.shape[:-1]
        parts = value.reshape(lead + (self.upper, 2, 2, value.shape[-1] // self.count))
        k = len(lead)
        order = tuple(range(k)) + (k + 2, k + 1, k, k + 3)
        parts = jnp.transpose(parts, order)
        parts = self.flip(self.flip(parts, k, self.core), k + 1, self.side)
        return parts.reshape(value.shape)

    def from_relative(self, value):
        lead = value.shape[:-1]
        parts = value.reshape(lead + (2, 2, self.upper, value.shape[-1] // self.count))
        k = len(lead)
        parts = self.flip(self.flip(parts, k, self.core), k + 1, self.side)
        order = tuple(range(k)) + (k + 2, k + 1, k, k + 3)
        return jnp.transpose(parts, order).reshape(value.shape)

    def relative_blocks(self):
        spot = jnp.arange(self.count, dtype=jnp.int32)
        core = spot // (2 * self.upper)
        side = (spot // self.upper) % 2
        high = spot % self.upper
        return high * 4 + (side ^ self.side) * 2 + (core ^ self.core)

    def own_half(self, rows):
        half = rows.shape[0] // 2
        return lax.dynamic_slice_in_dim(rows, self.tensor * half, half, 0)

    def other_half(self, rows):
        half = rows.shape[0] // 2
        return lax.dynamic_slice_in_dim(rows, (1 - self.tensor) * half, half, 0)

    def in_order(self, own, other):
        return jnp.where(
            self.tensor == 0,
            jnp.concatenate([own, other], axis=0),
            jnp.concatenate([other, own], axis=0),
        )


def key_mask(block_rows, prompt_part, key_blocks, cont_row_ids, block_index):
    row_index = lax.broadcasted_iota(jnp.int32, (block_rows, 1), 0)
    prompt_key = (
        key_blocks[:, None] * prompt_part + jnp.arange(prompt_part, dtype=jnp.int32)[None]
    ).reshape(1, -1)
    position = block_index * prompt_part + row_index
    prompt_cols = jnp.where(row_index < prompt_part, prompt_key <= position, True)
    cont_len = cont_row_ids.shape[0]
    cont_key = lax.broadcasted_iota(jnp.int32, (1, cont_len), 1)
    row_ids = jnp.concatenate([jnp.full((prompt_part,), -1, jnp.int32), cont_row_ids])[:, None]
    cont_cols = (row_ids == cont_row_ids[None, :]) & (cont_key <= row_index - prompt_part)
    return jnp.concatenate([prompt_cols, cont_cols], axis=1)


def head_scores(query_head, key_head, allowed, score_scale):
    scores = (
        jnp.einsum("qcd,kcd->cqk", query_head, key_head, preferred_element_type=f32)
        * score_scale
    )
    return jnp.where(allowed[None], scores, masked_value)


def head_forward(query_head, key_head, value_head, lam_head, allowed, score_scale):
    scores = head_scores(query_head, key_head, allowed, score_scale)
    row_top = jnp.max(scores, axis=-1, keepdims=True)
    exp_terms = jnp.exp(scores - row_top)
    row_total = jnp.sum(exp_terms, axis=-1, keepdims=True)
    weights = exp_terms / row_total
    mixed_map = (weights[0] - lam_head * weights[1]).astype(bf16)
    heads_out = jnp.dot(mixed_map, value_head, preferred_element_type=f32)
    return (heads_out, (row_top + jnp.log(row_total))[:, :, 0])


def head_backward(
    query_head, key_head, value_head, lam_head, lse_head, grad_head, allowed, score_scale
):
    scores = head_scores(query_head, key_head, allowed, score_scale)
    weights = jnp.exp(scores - lse_head[:, :, None])
    mixed_map = (weights[0] - lam_head * weights[1]).astype(bf16)
    mixed_grad = cols_product(grad_head, value_head)
    value_grad = rows_product(mixed_map, grad_head)
    lam_grad = -jnp.sum(weights[1] * mixed_grad)
    first_grad = weights[0] * (
        mixed_grad - jnp.sum(mixed_grad * weights[0], axis=-1, keepdims=True)
    )
    second_in = -lam_head * mixed_grad
    second_grad = weights[1] * (second_in - jnp.sum(second_in * weights[1], axis=-1, keepdims=True))
    score_grad = jnp.stack([first_grad, second_grad]).astype(bf16)
    query_grad = (
        jnp.einsum("cqk,kcd->qcd", score_grad, key_head, preferred_element_type=f32) * score_scale
    )
    key_grad = (
        jnp.einsum("cqk,qcd->kcd", score_grad, query_head, preferred_element_type=f32)
        * score_scale
    )
    return (query_grad, key_grad, value_grad, lam_grad)


def attend(queries, keys_values, lam_vec, allowed, score_scale):
    heads = lam_vec.shape[0]
    rows, keys = queries.shape[0], keys_values.shape[0]
    width = heads * 2 * DK
    q_four = queries.reshape(rows, heads, 2, DK).transpose(1, 0, 2, 3)
    k_four = keys_values[:, :width].reshape(keys, heads, 2, DK).transpose(1, 0, 2, 3)
    v_three = keys_values[:, width:].reshape(keys, heads, DV).transpose(1, 0, 2)

    def one(pieces):
        return head_forward(pieces[0], pieces[1], pieces[2], pieces[3], allowed, score_scale)

    out, lse = lax.map(one, (q_four, k_four, v_three, lam_vec))
    return out.transpose(1, 0, 2).reshape(rows, heads * DV), lse


def attend_back(queries, keys_values, lam_vec, lse, heads_grad, allowed, score_scale):
    heads = lam_vec.shape[0]
    rows, keys = queries.shape[0], keys_values.shape[0]
    width = heads * 2 * DK
    q_four = queries.reshape(rows, heads, 2, DK).transpose(1, 0, 2, 3)
    k_four = keys_values[:, :width].reshape(keys, heads, 2, DK).transpose(1, 0, 2, 3)
    v_three = keys_values[:, width:].reshape(keys, heads, DV).transpose(1, 0, 2)
    g_three = heads_grad.reshape(rows, heads, DV).transpose(1, 0, 2)

    def one(pieces):
        return head_backward(*pieces, allowed, score_scale)

    dq, dk, dv, dlam = lax.map(one, (q_four, k_four, v_three, lam_vec, lse, g_three))
    dq = dq.transpose(1, 0, 2, 3).reshape(rows, width).astype(bf16)
    dk = dk.transpose(1, 0, 2, 3).reshape(keys, width).astype(bf16)
    dv = dv.transpose(1, 0, 2).reshape(keys, heads * DV).astype(bf16)
    return dq, jnp.concatenate([dk, dv], axis=1), dlam


def per_device(
    tokens,
    cotangent,
    cont_ids,
    q_weight,
    k_weight,
    v_weight,
    out_weight,
    attn_gain,
    head_gain,
    lam_q1,
    lam_k1,
    lam_q2,
    lam_k2,
    gate_weight,
    up_weight,
    down_weight,
    ffn_gain,
):
    at = Places()
    local_rows = tokens.shape[0]
    block_rows = 2 * local_rows
    row_ids = cont_ids[0]
    prompt_part = block_rows - row_ids.shape[0]
    prompt_len = prompt_part * at.count
    score_scale = DK ** (-0.5)
    heads = q_weight.shape[1] // (2 * DK)
    width = heads * 2 * DK

    prompt_sent = lax.ppermute(tokens[:prompt_part], "tensor", [(0, 1)])
    prompt_own = jnp.where(at.tensor == 0, tokens[:prompt_part], prompt_sent)
    prompt_all = at.gather(prompt_own)
    kv_full = at.gather(jnp.concatenate([k_weight, v_weight], axis=1))
    qo_full = at.gather(jnp.concatenate([q_weight, out_weight], axis=1))
    q_full, out_full = qo_full[:, :width], qo_full[:, width:]
    gate_full = at.gather(gate_weight)
    up_full = at.gather(up_weight)
    down_full = at.gather(down_weight)
    small_parts = (attn_gain, ffn_gain, head_gain, lam_q1, lam_k1, lam_q2, lam_k2)
    small_all = lax.all_gather(
        jnp.concatenate([part.reshape(-1) for part in small_parts]), "dp", axis=0
    ).astype(f32)
    small_full = []
    start = 0
    for part in small_parts:
        small_full.append(
            small_all[:, start : start + part.size].reshape((-1,) + part.shape[1:])
        )
        start += part.size
    attn_gain_row = at.to_relative(small_full[0])
    ffn_gain_row = at.to_relative(small_full[1])
    head_gain_row = small_full[2].T.reshape(-1)
    first_exp = jnp.exp(jnp.sum(small_full[3] * small_full[4], axis=0))
    second_exp = jnp.exp(jnp.sum(small_full[5] * small_full[6], axis=0))
    lam_vec = first_exp - second_exp + lambda_init

    tokens_rel = at.to_relative(tokens)
    tokens_f32 = tokens_rel.astype(f32)
    tokens_all = at.in_order(tokens_rel, at.swap_tensor(tokens_rel)).astype(f32)
    normed = (tokens_all * inv_rms(tokens_all, norm_eps) * attn_gain_row).astype(bf16)
    prompt_f32 = at.to_relative(prompt_all).astype(f32)
    prompt_normed = (prompt_f32 * inv_rms(prompt_f32, norm_eps) * attn_gain_row).astype(bf16)
    normed_keys = jnp.concatenate([prompt_normed, normed[prompt_part:]], axis=0)
    queries = plain_product(normed, q_full).astype(bf16)
    keys_values = plain_product(normed_keys, kv_full).astype(bf16)
    allowed = key_mask(block_rows, prompt_part, at.relative_blocks(), row_ids, at.index)
    heads_out, lse = attend(queries, keys_values, lam_vec, allowed, score_scale)

    def per_head(rows):
        return rows.reshape(rows.shape[0], heads, DV)

    heads_three = per_head(heads_out)
    head_gain_three = head_gain_row.reshape(1, heads, DV)
    head_inv = inv_rms(heads_three, head_eps)
    attn_vec = (heads_three * head_inv * head_gain_three * (1.0 - lambda_init)).astype(bf16)
    attn_vec = attn_vec.reshape(block_rows, heads * DV)
    attn_own, attn_other = at.own_half(attn_vec), at.other_half(attn_vec)
    attn_two = jnp.concatenate([attn_own, attn_other], axis=0)
    out_sent = at.swap_tensor(cols_product(attn_other, out_full).astype(bf16))
    residual = tokens_f32 + (cols_product(attn_own, out_full) + out_sent.astype(f32))

    inv_second = inv_rms(residual, norm_eps)
    ffn_own = (residual * inv_second * ffn_gain_row).astype(bf16)
    ffn_in = jnp.concatenate([ffn_own, at.swap_tensor(ffn_own)], axis=0)
    gate_proj = plain_product(ffn_in, gate_full)
    up_proj = plain_product(ffn_in, up_full)
    gate_sigmoid = jax.nn.sigmoid(gate_proj)
    hidden = (gate_proj * gate_sigmoid * up_proj).astype(bf16)
    down_sent = at.swap_tensor(cols_product(hidden[local_rows:], down_full).astype(bf16))
    output = residual + (cols_product(hidden[:local_rows], down_full) + down_sent.astype(f32))
    output = at.from_relative(output.astype(bf16))

    cot_rel = at.to_relative(cotangent)
    cot_rows = jnp.concatenate([cot_rel, at.swap_tensor(cot_rel)], axis=0)
    hidden_grad = plain_product(cot_rows, down_full)
    grad_down = at.scatter_product(cot_rows, hidden)
    gate_grad = (
        hidden_grad * up_proj * gate_sigmoid * (1.0 + gate_proj * (1.0 - gate_sigmoid))
    ).astype(bf16)
    up_grad = (hidden_grad * gate_proj * gate_sigmoid).astype(bf16)

    def back_ffn(rows):
        return cols_product(gate_grad[rows], gate_full) + cols_product(up_grad[rows], up_full)

    ffn_sent = at.swap_tensor(back_ffn(slice(local_rows, None)).astype(bf16))
    ffn_in_grad = back_ffn(slice(0, local_rows)) + ffn_sent.astype(f32)
    grad_gate = at.scatter_product(ffn_in, gate_grad)
    grad_up = at.scatter_product(ffn_in, up_grad)
    residual_grad = cot_rel.astype(f32) + norm_back(
        residual, inv_second, ffn_gain_row, ffn_in_grad
    )
    ffn_gain_part = jnp.sum(ffn_in_grad * residual * inv_second, axis=0)

    branch_own = residual_grad.astype(bf16)
    branch = jnp.concatenate([branch_own, at.swap_tensor(branch_own)], axis=0)
    grad_out = at.scatter_product(branch, attn_two)
    vec_two = plain_product(branch, out_full)
    vec_three = per_head(at.in_order(vec_two[:local_rows], vec_two[local_rows:]))
    scaled_grad = vec_three * head_gain_three * (1.0 - lambda_init)
    heads_grad = (
        head_inv * scaled_grad
        - heads_three
        * head_inv**3
        * jnp.mean(heads_three * scaled_grad, axis=-1, keepdims=True)
    ).astype(bf16)
    head_gain_part = jnp.sum(vec_three * heads_three * head_inv * (1.0 - lambda_init), axis=0)
    queries_grad, kv_grad, lam_grad = attend_back(
        queries,
        keys_values,
        lam_vec,
        lse,
        heads_grad.reshape(block_rows, heads * DV),
        allowed,
        score_scale,
    )
    prompt_grad = at.scatter_rows(kv_grad[:prompt_len])
    grad_kv = at.scatter_product(normed_keys, kv_grad)
    grad_q = at.scatter_product(normed, queries_grad)
    kv_here = jnp.concatenate([prompt_grad, kv_grad[prompt_len:]], axis=0)
    joint_grad = jnp.concatenate([queries_grad, kv_here], axis=1)
    back_own, back_other = at.own_half(joint_grad), at.other_half(joint_grad)

    def back_attn(rows):
        return cols_product(rows[:, :width], q_full) + cols_product(rows[:, width:], kv_full)

    normed_sent = at.swap_tensor(back_attn(back_other).astype(bf16))
    normed_grad = back_attn(back_own) + normed_sent.astype(f32)
    inv_first = inv_rms(tokens_f32, norm_eps)
    tokens_grad = residual_grad + norm_back(tokens_f32, inv_first, attn_gain_row, normed_grad)
    tokens_grad = at.from_relative(tokens_grad.astype(bf16))
    attn_gain_part = jnp.sum(normed_grad * tokens_f32 * inv_first, axis=0)

    head_rows = head_gain.shape[0]
    gain_rows = attn_gain.shape[0]
    attn_gain_sum, ffn_gain_sum, head_gain_sum, lam_sum = lax.psum(
        (
            at.from_relative(attn_gain_part),
            at.from_relative(ffn_gain_part),
            head_gain_part.T,
            lam_grad,
        ),
        "dp",
    )
    gain_two = jnp.stack([attn_gain_sum, ffn_gain_sum])
    gain_two = lax.psum(
        lax.dynamic_slice_in_dim(gain_two, at.index * gain_rows, gain_rows, 1), "tensor"
    )
    grad_head_gain = lax.dynamic_slice_in_dim(head_gain_sum, at.index * head_rows, head_rows, 0)
    one_scale, two_scale = lam_sum * first_exp, -lam_sum * second_exp
    return (
        output,
        tokens_grad,
        grad_q.astype(f32),
        grad_kv[:, :width].astype(f32),
        grad_kv[:, width:].astype(f32),
        grad_out.astype(f32),
        gain_two[0],
        grad_head_gain,
        one_scale * lam_k1.astype(f32),
        one_scale * lam_q1.astype(f32),
        two_scale * lam_k2.astype(f32),
        two_scale * lam_q2.astype(f32),
        grad_gate.astype(f32),
        grad_up.astype(f32),
        grad_down.astype(f32),
        gain_two[1],
    )


def solution(mesh):
    rows = P(("dp", "tensor"), None)
    both = P("dp", "tensor")
    placed = (
        (rows, rows, P("dp", None))
        + (both,) * 4
        + (P("dp"),)
        + (both,) * 5
        + (both,) * 3
        + (P("dp"),)
    )
    return jax.shard_map(
        per_device,
        mesh=mesh,
        in_specs=placed,
        out_specs=(rows, rows)
        + (both,) * 4
        + (P("dp"),)
        + (both,) * 5
        + (both,) * 3
        + (P("dp"),),
        check_vma=False,
    )
```

```python
import jax
import jax.numpy as jnp
from jax import lax
from jax.experimental import pallas as pl
from jax.experimental.pallas import tpu as pltpu
from jax.sharding import PartitionSpec as P

D = 2048
DK = 128
DV = 256

norm_eps = 1e-06
head_eps = 1e-05
lambda_init = 0.2
masked_value = -1e30
f32 = jnp.float32
bf16 = jnp.bfloat16
CHUNK = 256


def inv_rms(entries, eps_value):
    return lax.rsqrt(jnp.mean(entries * entries, axis=-1, keepdims=True) + eps_value)


def norm_back(entries, inverse, gain_row, incoming):
    scaled = gain_row * incoming
    return inverse * scaled - entries * inverse**3 * jnp.mean(
        entries * scaled, axis=-1, keepdims=True
    )


def plain_product(first_arg, second_arg):
    return jnp.dot(first_arg, second_arg, preferred_element_type=f32)


def rows_product(first_arg, second_arg):
    return lax.dot_general(
        first_arg, second_arg, (((0,), (0,)), ((), ())), preferred_element_type=f32
    )


def cols_product(first_arg, second_arg):
    return lax.dot_general(
        first_arg, second_arg, (((1,), (1,)), ((), ())), preferred_element_type=f32
    )


def together(*values):
    return lax.optimization_barrier(values)


def after(value, *others):
    if not others:
        return value
    return lax.optimization_barrier((value,) + others)[0]


class Places:
    def __init__(self):
        self.count = lax.axis_size("dp")
        self.upper = self.count // 4
        index = lax.axis_index("dp")
        self.index = index
        self.core = index % 2
        self.side = (index // 2) % 2
        self.tensor = lax.axis_index("tensor")
        self.upper_groups = [
            [low + 4 * high for high in range(self.upper)] for low in range(4)
        ]
        self.core_pairs = [(k, k ^ 1) for k in range(self.count)]
        self.side_pairs = [(k, k ^ 2) for k in range(self.count)]

    def swap_core(self, value):
        return lax.ppermute(value, "dp", self.core_pairs)

    def swap_side(self, value):
        return lax.ppermute(value, "dp", self.side_pairs)

    def swap_tensor(self, value):
        return lax.ppermute(value, "tensor", [(0, 1), (1, 0)])

    def gather_upper(self, shard):
        return lax.all_gather(
            shard, "dp", axis=0, tiled=True, axis_index_groups=self.upper_groups
        )

    def gather_near(self, here, *others):
        here = after(here, *others)
        aside = self.swap_side(here)
        return [here, aside, self.swap_core(here), self.swap_core(aside)]

    def sum_small(self, value):
        step = 1
        while step < self.count:
            value = value + lax.ppermute(
                value, "dp", [(k, k ^ step) for k in range(self.count)]
            )
            step *= 2
        return value

    def block_order(self, value):
        parts = value.reshape((2, 2, self.upper) + value.shape[1:])
        parts = self.flip(self.flip(parts, 0, self.core), 1, self.side)
        order = (2, 1, 0) + tuple(range(3, parts.ndim))
        return jnp.transpose(parts, order).reshape(value.shape)

    def scatter_upper(self, value):
        return lax.psum_scatter(
            value, "dp", scatter_dimension=0, tiled=True, axis_index_groups=self.upper_groups
        )

    def far_part(self, first_arg, second_arg):
        half = first_arg.shape[1] // 2
        return rows_product(first_arg[:, half:], second_arg).astype(bf16)

    def aside_part(self, first_arg, second_arg, far):
        half, quarter = first_arg.shape[1] // 2, first_arg.shape[1] // 4
        aside = rows_product(first_arg[:, quarter:half], second_arg) + far[quarter:].astype(f32)
        return aside.astype(bf16)

    def near_part(self, first_arg, second_arg, far, aside):
        quarter = first_arg.shape[1] // 4
        near = rows_product(first_arg[:, :quarter], second_arg) + far[:quarter].astype(f32)
        return (near + aside.astype(f32)).astype(bf16)

    def flip(self, value, axis, bit):
        return jnp.where(bit == 1, jnp.flip(value, axis), value)

    def to_relative(self, value):
        lead = value.shape[:-1]
        parts = value.reshape(lead + (self.upper, 2, 2, value.shape[-1] // self.count))
        k = len(lead)
        order = tuple(range(k)) + (k + 2, k + 1, k, k + 3)
        parts = jnp.transpose(parts, order)
        parts = self.flip(self.flip(parts, k, self.core), k + 1, self.side)
        return parts.reshape(value.shape)

    def from_relative(self, value):
        lead = value.shape[:-1]
        parts = value.reshape(lead + (2, 2, self.upper, value.shape[-1] // self.count))
        k = len(lead)
        parts = self.flip(self.flip(parts, k, self.core), k + 1, self.side)
        order = tuple(range(k)) + (k + 2, k + 1, k, k + 3)
        return jnp.transpose(parts, order).reshape(value.shape)

    def relative_blocks(self):
        spot = jnp.arange(self.count, dtype=jnp.int32)
        core = spot // (2 * self.upper)
        side = (spot // self.upper) % 2
        high = spot % self.upper
        return high * 4 + (side ^ self.side) * 2 + (core ^ self.core)

    def own_half(self, rows):
        half = rows.shape[0] // 2
        return lax.dynamic_slice_in_dim(rows, self.tensor * half, half, 0)

    def other_half(self, rows):
        half = rows.shape[0] // 2
        return lax.dynamic_slice_in_dim(rows, (1 - self.tensor) * half, half, 0)

    def in_order(self, own, other):
        return jnp.where(
            self.tensor == 0,
            jnp.concatenate([own, other], axis=0),
            jnp.concatenate([other, own], axis=0),
        )


def dot_nt(first, second):
    return lax.dot_general(first, second, (((1,), (1,)), ((), ())), preferred_element_type=f32)


def dot_nn(first, second):
    return lax.dot_general(first, second, (((1,), (0,)), ((), ())), preferred_element_type=f32)


def dot_tn(first, second):
    return lax.dot_general(first, second, (((0,), (0,)), ((), ())), preferred_element_type=f32)


def forward_kernel(
    prompt_len, top_rows, first_head, lam_ref, q_ref, kv_ref, gain_ref, spot_ref, reach_ref, low_ref, high_ref,
    out_ref, vec_ref, lse_ref, one_ref, two_ref, stat_ref,
):
    lam = lam_ref[first_head + pl.program_id(0)]
    rows, keys = q_ref.shape[0], kv_ref.shape[0]
    scale = DK ** (-0.5)
    scores = (one_ref, two_ref)

    def chunk_scores(chunk):
        for comp in range(2):
            lanes = slice(comp * DK, (comp + 1) * DK)
            scores[comp][chunk] = dot_nt(q_ref[:, lanes], kv_ref[pl.ds(chunk * CHUNK, CHUNK), lanes])

    def prompt_chunk(chunk, tops):
        chunk_scores(chunk)
        spots = spot_ref[chunk]
        for comp in range(2):
            ref = scores[comp]
            for part in range(CHUNK // 128):
                lanes = slice(part * 128, (part + 1) * 128)
                ref[chunk, :top_rows, lanes] = jnp.where(
                    spots[:, lanes] <= reach_ref[...], ref[chunk, :top_rows, lanes], masked_value
                )
        return 0

    def cont_chunk(chunk, tops):
        chunk_scores(chunk)
        first = chunk * CHUNK - prompt_len
        for part in range(CHUNK // 128):
            lanes = slice(part * 128, (part + 1) * 128)
            spot = lax.broadcasted_iota(jnp.int32, (rows, 128), 1) + (first + part * 128)
            allowed = (spot >= low_ref[...]) & (spot <= high_ref[...])
            for comp in range(2):
                ref = scores[comp]
                ref[chunk, :, lanes] = jnp.where(allowed, ref[chunk, :, lanes], masked_value)
        return 0

    first_cont = prompt_len // CHUNK
    count = keys // CHUNK
    lax.fori_loop(0, first_cont, prompt_chunk, 0)
    lax.fori_loop(first_cont, count, cont_chunk, 0)

    ROWS = 32
    def row_block(block, carry):
        span = pl.ds(pl.multiple_of(block * ROWS, ROWS), ROWS)
        totals = []
        for comp in range(2):
            ref = scores[comp]
            top = ref[0, span, :128]
            for chunk in range(count):
                for part in range(CHUNK // 128):
                    if chunk + part > 0:
                        top = jnp.maximum(top, ref[chunk, span, part * 128 : (part + 1) * 128])
            top = jnp.max(top, axis=1, keepdims=True)
            total = jnp.zeros((ROWS, 128), f32)
            for chunk in range(count):
                for part in range(CHUNK // 128):
                    lanes = slice(part * 128, (part + 1) * 128)
                    terms = jnp.exp((ref[chunk, span, lanes] - top) * scale)
                    total = total + terms
                    ref[chunk, span, lanes] = terms
            total = jnp.sum(total, axis=1, keepdims=True)
            totals.append(total)
            stat_ref[comp, span, :] = jnp.broadcast_to(top * scale + jnp.log(total), (ROWS, 128))
        first = 1.0 / totals[0]
        second = lam / totals[1]
        for chunk in range(count):
            for part in range(CHUNK // 128):
                lanes = slice(part * 128, (part + 1) * 128)
                one_ref[chunk, span, lanes] = (
                    one_ref[chunk, span, lanes] * first - two_ref[chunk, span, lanes] * second
                )
        return carry

    lax.fori_loop(0, rows // ROWS, row_block, 0)

    turn = (lax.broadcasted_iota(jnp.int32, (8, 128), 1) == 0).astype(f32)
    for comp in range(2):
        lse_ref[0, comp * 8 : (comp + 1) * 8, :] = lax.dot_general(
            turn,
            stat_ref[comp],
            (((1,), (1,)), ((), ())),
            precision=lax.Precision.HIGHEST,
            preferred_element_type=f32,
        )
    out_ref[...] = jnp.zeros_like(out_ref)

    def mix(chunk, carry):
        out_ref[...] += dot_nn(
            one_ref[chunk].astype(bf16), kv_ref[pl.ds(chunk * CHUNK, CHUNK), 2 * DK :]
        )
        return carry

    lax.fori_loop(0, count, mix, 0)
    out = out_ref[...]
    inverse = lax.rsqrt(jnp.mean(out * out, axis=1, keepdims=True) + head_eps)
    vec_ref[...] = (out * inverse * gain_ref[...] * (1.0 - lambda_init)).astype(bf16)


def backward_kernel(
    prompt_len, top_rows, lam_ref, q_ref, kv_ref, gain_ref, vec_ref, out_ref, lse_ref, spot_ref, reach_ref,
    dq_ref, dkv_ref, sums_ref, one_ref, two_ref, mix_ref, grad_ref, turn_ref,
):
    head = pl.program_id(0)
    lam = lam_ref[head]
    rows, keys = q_ref.shape[0], kv_ref.shape[0]
    scale = DK ** (-0.5)
    out = out_ref[...]
    vec = vec_ref[...]
    inverse = lax.rsqrt(jnp.mean(out * out, axis=1, keepdims=True) + head_eps)
    plain = vec * out * inverse * (1.0 - lambda_init)
    scaled = vec * gain_ref[...] * (1.0 - lambda_init)
    grad_ref[...] = (
        inverse * scaled - out * inverse**3 * jnp.mean(out * scaled, axis=1, keepdims=True)
    ).astype(bf16)
    gain_part = jnp.sum(plain, axis=0, keepdims=True)
    grad = grad_ref[...]
    count = keys // CHUNK
    first_cont = prompt_len // CHUNK

    def weigh(chunk):
        span = pl.ds(pl.multiple_of(chunk * CHUNK, CHUNK), CHUNK)
        for comp, ref in ((0, one_ref), (1, two_ref)):
            lanes = slice(comp * DK, (comp + 1) * DK)
            scores = dot_nt(kv_ref[span, lanes], q_ref[:, lanes])
            ref[chunk] = jnp.exp(scores * scale - lse_ref[0, 8 * comp : 8 * comp + 1, :])
        mix_ref[chunk] = dot_nt(kv_ref[span, 2 * DK :], grad)

    def gather_sums(chunk, sums):
        span = pl.ds(pl.multiple_of(chunk * CHUNK, CHUNK), CHUNK)
        one, two, mix = one_ref[chunk], two_ref[chunk], mix_ref[chunk]
        mixed = (one - lam * two).astype(bf16)
        dkv_ref[span, 2 * DK :] = dot_nn(mixed, grad).astype(bf16)
        return (
            sums[0] + jnp.sum((one * mix).reshape(CHUNK // 8, 8, rows), axis=0),
            sums[1] + jnp.sum((two * mix).reshape(CHUNK // 8, 8, rows), axis=0),
        )

    def prompt_chunk(chunk, sums):
        weigh(chunk)
        allowed = spot_ref[pl.ds(chunk * CHUNK, CHUNK), :top_rows] <= reach_ref[0:1, :top_rows]
        for ref in (one_ref, two_ref):
            ref[chunk, :, :top_rows] = jnp.where(allowed, ref[chunk, :, :top_rows], 0.0)
        return gather_sums(chunk, sums)

    def cont_chunk(chunk, sums):
        weigh(chunk)
        spot = lax.broadcasted_iota(jnp.int32, (CHUNK, rows), 0) + (chunk * CHUNK - prompt_len)
        allowed = (spot >= reach_ref[1:2, :]) & (spot <= reach_ref[2:3, :])
        for ref in (one_ref, two_ref):
            ref[chunk] = jnp.where(allowed, ref[chunk], 0.0)
        return gather_sums(chunk, sums)

    sums = (jnp.zeros((8, rows), f32), jnp.zeros((8, rows), f32))
    sums = lax.fori_loop(0, first_cont, prompt_chunk, sums)
    sums = lax.fori_loop(first_cont, count, cont_chunk, sums)
    first = jnp.sum(sums[0], axis=0, keepdims=True)
    second = jnp.sum(sums[1], axis=0, keepdims=True)
    sums_ref[0, 0:1, :] = gain_part
    sums_ref[0, 1:2, :] = jnp.broadcast_to(-jnp.sum(second, axis=1, keepdims=True), (1, DV))
    turn_ref[...] = jnp.zeros_like(turn_ref)

    def back(chunk, carry):
        span = pl.ds(pl.multiple_of(chunk * CHUNK, CHUNK), CHUNK)
        mix = mix_ref[chunk]
        grads = (
            (one_ref[chunk] * (mix - first)).astype(bf16),
            (two_ref[chunk] * ((mix - second) * (-lam))).astype(bf16),
        )
        for comp in range(2):
            lanes = slice(comp * DK, (comp + 1) * DK)
            dkv_ref[span, lanes] = (dot_nn(grads[comp], q_ref[:, lanes]) * scale).astype(bf16)
            turn_ref[lanes, :] += dot_tn(kv_ref[span, lanes], grads[comp])
        return carry

    lax.fori_loop(0, count, back, 0)
    dq_ref[...] = (turn_ref[...] * scale).astype(bf16)


def attend(queries, keys_values, lam_vec, gain_rows, prompt_spots, bounds, prompt_part, span):
    first, heads = span[0], span[1] - span[0]
    rows, keys = queries.shape[0], keys_values.shape[0]
    prompt_len = prompt_spots.shape[0]
    top_rows = min(rows, -(-prompt_part // 16) * 16)
    wide = [jnp.broadcast_to(bound[:, None], (rows, 128)) for bound in bounds]
    count = keys // CHUNK
    return pl.pallas_call(
        lambda *refs: forward_kernel(prompt_len, top_rows, first, *refs),
        grid=(heads,),
        in_specs=[
            pl.BlockSpec(memory_space=pltpu.SMEM),
            pl.BlockSpec((rows, 2 * DK), lambda h: (0, h + first)),
            pl.BlockSpec((keys, 2 * DK + DV), lambda h: (0, h + first)),
            pl.BlockSpec((1, DV), lambda h: (0, h + first)),
            pl.BlockSpec((prompt_len // CHUNK, 1, CHUNK), lambda h: (0, 0, 0)),
            pl.BlockSpec((top_rows, 128), lambda h: (0, 0)),
            pl.BlockSpec((rows, 128), lambda h: (0, 0)),
            pl.BlockSpec((rows, 128), lambda h: (0, 0)),
        ],
        out_specs=[
            pl.BlockSpec((rows, DV), lambda h: (0, h)),
            pl.BlockSpec((rows, DV), lambda h: (0, h)),
            pl.BlockSpec((1, 16, rows), lambda h: (h, 0, 0)),
        ],
        out_shape=[
            jax.ShapeDtypeStruct((rows, heads * DV), f32),
            jax.ShapeDtypeStruct((rows, heads * DV), bf16),
            jax.ShapeDtypeStruct((heads, 16, rows), f32),
        ],
        scratch_shapes=[
            pltpu.VMEM((count, rows, CHUNK), f32),
            pltpu.VMEM((count, rows, CHUNK), f32),
            pltpu.VMEM((2, rows, 128), f32),
        ],
        compiler_params=pltpu.CompilerParams(vmem_limit_bytes=56 * 2**20),
        name="attend",
    )(
        lam_vec,
        queries,
        keys_values,
        gain_rows,
        prompt_spots.reshape(prompt_len // CHUNK, 1, CHUNK),
        wide[0][:top_rows],
        wide[1],
        wide[2],
    )


def attend_back(queries, keys_values, lam_vec, gain_rows, vec_grad, out, lse, prompt_spots, bounds, prompt_part):
    heads = lam_vec.shape[0]
    rows, keys = queries.shape[0], keys_values.shape[0]
    prompt_len = prompt_spots.shape[0]
    top_rows = min(rows, -(-prompt_part // 128) * 128)
    count = keys // CHUNK
    reach = jnp.concatenate([jnp.stack(bounds), jnp.zeros((5, rows), jnp.int32)])
    return pl.pallas_call(
        lambda *refs: backward_kernel(prompt_len, top_rows, *refs),
        grid=(heads,),
        in_specs=[
            pl.BlockSpec(memory_space=pltpu.SMEM),
            pl.BlockSpec((rows, 2 * DK), lambda h: (0, h)),
            pl.BlockSpec((keys, 2 * DK + DV), lambda h: (0, h)),
            pl.BlockSpec((1, DV), lambda h: (0, h)),
            pl.BlockSpec((rows, DV), lambda h: (0, h)),
            pl.BlockSpec((rows, DV), lambda h: (0, h)),
            pl.BlockSpec((1, 16, rows), lambda h: (h, 0, 0)),
            pl.BlockSpec((prompt_len, 128), lambda h: (0, 0)),
            pl.BlockSpec((8, rows), lambda h: (0, 0)),
        ],
        out_specs=[
            pl.BlockSpec((2 * DK, rows), lambda h: (h, 0)),
            pl.BlockSpec((keys, 2 * DK + DV), lambda h: (0, h)),
            pl.BlockSpec((1, 8, DV), lambda h: (h, 0, 0)),
        ],
        out_shape=[
            jax.ShapeDtypeStruct((heads * 2 * DK, rows), bf16),
            jax.ShapeDtypeStruct((keys, heads * (2 * DK + DV)), bf16),
            jax.ShapeDtypeStruct((heads, 8, DV), f32),
        ],
        scratch_shapes=[
            pltpu.VMEM((count, CHUNK, rows), f32),
            pltpu.VMEM((count, CHUNK, rows), f32),
            pltpu.VMEM((count, CHUNK, rows), f32),
            pltpu.VMEM((rows, DV), bf16),
            pltpu.VMEM((2 * DK, rows), f32),
        ],
        compiler_params=pltpu.CompilerParams(vmem_limit_bytes=58 * 2**20),
        name="attend_back",
    )(
        lam_vec,
        queries,
        keys_values,
        gain_rows,
        vec_grad,
        out,
        lse,
        jnp.broadcast_to(prompt_spots[:, None], (prompt_len, 128)),
        reach,
    )


def norm_kernel(count, blocks_ref, swap_ref, *refs):
    *sources, gain_ref, out_ref = refs
    step = pl.program_id(0)
    rows, depth = out_ref.shape
    block = depth // count
    upper = count // 4

    def norm_from(pieces):
        total = jnp.zeros((rows, 1), f32)
        for piece in pieces:
            x = piece[:rows, :].astype(f32)
            total = total + jnp.sum(x * x, axis=1, keepdims=True)
        inverse = lax.rsqrt(total * (1.0 / depth) + norm_eps)
        size = depth // len(pieces)
        for spot in range(count):
            lanes = slice(spot * block, (spot + 1) * block)
            high = spot % upper
            piece = pieces[high * 4 * block // size]
            start = blocks_ref[spot] * block - (high * 4 * block // size) * size
            part = piece[:rows, pl.ds(pl.multiple_of(start, block), block)].astype(f32)
            out_ref[:, lanes] = (part * inverse * gain_ref[:, lanes]).astype(bf16)

    for core in range(2):

        @pl.when((step >= core * 2 * upper) & (step < (core + 1) * 2 * upper))
        def _():
            norm_from(sources[2 * core : 2 * core + 2])

    @pl.when(step >= count)
    def _():
        norm_from(sources[4:5])


def norm_keys(at, prompt_two, prompt_far, tokens_all, gain_row, prompt_part):
    depth = tokens_all.shape[1]
    count, upper = at.count, at.upper
    cont_len = tokens_all.shape[0] - prompt_part
    unit = prompt_two.shape[0] // (4 * upper)
    if (depth // count) % 128 or cont_len % prompt_part or upper % 2:
        cores = []
        for group in (prompt_two, prompt_far):
            parts = group.reshape(2, 2 * upper, unit, depth // 2)[:, :, :prompt_part]
            parts = parts.reshape(2, 2 * upper * prompt_part, depth // 2)
            parts = at.flip(parts, 0, at.tensor)
            cores.append(jnp.concatenate([parts[0], parts[1]], axis=1))
        rows = at.to_relative(jnp.concatenate(cores + [tokens_all[prompt_part:]], axis=0))
        rows = rows.astype(f32)
        return (rows * inv_rms(rows, norm_eps) * gain_row).astype(bf16)

    def spot_of(core, half):
        first = core * 2 * upper
        return lambda i, blocks, swap: (
            (swap[0] ^ half) * 2 * upper + jnp.clip(i - first, 0, 2 * upper - 1),
            0,
        )

    return pl.pallas_call(
        lambda *refs: norm_kernel(count, *refs),
        grid_spec=pltpu.PrefetchScalarGridSpec(
            num_scalar_prefetch=2,
            grid=(count + cont_len // prompt_part,),
            in_specs=[
                pl.BlockSpec((unit, depth // 2), spot_of(core, half))
                for core in range(2)
                for half in range(2)
            ]
            + [
                pl.BlockSpec(
                    (prompt_part, depth),
                    lambda i, blocks, swap: (1 + jnp.maximum(i - count, 0), 0),
                ),
                pl.BlockSpec((1, depth), lambda i, blocks, swap: (0, 0)),
            ],
            out_specs=pl.BlockSpec((prompt_part, depth), lambda i, blocks, swap: (i, 0)),
        ),
        out_shape=jax.ShapeDtypeStruct((prompt_part * count + cont_len, depth), bf16),
        name="norm_keys",
    )(
        at.relative_blocks(),
        at.tensor.reshape(1).astype(jnp.int32),
        prompt_two,
        prompt_two,
        prompt_far,
        prompt_far,
        tokens_all,
        gain_row.reshape(1, depth),
    )


def per_device(
    tokens,
    cotangent,
    cont_ids,
    q_weight,
    k_weight,
    v_weight,
    out_weight,
    attn_gain,
    head_gain,
    lam_q1,
    lam_k1,
    lam_q2,
    lam_k2,
    gate_weight,
    up_weight,
    down_weight,
    ffn_gain,
):
    at = Places()
    local_rows = tokens.shape[0]
    block_rows = 2 * local_rows
    row_ids = cont_ids[0]
    cont_len = row_ids.shape[0]
    prompt_part = block_rows - cont_len
    prompt_len = prompt_part * at.count
    heads = q_weight.shape[1] // (2 * DK)
    width = heads * 2 * DK
    shard_rows = q_weight.shape[0]

    small_parts = (attn_gain, ffn_gain, head_gain, lam_q1, lam_k1, lam_q2, lam_k2)
    small = jnp.concatenate([part.reshape(-1) for part in small_parts])
    half = D // 2
    small_rows = jnp.zeros((16, half), bf16).at[0, : small.size].set(small)
    prompt_sent = lax.ppermute(tokens[:prompt_part, half:], "tensor", [(0, 1)])
    prompt_own = jnp.where(at.tensor == 0, tokens[:prompt_part, :half], prompt_sent)
    prompt_own = jnp.concatenate([prompt_own, small_rows], axis=0)
    prompt_here = at.gather_upper(prompt_own)

    def by_head(weight):
        return weight.reshape(shard_rows, heads, -1)

    kv_here = at.gather_upper(
        after(
            jnp.concatenate([by_head(k_weight), by_head(v_weight)], axis=2).reshape(
                shard_rows, -1
            ),
            prompt_own,
        )
    )
    q_here = at.gather_upper(after(q_weight, prompt_own))
    out_here = at.gather_upper(after(out_weight, prompt_own))
    gate_here = at.gather_upper(after(gate_weight, prompt_own))
    up_here = at.gather_upper(after(up_weight, prompt_own))
    down_here = at.gather_upper(after(down_weight, prompt_own))

    tokens_rel = at.to_relative(tokens)
    cot_rel = at.to_relative(cotangent)
    prompt_here, tokens_rel, cot_rel = together(prompt_here, tokens_rel, cot_rel)
    prompt_pair = jnp.concatenate([prompt_here, at.swap_side(prompt_here)], axis=0)
    prompt_turned = at.swap_tensor(prompt_pair)
    kv_here = after(kv_here, prompt_pair)
    kv_side, kv_near = at.swap_side(kv_here), at.swap_core(kv_here)
    tokens_turned = at.swap_tensor(after(tokens, prompt_turned))
    prompt_two = jnp.concatenate([prompt_pair, prompt_turned], axis=0)
    prompt_far = at.swap_core(prompt_two)
    prompt_far, kv_side = together(prompt_far, kv_side)
    kv_far = at.swap_core(kv_side)
    q_here = after(q_here, kv_side)
    q_side, q_near = at.swap_side(q_here), at.swap_core(q_here)
    tokens_all = at.in_order(tokens, tokens_turned)

    small_all = jnp.concatenate(
        [
            group.reshape(2, 2 * at.upper, -1, half)[0, :, prompt_part, : small.size]
            for group in (prompt_two, prompt_far)
        ],
        axis=0,
    ).astype(f32)
    small_full = []
    start = 0
    for part in small_parts:
        small_full.append(
            small_all[:, start : start + part.size].reshape((at.count,) + part.shape)
        )
        start += part.size
    attn_gain_row = small_full[0].reshape(-1)
    ffn_gain_row = small_full[1].reshape(-1)
    head_gain_row = at.block_order(small_full[2]).reshape(DV, heads).T.reshape(1, heads * DV)
    first_exp = jnp.exp(jnp.sum(small_full[3] * small_full[4], axis=(0, 1)))
    second_exp = jnp.exp(jnp.sum(small_full[5] * small_full[6], axis=(0, 1)))
    lam_vec = first_exp - second_exp + lambda_init

    prompt_spots = (
        at.relative_blocks()[:, None] * prompt_part
        + jnp.arange(prompt_part, dtype=jnp.int32)[None]
    ).reshape(-1)
    cont_spot = jnp.arange(cont_len, dtype=jnp.int32)
    earlier = jnp.sum((row_ids[None, :] < row_ids[:, None]).astype(jnp.int32), axis=1)
    far_spot = jnp.full((prompt_part,), prompt_len + cont_len, jnp.int32)
    reach = jnp.concatenate(
        [
            at.index * prompt_part + jnp.arange(prompt_part, dtype=jnp.int32),
            jnp.full((cont_len,), prompt_len, jnp.int32),
        ]
    )
    bounds = (
        reach,
        jnp.concatenate([far_spot, earlier]),
        jnp.concatenate([jnp.full((prompt_part,), -1, jnp.int32), cont_spot]),
    )

    tokens_f32 = tokens_rel.astype(f32)
    normed_keys = norm_keys(at, prompt_two, prompt_far, tokens_all, attn_gain_row, prompt_part)
    normed_keys, kv_far, kv_near = together(normed_keys, kv_far, kv_near)
    own_block = lax.dynamic_slice_in_dim(
        normed_keys, (at.index // 4) * prompt_part, prompt_part, 0
    )
    normed = jnp.concatenate([own_block, normed_keys[prompt_len:]], axis=0)
    kv_full = jnp.concatenate([kv_here, kv_side, kv_near, kv_far], axis=0)
    keys_values = plain_product(normed_keys, kv_full).astype(bf16)
    keys_values, normed, q_side, q_near = together(keys_values, normed, q_side, q_near)
    q_far = at.swap_core(q_side)
    out_here = after(out_here, q_side)
    out_side, out_near = at.swap_side(out_here), at.swap_core(out_here)
    q_full = jnp.concatenate([q_here, q_side, q_near, q_far], axis=0)
    queries = plain_product(normed, q_full).astype(bf16)
    fixed = (lam_vec, head_gain_row, prompt_spots, bounds, prompt_part)
    middle = heads // 2
    first_out, first_vec, first_lse = attend(queries, keys_values, *fixed, (0, middle))
    first_vec, out_side, out_near, gate_here = together(first_vec, out_side, out_near, gate_here)
    out_far = at.swap_core(out_side)
    gate_side, gate_near = at.swap_side(gate_here), at.swap_core(gate_here)
    second_out, second_vec, second_lse = attend(
        after(queries, first_vec), keys_values, *fixed, (middle, heads)
    )
    second_vec, out_far, gate_near = together(second_vec, out_far, gate_near)
    heads_out = jnp.concatenate([first_out, second_out], axis=1)
    lse = jnp.concatenate([first_lse, second_lse], axis=0)
    attn_vec = jnp.concatenate([first_vec, second_vec], axis=1)
    out_full = jnp.concatenate([out_here, out_side, out_near, out_far], axis=0)
    attn_own, attn_other = at.own_half(attn_vec), at.other_half(attn_vec)
    out_send = cols_product(attn_other, out_full).astype(bf16)
    out_sent = at.swap_tensor(out_send)
    out_part = cols_product(after(attn_own, out_send), out_full)
    attn_two = jnp.concatenate([attn_own, attn_other], axis=0)
    out_sent, out_part, gate_side, up_here, attn_two = together(
        out_sent, out_part, gate_side, up_here, attn_two
    )
    gate_far = at.swap_core(gate_side)
    up_side, up_near = at.swap_side(up_here), at.swap_core(up_here)
    residual = tokens_f32 + (out_part + out_sent.astype(f32))

    inv_second = inv_rms(residual, norm_eps)
    ffn_own = (residual * inv_second * ffn_gain_row).astype(bf16)
    ffn_turned = at.swap_tensor(ffn_own)
    cot_turned = at.swap_tensor(after(cot_rel, ffn_own))
    ffn_turned, gate_far, up_near = together(ffn_turned, gate_far, up_near)
    ffn_in = jnp.concatenate([ffn_own, ffn_turned], axis=0)
    cot_rows = jnp.concatenate([cot_rel, cot_turned], axis=0)
    gate_full = jnp.concatenate([gate_here, gate_side, gate_near, gate_far], axis=0)
    gate_proj = plain_product(ffn_in, gate_full)
    gate_proj, up_side, down_here, cot_rows = together(gate_proj, up_side, down_here, cot_rows)
    up_far = at.swap_core(up_side)
    down_side, down_near = at.swap_side(down_here), at.swap_core(down_here)
    up_full = jnp.concatenate([up_here, up_side, up_near, up_far], axis=0)
    up_proj = plain_product(ffn_in, up_full)
    gate_sigmoid = jax.nn.sigmoid(gate_proj)
    hidden = (gate_proj * gate_sigmoid * up_proj).astype(bf16)

    down_send = at.far_part(cot_rows, hidden)
    down_grad_far = at.swap_core(down_send)
    down_send, down_side, down_near = together(down_send, down_side, down_near)
    down_far = at.swap_core(down_side)
    down_grad_side = at.aside_part(cot_rows, hidden, after(down_grad_far, down_side))
    down_grad_aside = at.swap_side(down_grad_side)
    down_full = jnp.concatenate([down_here, down_side, down_near, down_far], axis=0)
    hidden_grad = plain_product(after(cot_rows, down_grad_side), down_full)
    gate_grad = (
        hidden_grad * up_proj * gate_sigmoid * (1.0 + gate_proj * (1.0 - gate_sigmoid))
    ).astype(bf16)
    up_grad = (hidden_grad * gate_proj * gate_sigmoid).astype(bf16)

    def back_ffn(one, two):
        return cols_product(one, gate_full) + cols_product(two, up_full)

    ffn_send = back_ffn(gate_grad[local_rows:], up_grad[local_rows:]).astype(bf16)
    ffn_sent = at.swap_tensor(ffn_send)
    gate_send = at.far_part(ffn_in, after(gate_grad, ffn_send))
    gate_grad_far = at.swap_core(gate_send)
    ffn_part = back_ffn(after(gate_grad[:local_rows], gate_send), up_grad[:local_rows])
    ffn_part, ffn_sent, gate_grad_far = together(ffn_part, ffn_sent, gate_grad_far)
    ffn_in_grad = ffn_part + ffn_sent.astype(f32)
    residual_grad = cot_rel.astype(f32) + norm_back(
        residual, inv_second, ffn_gain_row, ffn_in_grad
    )

    branch_own = residual_grad.astype(bf16)
    branch_sent = at.swap_tensor(branch_own)
    gate_grad_side = at.aside_part(ffn_in, gate_grad, after(gate_grad_far, branch_own))
    up_send = at.far_part(ffn_in, after(up_grad, gate_grad_side))
    up_grad_far = at.swap_core(up_send)
    up_send, branch_sent, down_grad_aside = together(up_send, branch_sent, down_grad_aside)
    gate_grad_aside = at.swap_side(after(gate_grad_side, down_grad_aside))
    branch = jnp.concatenate([branch_own, branch_sent], axis=0)
    out_grad_send = at.far_part(branch, attn_two)
    out_grad_far = at.swap_core(out_grad_send)
    down_last = at.near_part(
        cot_rows, after(hidden, out_grad_send), down_grad_far, down_grad_aside
    )
    grad_down = at.scatter_upper(down_last)
    up_grad_side = at.aside_part(ffn_in, after(up_grad, down_last), up_grad_far)
    up_grad_aside = at.swap_side(up_grad_side)
    vec_two = plain_product(after(branch, up_grad_side), out_full)
    out_grad_side = at.aside_part(branch, after(attn_two, vec_two), out_grad_far)
    out_grad_aside = at.swap_side(out_grad_side)
    vec_grad = at.in_order(vec_two[:local_rows], vec_two[local_rows:])
    queries_grad, kv_grad, head_sums = attend_back(
        queries,
        keys_values,
        lam_vec,
        head_gain_row,
        after(vec_grad, out_grad_side),
        heads_out,
        lse,
        prompt_spots,
        bounds,
        prompt_part,
    )
    queries_grad, kv_grad, head_sums, gate_grad_aside = together(
        queries_grad, kv_grad, head_sums, gate_grad_aside
    )
    queries_grad = queries_grad.T

    two, four = prompt_len // 2, prompt_len // 4
    prompt_send = kv_grad[two:prompt_len]
    prompt_grad_far = at.swap_core(prompt_send)
    kv_send = at.far_part(normed_keys, after(kv_grad, prompt_send))
    kv_grad_far = at.swap_core(kv_send)
    kv_send, prompt_grad_far = together(kv_send, prompt_grad_far)
    prompt_side = (kv_grad[four:two].astype(f32) + prompt_grad_far[four:].astype(f32)).astype(bf16)
    prompt_aside = at.swap_side(prompt_side)
    gate_last = at.near_part(
        ffn_in, after(gate_grad, prompt_side), gate_grad_far, gate_grad_aside
    )
    grad_gate = at.scatter_upper(gate_last)
    gate_last, kv_grad_far = together(gate_last, kv_grad_far)
    kv_grad_side = at.aside_part(normed_keys, kv_grad, kv_grad_far)
    kv_grad_aside = at.swap_side(kv_grad_side)
    q_send = at.far_part(normed, after(queries_grad, kv_grad_side))
    q_grad_far = at.swap_core(q_send)
    up_last = at.near_part(ffn_in, up_grad, up_grad_far, after(up_grad_aside, q_send))
    grad_up = at.scatter_upper(up_last)
    q_grad_side = at.aside_part(normed, queries_grad, after(q_grad_far, up_last))
    q_grad_aside = at.swap_side(q_grad_side)

    hidden_late = after(hidden, q_grad_side)
    output_send = cols_product(hidden_late[local_rows:], down_full).astype(bf16)
    output_sent = at.swap_tensor(output_send)
    output_part = cols_product(hidden_late[:local_rows], down_full)
    output_part, output_sent, prompt_aside = together(output_part, output_sent, prompt_aside)
    output = at.from_relative((residual + (output_part + output_sent.astype(f32))).astype(bf16))

    prompt_last = (
        kv_grad[:four].astype(f32)
        + prompt_grad_far[:four].astype(f32)
        + prompt_aside.astype(f32)
    ).astype(bf16)
    prompt_grad = at.scatter_upper(prompt_last)
    out_last = at.near_part(
        branch, after(attn_two, prompt_last), out_grad_far, out_grad_aside
    )
    grad_out = at.scatter_upper(out_last)
    kv_last = at.near_part(
        normed_keys, kv_grad, kv_grad_far, after(kv_grad_aside, out_last)
    )
    grad_kv = at.scatter_upper(kv_last)
    q_last = at.near_part(normed, queries_grad, q_grad_far, after(q_grad_aside, kv_last))
    grad_q = at.scatter_upper(q_last)
    here_grad = jnp.concatenate([after(prompt_grad, q_last), kv_grad[prompt_len:]], axis=0)

    def back_attn(half_of):
        return cols_product(half_of(queries_grad), q_full) + cols_product(
            half_of(here_grad), kv_full
        )

    normed_send = back_attn(at.other_half).astype(bf16)
    normed_sent = at.swap_tensor(normed_send)
    normed_grad = back_attn(at.own_half) + normed_sent.astype(f32)
    inv_first = inv_rms(tokens_f32, norm_eps)
    tokens_grad = residual_grad + norm_back(tokens_f32, inv_first, attn_gain_row, normed_grad)
    tokens_grad = at.from_relative(tokens_grad.astype(bf16))

    def row_sum(grad, weight):
        return jnp.sum(grad.astype(f32) * weight.astype(f32), axis=1)

    head_sums = at.sum_small(jnp.concatenate([head_sums[:, 0], head_sums[:, 1]], axis=1))
    head_gain_sum, lam_sum = head_sums[:, :DV], head_sums[:, DV]
    head_rows = head_gain.shape[0]
    grad_head_gain = lax.dynamic_slice_in_dim(head_gain_sum.T, at.index * head_rows, head_rows, 0)
    one_scale, two_scale = lam_sum * first_exp, -lam_sum * second_exp
    grad_q = grad_q.astype(f32)
    grad_kv = grad_kv.astype(f32).reshape(shard_rows, heads, -1)
    grad_k = grad_kv[:, :, : 2 * DK].reshape(shard_rows, -1)
    grad_v = grad_kv[:, :, 2 * DK :].reshape(shard_rows, -1)
    attn_gain_part = row_sum(grad_q, q_weight) + row_sum(grad_k, k_weight) + row_sum(grad_v, v_weight)
    ffn_gain_part = row_sum(grad_gate, gate_weight) + row_sum(grad_up, up_weight)
    attn_gain_sum = attn_gain_part + at.swap_tensor(attn_gain_part)
    ffn_gain_sum = ffn_gain_part + at.swap_tensor(ffn_gain_part)
    return (
        output,
        tokens_grad,
        grad_q,
        grad_k,
        grad_v,
        grad_out.astype(f32),
        attn_gain_sum / attn_gain.astype(f32),
        grad_head_gain,
        one_scale * lam_k1.astype(f32),
        one_scale * lam_q1.astype(f32),
        two_scale * lam_k2.astype(f32),
        two_scale * lam_q2.astype(f32),
        grad_gate.astype(f32),
        grad_up.astype(f32),
        grad_down.astype(f32),
        ffn_gain_sum / ffn_gain.astype(f32),
    )


def solution(mesh):
    rows = P(("dp", "tensor"), None)
    both = P("dp", "tensor")
    placed = (
        (rows, rows, P("dp", None))
        + (both,) * 4
        + (P("dp"),)
        + (both,) * 5
        + (both,) * 3
        + (P("dp"),)
    )
    return jax.shard_map(
        per_device,
        mesh=mesh,
        in_specs=placed,
        out_specs=(rows, rows)
        + (both,) * 4
        + (P("dp"),)
        + (both,) * 5
        + (both,) * 3
        + (P("dp"),),
        check_vma=False,
    )
```

```python
import jax
import jax.numpy as jnp
from jax import lax
from jax.experimental import pallas as pl
from jax.experimental.pallas import tpu as pltpu
from jax.sharding import PartitionSpec as P

D = 2048
DK = 128
DV = 256

norm_eps = 1e-06
head_eps = 1e-05
lambda_init = 0.2
masked_value = -1e30
f32 = jnp.float32
bf16 = jnp.bfloat16
CHUNK = 256


def inv_rms(entries, eps_value):
    return lax.rsqrt(jnp.mean(entries * entries, axis=-1, keepdims=True) + eps_value)


def norm_back(entries, inverse, gain_row, incoming):
    scaled = gain_row * incoming
    return inverse * scaled - entries * inverse**3 * jnp.mean(
        entries * scaled, axis=-1, keepdims=True
    )


def plain_product(first_arg, second_arg):
    return jnp.dot(first_arg, second_arg, preferred_element_type=f32)


def rows_product(first_arg, second_arg):
    return lax.dot_general(
        first_arg, second_arg, (((0,), (0,)), ((), ())), preferred_element_type=f32
    )


def cols_product(first_arg, second_arg):
    return lax.dot_general(
        first_arg, second_arg, (((1,), (1,)), ((), ())), preferred_element_type=f32
    )


def together(*values):
    return lax.optimization_barrier(values)


def after(value, *others):
    if not others:
        return value
    return lax.optimization_barrier((value,) + others)[0]


class Places:
    def __init__(self):
        self.count = lax.axis_size("dp")
        self.upper = self.count // 4
        index = lax.axis_index("dp")
        self.index = index
        self.core = index % 2
        self.side = (index // 2) % 2
        self.tensor = lax.axis_index("tensor")
        self.upper_groups = [
            [low + 4 * high for high in range(self.upper)] for low in range(4)
        ]
        self.core_pairs = [(k, k ^ 1) for k in range(self.count)]
        self.side_pairs = [(k, k ^ 2) for k in range(self.count)]

    def swap_core(self, value):
        return lax.ppermute(value, "dp", self.core_pairs)

    def swap_side(self, value):
        return lax.ppermute(value, "dp", self.side_pairs)

    def swap_tensor(self, value):
        return lax.ppermute(value, "tensor", [(0, 1), (1, 0)])

    def gather_upper(self, shard):
        return lax.all_gather(
            shard, "dp", axis=0, tiled=True, axis_index_groups=self.upper_groups
        )

    def gather_near(self, here, *others):
        here = after(here, *others)
        aside = self.swap_side(here)
        return [here, aside, self.swap_core(here), self.swap_core(aside)]

    def sum_small(self, value):
        step = 1
        while step < self.count:
            value = value + lax.ppermute(
                value, "dp", [(k, k ^ step) for k in range(self.count)]
            )
            step *= 2
        return value

    def block_order(self, value):
        parts = value.reshape((2, 2, self.upper) + value.shape[1:])
        parts = self.flip(self.flip(parts, 0, self.core), 1, self.side)
        order = (2, 1, 0) + tuple(range(3, parts.ndim))
        return jnp.transpose(parts, order).reshape(value.shape)

    def scatter_upper(self, value):
        return lax.psum_scatter(
            value, "dp", scatter_dimension=0, tiled=True, axis_index_groups=self.upper_groups
        )

    def product_part(self, first_arg, second_arg, part):
        quarter = first_arg.shape[1] // 4
        return rows_product(first_arg[:, part * quarter : (part + 1) * quarter], second_arg)

    def far_part(self, first_arg, second_arg, part):
        send = self.product_part(first_arg, second_arg, part).astype(bf16)
        return self.swap_core(send), send

    def aside_part(self, first_arg, second_arg, far):
        return (self.product_part(first_arg, second_arg, 1) + far.astype(f32)).astype(bf16)

    def near_part(self, first_arg, second_arg, far, aside):
        near = self.product_part(first_arg, second_arg, 0) + far.astype(f32)
        return (near + aside.astype(f32)).astype(bf16)

    def flip(self, value, axis, bit):
        return jnp.where(bit == 1, jnp.flip(value, axis), value)

    def to_relative(self, value):
        lead = value.shape[:-1]
        parts = value.reshape(lead + (self.upper, 2, 2, value.shape[-1] // self.count))
        k = len(lead)
        order = tuple(range(k)) + (k + 2, k + 1, k, k + 3)
        parts = jnp.transpose(parts, order)
        parts = self.flip(self.flip(parts, k, self.core), k + 1, self.side)
        return parts.reshape(value.shape)

    def from_relative(self, value):
        lead = value.shape[:-1]
        parts = value.reshape(lead + (2, 2, self.upper, value.shape[-1] // self.count))
        k = len(lead)
        parts = self.flip(self.flip(parts, k, self.core), k + 1, self.side)
        order = tuple(range(k)) + (k + 2, k + 1, k, k + 3)
        return jnp.transpose(parts, order).reshape(value.shape)

    def relative_blocks(self):
        spot = jnp.arange(self.count, dtype=jnp.int32)
        core = spot // (2 * self.upper)
        side = (spot // self.upper) % 2
        high = spot % self.upper
        return high * 4 + (side ^ self.side) * 2 + (core ^ self.core)

    def own_half(self, rows):
        half = rows.shape[0] // 2
        return lax.dynamic_slice_in_dim(rows, self.tensor * half, half, 0)

    def other_half(self, rows):
        half = rows.shape[0] // 2
        return lax.dynamic_slice_in_dim(rows, (1 - self.tensor) * half, half, 0)

    def in_order(self, own, other):
        return jnp.where(
            self.tensor == 0,
            jnp.concatenate([own, other], axis=0),
            jnp.concatenate([other, own], axis=0),
        )


def dot_nt(first, second):
    return lax.dot_general(first, second, (((1,), (1,)), ((), ())), preferred_element_type=f32)


def dot_nn(first, second):
    return lax.dot_general(first, second, (((1,), (0,)), ((), ())), preferred_element_type=f32)


def dot_tn(first, second):
    return lax.dot_general(first, second, (((0,), (0,)), ((), ())), preferred_element_type=f32)


def forward_kernel(
    prompt_len, top_rows, first_head, lam_ref, q_ref, kv_ref, gain_ref, spot_ref, reach_ref, low_ref, high_ref,
    out_ref, vec_ref, lse_ref, one_ref, two_ref, stat_ref,
):
    lam = lam_ref[first_head + pl.program_id(0)]
    rows, keys = q_ref.shape[0], kv_ref.shape[0]
    scale = DK ** (-0.5)
    scores = (one_ref, two_ref)

    def chunk_scores(chunk):
        for comp in range(2):
            lanes = slice(comp * DK, (comp + 1) * DK)
            scores[comp][chunk] = dot_nt(q_ref[:, lanes], kv_ref[pl.ds(chunk * CHUNK, CHUNK), lanes])

    def prompt_chunk(chunk, tops):
        chunk_scores(chunk)
        spots = spot_ref[chunk]
        for comp in range(2):
            ref = scores[comp]
            for part in range(CHUNK // 128):
                lanes = slice(part * 128, (part + 1) * 128)
                ref[chunk, :top_rows, lanes] = jnp.where(
                    spots[:, lanes] <= reach_ref[...], ref[chunk, :top_rows, lanes], masked_value
                )
        return 0

    def cont_chunk(chunk, tops):
        chunk_scores(chunk)
        first = chunk * CHUNK - prompt_len
        for part in range(CHUNK // 128):
            lanes = slice(part * 128, (part + 1) * 128)
            spot = lax.broadcasted_iota(jnp.int32, (rows, 128), 1) + (first + part * 128)
            allowed = (spot >= low_ref[...]) & (spot <= high_ref[...])
            for comp in range(2):
                ref = scores[comp]
                ref[chunk, :, lanes] = jnp.where(allowed, ref[chunk, :, lanes], masked_value)
        return 0

    first_cont = prompt_len // CHUNK
    count = keys // CHUNK
    lax.fori_loop(0, first_cont, prompt_chunk, 0)
    lax.fori_loop(first_cont, count, cont_chunk, 0)

    ROWS = 32
    def row_block(block, carry):
        span = pl.ds(pl.multiple_of(block * ROWS, ROWS), ROWS)
        totals = []
        for comp in range(2):
            ref = scores[comp]
            top = ref[0, span, :128]
            for chunk in range(count):
                for part in range(CHUNK // 128):
                    if chunk + part > 0:
                        top = jnp.maximum(top, ref[chunk, span, part * 128 : (part + 1) * 128])
            top = jnp.max(top, axis=1, keepdims=True)
            total = jnp.zeros((ROWS, 128), f32)
            for chunk in range(count):
                for part in range(CHUNK // 128):
                    lanes = slice(part * 128, (part + 1) * 128)
                    terms = jnp.exp((ref[chunk, span, lanes] - top) * scale)
                    total = total + terms
                    ref[chunk, span, lanes] = terms
            total = jnp.sum(total, axis=1, keepdims=True)
            totals.append(total)
            stat_ref[comp, span, :] = jnp.broadcast_to(top * scale + jnp.log(total), (ROWS, 128))
        first = 1.0 / totals[0]
        second = lam / totals[1]
        for chunk in range(count):
            for part in range(CHUNK // 128):
                lanes = slice(part * 128, (part + 1) * 128)
                one_ref[chunk, span, lanes] = (
                    one_ref[chunk, span, lanes] * first - two_ref[chunk, span, lanes] * second
                )
        return carry

    lax.fori_loop(0, rows // ROWS, row_block, 0)

    turn = (lax.broadcasted_iota(jnp.int32, (8, 128), 1) == 0).astype(f32)
    for comp in range(2):
        lse_ref[0, comp * 8 : (comp + 1) * 8, :] = lax.dot_general(
            turn,
            stat_ref[comp],
            (((1,), (1,)), ((), ())),
            precision=lax.Precision.HIGHEST,
            preferred_element_type=f32,
        )
    out_ref[...] = jnp.zeros_like(out_ref)

    def mix(chunk, carry):
        out_ref[...] += dot_nn(
            one_ref[chunk].astype(bf16), kv_ref[pl.ds(chunk * CHUNK, CHUNK), 2 * DK :]
        )
        return carry

    lax.fori_loop(0, count, mix, 0)
    out = out_ref[...]
    inverse = lax.rsqrt(jnp.mean(out * out, axis=1, keepdims=True) + head_eps)
    vec_ref[...] = (out * inverse * gain_ref[...] * (1.0 - lambda_init)).astype(bf16)


def backward_kernel(
    prompt_len, top_rows, first_head, lam_ref, q_ref, kv_ref, gain_ref, vec_ref, out_ref, lse_ref, spot_ref, reach_ref,
    dq_ref, dkv_ref, sums_ref, one_ref, two_ref, mix_ref, grad_ref, turn_ref,
):
    lam = lam_ref[first_head + pl.program_id(0)]
    rows, keys = q_ref.shape[0], kv_ref.shape[0]
    scale = DK ** (-0.5)
    out = out_ref[...]
    vec = vec_ref[...]
    inverse = lax.rsqrt(jnp.mean(out * out, axis=1, keepdims=True) + head_eps)
    plain = vec * out * inverse * (1.0 - lambda_init)
    scaled = vec * gain_ref[...] * (1.0 - lambda_init)
    grad_ref[...] = (
        inverse * scaled - out * inverse**3 * jnp.mean(out * scaled, axis=1, keepdims=True)
    ).astype(bf16)
    gain_part = jnp.sum(plain, axis=0, keepdims=True)
    grad = grad_ref[...]
    count = keys // CHUNK
    first_cont = prompt_len // CHUNK

    def weigh(chunk):
        span = pl.ds(pl.multiple_of(chunk * CHUNK, CHUNK), CHUNK)
        for comp, ref in ((0, one_ref), (1, two_ref)):
            lanes = slice(comp * DK, (comp + 1) * DK)
            scores = dot_nt(kv_ref[span, lanes], q_ref[:, lanes])
            ref[chunk] = jnp.exp(scores * scale - lse_ref[0, 8 * comp : 8 * comp + 1, :])
        mix_ref[chunk] = dot_nt(kv_ref[span, 2 * DK :], grad)

    def gather_sums(chunk, sums):
        span = pl.ds(pl.multiple_of(chunk * CHUNK, CHUNK), CHUNK)
        one, two, mix = one_ref[chunk], two_ref[chunk], mix_ref[chunk]
        mixed = (one - lam * two).astype(bf16)
        dkv_ref[span, 2 * DK :] = dot_nn(mixed, grad).astype(bf16)
        return (
            sums[0] + jnp.sum((one * mix).reshape(CHUNK // 8, 8, rows), axis=0),
            sums[1] + jnp.sum((two * mix).reshape(CHUNK // 8, 8, rows), axis=0),
        )

    def prompt_chunk(chunk, sums):
        weigh(chunk)
        allowed = spot_ref[pl.ds(chunk * CHUNK, CHUNK), :top_rows] <= reach_ref[0:1, :top_rows]
        for ref in (one_ref, two_ref):
            ref[chunk, :, :top_rows] = jnp.where(allowed, ref[chunk, :, :top_rows], 0.0)
        return gather_sums(chunk, sums)

    def cont_chunk(chunk, sums):
        weigh(chunk)
        spot = lax.broadcasted_iota(jnp.int32, (CHUNK, rows), 0) + (chunk * CHUNK - prompt_len)
        allowed = (spot >= reach_ref[1:2, :]) & (spot <= reach_ref[2:3, :])
        for ref in (one_ref, two_ref):
            ref[chunk] = jnp.where(allowed, ref[chunk], 0.0)
        return gather_sums(chunk, sums)

    sums = (jnp.zeros((8, rows), f32), jnp.zeros((8, rows), f32))
    sums = lax.fori_loop(0, first_cont, prompt_chunk, sums)
    sums = lax.fori_loop(first_cont, count, cont_chunk, sums)
    first = jnp.sum(sums[0], axis=0, keepdims=True)
    second = jnp.sum(sums[1], axis=0, keepdims=True)
    sums_ref[0, 0:1, :] = gain_part
    sums_ref[0, 1:2, :] = jnp.broadcast_to(-jnp.sum(second, axis=1, keepdims=True), (1, DV))
    turn_ref[...] = jnp.zeros_like(turn_ref)

    def back(chunk, carry):
        span = pl.ds(pl.multiple_of(chunk * CHUNK, CHUNK), CHUNK)
        mix = mix_ref[chunk]
        grads = (
            (one_ref[chunk] * (mix - first)).astype(bf16),
            (two_ref[chunk] * ((mix - second) * (-lam))).astype(bf16),
        )
        for comp in range(2):
            lanes = slice(comp * DK, (comp + 1) * DK)
            dkv_ref[span, lanes] = (dot_nn(grads[comp], q_ref[:, lanes]) * scale).astype(bf16)
            turn_ref[lanes, :] += dot_tn(kv_ref[span, lanes], grads[comp])
        return carry

    lax.fori_loop(0, count, back, 0)
    dq_ref[...] = (turn_ref[...] * scale).astype(bf16)


def attend(queries, keys_values, lam_vec, gain_rows, prompt_spots, bounds, prompt_part, span):
    first, heads = span[0], span[1] - span[0]
    rows, keys = queries.shape[0], keys_values.shape[0]
    prompt_len = prompt_spots.shape[0]
    top_rows = min(rows, -(-prompt_part // 16) * 16)
    wide = [jnp.broadcast_to(bound[:, None], (rows, 128)) for bound in bounds]
    count = keys // CHUNK
    return pl.pallas_call(
        lambda *refs: forward_kernel(prompt_len, top_rows, first, *refs),
        grid=(heads,),
        in_specs=[
            pl.BlockSpec(memory_space=pltpu.SMEM),
            pl.BlockSpec((rows, 2 * DK), lambda h: (0, h + first)),
            pl.BlockSpec((keys, 2 * DK + DV), lambda h: (0, h + first)),
            pl.BlockSpec((1, DV), lambda h: (0, h + first)),
            pl.BlockSpec((prompt_len // CHUNK, 1, CHUNK), lambda h: (0, 0, 0)),
            pl.BlockSpec((top_rows, 128), lambda h: (0, 0)),
            pl.BlockSpec((rows, 128), lambda h: (0, 0)),
            pl.BlockSpec((rows, 128), lambda h: (0, 0)),
        ],
        out_specs=[
            pl.BlockSpec((rows, DV), lambda h: (0, h)),
            pl.BlockSpec((rows, DV), lambda h: (0, h)),
            pl.BlockSpec((1, 16, rows), lambda h: (h, 0, 0)),
        ],
        out_shape=[
            jax.ShapeDtypeStruct((rows, heads * DV), f32),
            jax.ShapeDtypeStruct((rows, heads * DV), bf16),
            jax.ShapeDtypeStruct((heads, 16, rows), f32),
        ],
        scratch_shapes=[
            pltpu.VMEM((count, rows, CHUNK), f32),
            pltpu.VMEM((count, rows, CHUNK), f32),
            pltpu.VMEM((2, rows, 128), f32),
        ],
        compiler_params=pltpu.CompilerParams(vmem_limit_bytes=56 * 2**20),
        name="attend",
        cost_estimate=pl.CostEstimate(
            flops=12_000_000_000, transcendentals=0, bytes_accessed=0
        ),
    )(
        lam_vec,
        queries,
        keys_values,
        gain_rows,
        prompt_spots.reshape(prompt_len // CHUNK, 1, CHUNK),
        wide[0][:top_rows],
        wide[1],
        wide[2],
    )


def attend_back(
    queries, keys_values, lam_vec, gain_rows, vec_grad, out, lse, prompt_spots, bounds, prompt_part, span
):
    first, heads = span[0], span[1] - span[0]
    rows, keys = queries.shape[0], keys_values.shape[0]
    prompt_len = prompt_spots.shape[0]
    top_rows = min(rows, -(-prompt_part // 128) * 128)
    count = keys // CHUNK
    reach = jnp.concatenate([jnp.stack(bounds), jnp.zeros((5, rows), jnp.int32)])
    return pl.pallas_call(
        lambda *refs: backward_kernel(prompt_len, top_rows, first, *refs),
        grid=(heads,),
        in_specs=[
            pl.BlockSpec(memory_space=pltpu.SMEM),
            pl.BlockSpec((rows, 2 * DK), lambda h: (0, h + first)),
            pl.BlockSpec((keys, 2 * DK + DV), lambda h: (0, h + first)),
            pl.BlockSpec((1, DV), lambda h: (0, h + first)),
            pl.BlockSpec((rows, DV), lambda h: (0, h + first)),
            pl.BlockSpec((rows, DV), lambda h: (0, h + first)),
            pl.BlockSpec((1, 16, rows), lambda h: (h + first, 0, 0)),
            pl.BlockSpec((prompt_len, 128), lambda h: (0, 0)),
            pl.BlockSpec((8, rows), lambda h: (0, 0)),
        ],
        out_specs=[
            pl.BlockSpec((2 * DK, rows), lambda h: (h, 0)),
            pl.BlockSpec((keys, 2 * DK + DV), lambda h: (0, h)),
            pl.BlockSpec((1, 8, DV), lambda h: (h, 0, 0)),
        ],
        out_shape=[
            jax.ShapeDtypeStruct((heads * 2 * DK, rows), bf16),
            jax.ShapeDtypeStruct((keys, heads * (2 * DK + DV)), bf16),
            jax.ShapeDtypeStruct((heads, 8, DV), f32),
        ],
        scratch_shapes=[
            pltpu.VMEM((count, CHUNK, rows), f32),
            pltpu.VMEM((count, CHUNK, rows), f32),
            pltpu.VMEM((count, CHUNK, rows), f32),
            pltpu.VMEM((rows, DV), bf16),
            pltpu.VMEM((2 * DK, rows), f32),
        ],
        compiler_params=pltpu.CompilerParams(vmem_limit_bytes=58 * 2**20),
        name="attend_back",
        cost_estimate=pl.CostEstimate(
            flops=24_000_000_000, transcendentals=0, bytes_accessed=0
        ),
    )(
        lam_vec,
        queries,
        keys_values,
        gain_rows,
        vec_grad,
        out,
        lse,
        jnp.broadcast_to(prompt_spots[:, None], (prompt_len, 128)),
        reach,
    )


def norm_kernel(count, blocks_ref, swap_ref, *refs):
    *sources, gain_ref, out_ref = refs
    step = pl.program_id(0)
    rows, depth = out_ref.shape
    block = depth // count
    upper = count // 4
    straight = swap_ref[0] == 0

    def norm_from(pieces):
        total = jnp.zeros((rows, 1), f32)
        for piece in pieces:
            x = piece[:rows, :].astype(f32)
            total = total + jnp.sum(x * x, axis=1, keepdims=True)
        inverse = lax.rsqrt(total * (1.0 / depth) + norm_eps)
        size = depth // len(pieces)
        for spot in range(count):
            lanes = slice(spot * block, (spot + 1) * block)
            side = (spot % upper) * 4 * block // size
            start = pl.multiple_of(blocks_ref[spot] * block - side * size, block)
            part = pieces[side][:rows, pl.ds(start, block)]
            if len(pieces) == 2:
                part = jnp.where(straight, part, pieces[1 - side][:rows, pl.ds(start, block)])
            out_ref[:, lanes] = (part.astype(f32) * inverse * gain_ref[:, lanes]).astype(bf16)

    for core in range(2):

        @pl.when((step >= core * 2 * upper) & (step < (core + 1) * 2 * upper))
        def _():
            norm_from(sources[2 * core : 2 * core + 2])

    @pl.when(step >= count)
    def _():
        norm_from(sources[4:5])


def norm_keys(at, prompt_groups, tokens_all, gain_row, prompt_part):
    depth = tokens_all.shape[1]
    count, upper = at.count, at.upper
    cont_len = tokens_all.shape[0] - prompt_part
    unit = prompt_groups[0].shape[0] // (2 * upper)
    if (depth // count) % 128 or cont_len % prompt_part or upper % 2:
        cores = []
        for pair in (prompt_groups[:2], prompt_groups[2:]):
            parts = jnp.stack([part.reshape(2 * upper, unit, -1)[:, :prompt_part] for part in pair])
            parts = at.flip(parts.reshape(2, 2 * upper * prompt_part, depth // 2), 0, at.tensor)
            cores.append(jnp.concatenate([parts[0], parts[1]], axis=1))
        rows = at.to_relative(jnp.concatenate(cores + [tokens_all[prompt_part:]], axis=0))
        rows = rows.astype(f32)
        return (rows * inv_rms(rows, norm_eps) * gain_row).astype(bf16)

    def spot_of(core):
        first = core * 2 * upper
        return lambda i, blocks, swap: (jnp.clip(i - first, 0, 2 * upper - 1), 0)

    return pl.pallas_call(
        lambda *refs: norm_kernel(count, *refs),
        grid_spec=pltpu.PrefetchScalarGridSpec(
            num_scalar_prefetch=2,
            grid=(count + cont_len // prompt_part,),
            in_specs=[
                pl.BlockSpec((unit, depth // 2), spot_of(core)) for core in (0, 0, 1, 1)
            ]
            + [
                pl.BlockSpec(
                    (prompt_part, depth),
                    lambda i, blocks, swap: (1 + jnp.maximum(i - count, 0), 0),
                ),
                pl.BlockSpec((1, depth), lambda i, blocks, swap: (0, 0)),
            ],
            out_specs=pl.BlockSpec((prompt_part, depth), lambda i, blocks, swap: (i, 0)),
        ),
        out_shape=jax.ShapeDtypeStruct((prompt_part * count + cont_len, depth), bf16),
        name="norm_keys",
        cost_estimate=pl.CostEstimate(flops=8_000_000_000, transcendentals=0, bytes_accessed=0),
    )(
        at.relative_blocks(),
        at.tensor.reshape(1).astype(jnp.int32),
        *prompt_groups,
        tokens_all,
        gain_row.reshape(1, depth),
    )


def per_device(
    tokens,
    cotangent,
    cont_ids,
    q_weight,
    k_weight,
    v_weight,
    out_weight,
    attn_gain,
    head_gain,
    lam_q1,
    lam_k1,
    lam_q2,
    lam_k2,
    gate_weight,
    up_weight,
    down_weight,
    ffn_gain,
):
    at = Places()
    local_rows = tokens.shape[0]
    block_rows = 2 * local_rows
    row_ids = cont_ids[0]
    cont_len = row_ids.shape[0]
    prompt_part = block_rows - cont_len
    prompt_len = prompt_part * at.count
    heads = q_weight.shape[1] // (2 * DK)
    width = heads * 2 * DK
    shard_rows = q_weight.shape[0]

    small_parts = (attn_gain, ffn_gain, head_gain, lam_q1, lam_k1, lam_q2, lam_k2)
    small = jnp.concatenate([part.reshape(-1) for part in small_parts])
    half = D // 2
    small_rows = jnp.zeros((16, half), bf16).at[0, : small.size].set(small)
    prompt_sent = lax.ppermute(tokens[:prompt_part, half:], "tensor", [(0, 1)])
    prompt_own = jnp.where(at.tensor == 0, tokens[:prompt_part, :half], prompt_sent)
    prompt_own = jnp.concatenate([prompt_own, small_rows], axis=0)
    prompt_here = at.gather_upper(prompt_own)

    def by_head(weight):
        return weight.reshape(shard_rows, heads, -1)

    kv_here = at.gather_upper(
        after(
            jnp.concatenate([by_head(k_weight), by_head(v_weight)], axis=2).reshape(
                shard_rows, -1
            ),
            prompt_own,
        )
    )
    q_here = at.gather_upper(after(q_weight, prompt_own))
    out_here = at.gather_upper(after(out_weight, prompt_own))
    gate_here = at.gather_upper(after(gate_weight, prompt_own))
    up_here = at.gather_upper(after(up_weight, prompt_own))
    down_here = at.gather_upper(after(down_weight, prompt_own))

    tokens_rel = at.to_relative(tokens)
    cot_rel = at.to_relative(cotangent)
    tokens_turned = at.swap_tensor(after(tokens, prompt_own))
    prompt_here, tokens_rel, cot_rel, tokens_turned = together(
        prompt_here, tokens_rel, cot_rel, tokens_turned
    )
    prompt_pair = jnp.concatenate([prompt_here, at.swap_side(prompt_here)], axis=0)
    prompt_turned = at.swap_tensor(prompt_pair)
    prompt_far = at.swap_core(prompt_pair)
    kv_here = after(kv_here, prompt_pair)
    kv_side, kv_near = at.swap_side(kv_here), at.swap_core(kv_here)
    prompt_turned, kv_side_early = together(prompt_turned, kv_near)
    kv_near = kv_side_early
    prompt_far_turned = at.swap_core(prompt_turned)
    kv_side, q_here = together(kv_side, q_here)
    kv_far = at.swap_core(kv_side)
    q_side, q_near = at.swap_side(q_here), at.swap_core(q_here)
    prompt_far, prompt_far_turned = together(prompt_far, after(prompt_far_turned, kv_side))
    tokens_all = at.in_order(tokens, tokens_turned)
    cot_turned = at.swap_tensor(after(cot_rel, prompt_far_turned))

    small_all = jnp.concatenate(
        [
            group.reshape(2 * at.upper, -1, half)[:, prompt_part, : small.size]
            for group in (prompt_pair, prompt_far)
        ],
        axis=0,
    ).astype(f32)
    small_full = []
    start = 0
    for part in small_parts:
        small_full.append(
            small_all[:, start : start + part.size].reshape((at.count,) + part.shape)
        )
        start += part.size
    attn_gain_row = small_full[0].reshape(-1)
    ffn_gain_row = small_full[1].reshape(-1)
    head_gain_row = at.block_order(small_full[2]).reshape(DV, heads).T.reshape(1, heads * DV)
    first_exp = jnp.exp(jnp.sum(small_full[3] * small_full[4], axis=(0, 1)))
    second_exp = jnp.exp(jnp.sum(small_full[5] * small_full[6], axis=(0, 1)))
    lam_vec = first_exp - second_exp + lambda_init

    prompt_spots = (
        at.relative_blocks()[:, None] * prompt_part
        + jnp.arange(prompt_part, dtype=jnp.int32)[None]
    ).reshape(-1)
    cont_spot = jnp.arange(cont_len, dtype=jnp.int32)
    earlier = jnp.sum((row_ids[None, :] < row_ids[:, None]).astype(jnp.int32), axis=1)
    far_spot = jnp.full((prompt_part,), prompt_len + cont_len, jnp.int32)
    reach = jnp.concatenate(
        [
            at.index * prompt_part + jnp.arange(prompt_part, dtype=jnp.int32),
            jnp.full((cont_len,), prompt_len, jnp.int32),
        ]
    )
    bounds = (
        reach,
        jnp.concatenate([far_spot, earlier]),
        jnp.concatenate([jnp.full((prompt_part,), -1, jnp.int32), cont_spot]),
    )

    tokens_f32 = tokens_rel.astype(f32)
    prompt_groups = (prompt_pair, prompt_turned, prompt_far, prompt_far_turned)
    normed_keys = norm_keys(at, prompt_groups, tokens_all, attn_gain_row, prompt_part)
    kv_near, kv_far = after(kv_near, normed_keys), after(kv_far, normed_keys)
    kv_full = jnp.concatenate([kv_here, kv_side, kv_near, kv_far], axis=0)
    kv_full, q_side, out_here = together(kv_full, q_side, out_here)
    q_far = at.swap_core(q_side)
    out_side, out_near = at.swap_side(out_here), at.swap_core(out_here)
    own_block = lax.dynamic_slice_in_dim(
        normed_keys, (at.index // 4) * prompt_part, prompt_part, 0
    )
    normed = jnp.concatenate([own_block, normed_keys[prompt_len:]], axis=0)
    keys_values = plain_product(normed_keys, kv_full).astype(bf16)
    q_near, q_far = after(q_near, keys_values), after(q_far, keys_values)
    q_full = jnp.concatenate([q_here, q_side, q_near, q_far], axis=0)
    queries = plain_product(after(normed, keys_values), q_full).astype(bf16)
    fixed = (lam_vec, head_gain_row, prompt_spots, bounds, prompt_part)
    middle = heads // 2
    queries, out_side, gate_here = together(queries, out_side, gate_here)
    out_far = at.swap_core(out_side)
    gate_side, gate_near = at.swap_side(gate_here), at.swap_core(gate_here)
    first_out, first_vec, first_lse = attend(queries, keys_values, *fixed, (0, middle))
    first_vec, cot_turned = together(first_vec, cot_turned)
    second_out, second_vec, second_lse = attend(
        after(queries, first_vec), keys_values, *fixed, (middle, heads)
    )
    second_vec, up_here, gate_side = together(second_vec, up_here, gate_side)
    up_side, up_near = at.swap_side(up_here), at.swap_core(up_here)
    gate_far = at.swap_core(gate_side)
    out_near, out_far = after(out_near, second_vec), after(out_far, second_vec)
    heads_out = jnp.concatenate([first_out, second_out], axis=1)
    lse = jnp.concatenate([first_lse, second_lse], axis=0)
    attn_vec = jnp.concatenate([first_vec, second_vec], axis=1)
    out_full = jnp.concatenate([out_here, out_side, out_near, out_far], axis=0)
    attn_own, attn_other = at.own_half(attn_vec), at.other_half(attn_vec)
    out_send = cols_product(attn_other, out_full).astype(bf16)
    out_sent = at.swap_tensor(out_send)
    out_part = cols_product(after(attn_own, out_send), out_full)
    attn_two = jnp.concatenate([attn_own, attn_other], axis=0)
    out_part, attn_two = together(out_part, attn_two)
    out_sent = after(out_sent, out_part)
    residual = tokens_f32 + (out_part + out_sent.astype(f32))

    inv_second = inv_rms(residual, norm_eps)
    ffn_own = (residual * inv_second * ffn_gain_row).astype(bf16)
    ffn_turned = at.swap_tensor(ffn_own)
    gate_near, gate_far = after(gate_near, ffn_own), after(gate_far, ffn_own)
    gate_full = jnp.concatenate([gate_here, gate_side, gate_near, gate_far], axis=0)
    gate_full, down_here, up_side = together(gate_full, down_here, up_side)
    up_far = at.swap_core(up_side)
    down_side, down_near = at.swap_side(down_here), at.swap_core(down_here)
    ffn_turned = after(ffn_turned, gate_full)
    ffn_in = jnp.concatenate([ffn_own, ffn_turned], axis=0)
    gate_proj = plain_product(ffn_in, gate_full)
    cot_rows = jnp.concatenate([cot_rel, cot_turned], axis=0)
    up_near, up_far = after(up_near, gate_proj), after(up_far, gate_proj)
    up_full = jnp.concatenate([up_here, up_side, up_near, up_far], axis=0)
    up_proj = plain_product(after(ffn_in, gate_proj), up_full)
    gate_sigmoid = jax.nn.sigmoid(gate_proj)
    hidden = (gate_proj * gate_sigmoid * up_proj).astype(bf16)

    down_far_aside, down_send = at.far_part(cot_rows, hidden, 3)
    down_far_keep, down_send = at.far_part(cot_rows, after(hidden, down_send), 2)
    down_send, down_side = together(down_send, down_side)
    down_near = after(down_near, down_side)
    down_far = at.swap_core(down_side)
    down_far_aside = after(down_far_aside, down_side)
    down_grad_side = at.aside_part(cot_rows, hidden, down_far_aside)
    down_grad_aside = at.swap_side(down_grad_side)
    down_near, down_far = after(down_near, down_grad_side), after(down_far, down_grad_side)
    down_full = jnp.concatenate([down_here, down_side, down_near, down_far], axis=0)
    hidden_grad = plain_product(cot_rows, down_full)
    gate_grad = (
        hidden_grad * up_proj * gate_sigmoid * (1.0 + gate_proj * (1.0 - gate_sigmoid))
    ).astype(bf16)
    up_grad = (hidden_grad * gate_proj * gate_sigmoid).astype(bf16)

    def back_ffn(one, two):
        return cols_product(one, gate_full) + cols_product(two, up_full)

    gate_far_aside, gate_send = at.far_part(ffn_in, gate_grad, 3)
    ffn_send = back_ffn(
        after(gate_grad[local_rows:], gate_send), up_grad[local_rows:]
    ).astype(bf16)
    ffn_sent = at.swap_tensor(ffn_send)
    ffn_part = back_ffn(after(gate_grad[:local_rows], ffn_send), up_grad[:local_rows])
    gate_far_aside = after(gate_far_aside, ffn_part)
    gate_grad_side = at.aside_part(ffn_in, gate_grad, gate_far_aside)
    gate_grad_aside = at.swap_side(gate_grad_side)
    down_grad_aside = after(down_grad_aside, gate_grad_side)
    ffn_in_grad = ffn_part + after(ffn_sent, down_grad_aside).astype(f32)
    residual_grad = cot_rel.astype(f32) + norm_back(
        residual, inv_second, ffn_gain_row, ffn_in_grad
    )

    branch_own = residual_grad.astype(bf16)
    branch_sent = at.swap_tensor(branch_own)
    down_far_keep = after(down_far_keep, branch_own)
    down_last = at.near_part(cot_rows, hidden, down_far_keep, down_grad_aside)
    grad_down = at.scatter_upper(down_last)
    up_far_aside, up_send = at.far_part(ffn_in, after(up_grad, down_last), 3)
    up_far_keep, up_send = at.far_part(ffn_in, after(up_grad, up_send), 2)
    gate_far_keep, gate_send = at.far_part(ffn_in, after(gate_grad, up_send), 2)
    up_far_aside = after(up_far_aside, gate_send)
    up_grad_side = at.aside_part(ffn_in, up_grad, up_far_aside)
    branch = jnp.concatenate([branch_own, after(branch_sent, up_grad_side)], axis=0)
    vec_two = plain_product(branch, out_full)
    vec_grad = at.in_order(vec_two[:local_rows], vec_two[local_rows:])
    vec_grad, gate_far_keep, gate_grad_aside = together(vec_grad, gate_far_keep, gate_grad_aside)
    up_grad_aside = at.swap_side(after(up_grad_side, gate_grad_aside))
    gate_last = at.near_part(ffn_in, gate_grad, gate_far_keep, gate_grad_aside)
    grad_gate = at.scatter_upper(gate_last)
    queries_grad, kv_grad, head_sums = attend_back(
        queries,
        keys_values,
        lam_vec,
        head_gain_row,
        after(vec_grad, gate_last),
        heads_out,
        lse,
        prompt_spots,
        bounds,
        prompt_part,
        (0, heads),
    )
    queries_grad, kv_grad, head_sums, grad_down = together(
        queries_grad, kv_grad, head_sums, grad_down
    )
    queries_grad = queries_grad.T

    quarter = prompt_len // 4

    def prompt_rows(part):
        return kv_grad[part * quarter : (part + 1) * quarter]

    prompt_send = prompt_rows(3)
    prompt_far_aside = at.swap_core(prompt_send)
    prompt_keep = after(prompt_rows(2), prompt_send)
    prompt_far_keep = at.swap_core(prompt_keep)
    kv_far_aside, kv_send = at.far_part(normed_keys, after(kv_grad, prompt_keep), 3)
    kv_send, up_far_keep, up_grad_aside = together(kv_send, up_far_keep, up_grad_aside)
    prompt_far_aside = after(prompt_far_aside, up_grad_aside)
    prompt_side = (prompt_rows(1).astype(f32) + prompt_far_aside.astype(f32)).astype(bf16)
    prompt_aside = at.swap_side(prompt_side)
    up_last = at.near_part(ffn_in, after(up_grad, prompt_side), up_far_keep, up_grad_aside)
    up_last, grad_gate = together(up_last, grad_gate)
    grad_up = at.scatter_upper(up_last)
    kv_far_keep, kv_send = at.far_part(normed_keys, after(kv_grad, up_last), 2)
    kv_far_aside = after(kv_far_aside, kv_send)
    kv_grad_side = at.aside_part(normed_keys, kv_grad, kv_far_aside)
    kv_grad_aside = at.swap_side(kv_grad_side)
    q_far_aside, q_send = at.far_part(normed, after(queries_grad, kv_grad_side), 3)
    q_far_keep, q_send = at.far_part(normed, after(queries_grad, q_send), 2)
    out_far_aside, out_send_grad = at.far_part(branch, after(attn_two, q_send), 3)
    out_far_keep, out_send_grad = at.far_part(branch, after(attn_two, out_send_grad), 2)
    hidden_late = after(hidden, out_send_grad)
    output_part = cols_product(hidden_late[:local_rows], down_full)
    prompt_far_keep, prompt_aside = together(after(prompt_far_keep, output_part), prompt_aside)
    prompt_last = (
        prompt_rows(0).astype(f32) + prompt_far_keep.astype(f32) + prompt_aside.astype(f32)
    ).astype(bf16)
    prompt_grad = at.scatter_upper(prompt_last)
    q_far_aside = after(q_far_aside, prompt_last)
    q_grad_side = at.aside_part(normed, queries_grad, q_far_aside)
    q_grad_aside = at.swap_side(q_grad_side)
    out_far_aside = after(out_far_aside, q_grad_side)
    out_grad_side = at.aside_part(branch, attn_two, out_far_aside)
    out_grad_aside = at.swap_side(out_grad_side)
    output_send = cols_product(after(hidden_late, out_grad_side)[local_rows:], down_full).astype(bf16)
    output_sent = at.swap_tensor(output_send)
    kv_far_keep, kv_grad_aside = together(after(kv_far_keep, output_send), kv_grad_aside)
    kv_last = at.near_part(normed_keys, kv_grad, kv_far_keep, kv_grad_aside)
    grad_kv = at.scatter_upper(kv_last)
    output_sent, grad_up, q_far_keep = together(after(output_sent, kv_last), grad_up, q_far_keep)
    q_far_keep, q_grad_aside = together(q_far_keep, q_grad_aside)
    q_last = at.near_part(normed, queries_grad, q_far_keep, q_grad_aside)
    grad_q = at.scatter_upper(q_last)
    prompt_grad = after(prompt_grad, q_last)
    here_grad = jnp.concatenate([prompt_grad, kv_grad[prompt_len:]], axis=0)

    def back_attn(half_of):
        return cols_product(half_of(queries_grad), q_full) + cols_product(
            half_of(here_grad), kv_full
        )

    normed_send = back_attn(at.other_half).astype(bf16)
    normed_sent = at.swap_tensor(normed_send)
    out_far_keep, out_grad_aside = together(after(out_far_keep, normed_send), out_grad_aside)
    out_last = at.near_part(branch, attn_two, out_far_keep, out_grad_aside)
    grad_out = at.scatter_upper(out_last)
    normed_part = back_attn(lambda rows: at.own_half(after(rows, out_last)))
    normed_grad = normed_part + normed_sent.astype(f32)
    inv_first = inv_rms(tokens_f32, norm_eps)
    tokens_grad = residual_grad + norm_back(tokens_f32, inv_first, attn_gain_row, normed_grad)
    tokens_grad = at.from_relative(tokens_grad.astype(bf16))
    output = at.from_relative((residual + (output_part + output_sent.astype(f32))).astype(bf16))

    def row_sum(grad, weight):
        return jnp.sum(grad.astype(f32) * weight.astype(f32), axis=1)

    head_sums = at.sum_small(jnp.concatenate([head_sums[:, 0], head_sums[:, 1]], axis=1))
    head_gain_sum, lam_sum = head_sums[:, :DV], head_sums[:, DV]
    head_rows = head_gain.shape[0]
    grad_head_gain = lax.dynamic_slice_in_dim(head_gain_sum.T, at.index * head_rows, head_rows, 0)
    one_scale, two_scale = lam_sum * first_exp, -lam_sum * second_exp
    grad_q = grad_q.astype(f32)
    grad_kv = grad_kv.astype(f32).reshape(shard_rows, heads, -1)
    grad_k = grad_kv[:, :, : 2 * DK].reshape(shard_rows, -1)
    grad_v = grad_kv[:, :, 2 * DK :].reshape(shard_rows, -1)
    attn_gain_part = row_sum(grad_q, q_weight) + row_sum(grad_k, k_weight) + row_sum(grad_v, v_weight)
    ffn_gain_part = row_sum(grad_gate, gate_weight) + row_sum(grad_up, up_weight)
    attn_gain_sum = attn_gain_part + at.swap_tensor(attn_gain_part)
    ffn_gain_sum = ffn_gain_part + at.swap_tensor(ffn_gain_part)
    return (
        output,
        tokens_grad,
        grad_q,
        grad_k,
        grad_v,
        after(grad_out, attn_gain_sum).astype(f32),
        attn_gain_sum / attn_gain.astype(f32),
        grad_head_gain,
        one_scale * lam_k1.astype(f32),
        one_scale * lam_q1.astype(f32),
        two_scale * lam_k2.astype(f32),
        two_scale * lam_q2.astype(f32),
        grad_gate.astype(f32),
        grad_up.astype(f32),
        grad_down.astype(f32),
        ffn_gain_sum / ffn_gain.astype(f32),
    )


def solution(mesh):
    rows = P(("dp", "tensor"), None)
    both = P("dp", "tensor")
    placed = (
        (rows, rows, P("dp", None))
        + (both,) * 4
        + (P("dp"),)
        + (both,) * 5
        + (both,) * 3
        + (P("dp"),)
    )
    return jax.shard_map(
        per_device,
        mesh=mesh,
        in_specs=placed,
        out_specs=(rows, rows)
        + (both,) * 4
        + (P("dp"),)
        + (both,) * 5
        + (both,) * 3
        + (P("dp"),),
        check_vma=False,
    )
```

```python
import jax
import jax.numpy as jnp
from jax import lax
from jax.experimental import pallas as pl
from jax.experimental.pallas import tpu as pltpu
from jax.sharding import PartitionSpec as P

D = 2048
DK = 128
DV = 256

norm_eps = 1e-06
head_eps = 1e-05
lambda_init = 0.2
masked_value = -1e30
f32 = jnp.float32
bf16 = jnp.bfloat16
CHUNK = 512


def inv_rms(entries, eps_value):
    return lax.rsqrt(jnp.mean(entries * entries, axis=-1, keepdims=True) + eps_value)


def norm_back(entries, inverse, gain_row, incoming):
    scaled = gain_row * incoming
    return inverse * scaled - entries * inverse**3 * jnp.mean(
        entries * scaled, axis=-1, keepdims=True
    )


def plain_product(first_arg, second_arg):
    return jnp.dot(first_arg, second_arg, preferred_element_type=f32)


def rows_product(first_arg, second_arg):
    return lax.dot_general(
        first_arg, second_arg, (((0,), (0,)), ((), ())), preferred_element_type=f32
    )


def cols_product(first_arg, second_arg):
    return lax.dot_general(
        first_arg, second_arg, (((1,), (1,)), ((), ())), preferred_element_type=f32
    )


def together(*values):
    return lax.optimization_barrier(values)


def after(value, *others):
    if not others:
        return value
    return lax.optimization_barrier((value,) + others)[0]


class Places:
    def __init__(self):
        self.count = lax.axis_size("dp")
        self.upper = self.count // 4
        index = lax.axis_index("dp")
        self.index = index
        self.core = index % 2
        self.side = (index // 2) % 2
        self.tensor = lax.axis_index("tensor")
        self.upper_groups = [
            [low + 4 * high for high in range(self.upper)] for low in range(4)
        ]
        self.core_pairs = [(k, k ^ 1) for k in range(self.count)]
        self.side_pairs = [(k, k ^ 2) for k in range(self.count)]

    def swap_core(self, value):
        return lax.ppermute(value, "dp", self.core_pairs)

    def swap_side(self, value):
        return lax.ppermute(value, "dp", self.side_pairs)

    def swap_tensor(self, value):
        return lax.ppermute(value, "tensor", [(0, 1), (1, 0)])

    def gather_upper(self, shard):
        return lax.all_gather(
            shard, "dp", axis=0, tiled=True, axis_index_groups=self.upper_groups
        )

    def sum_small(self, value):
        step = 1
        while step < self.count:
            value = value + lax.ppermute(
                value, "dp", [(k, k ^ step) for k in range(self.count)]
            )
            step *= 2
        return value

    def block_order(self, value):
        parts = value.reshape((2, 2, self.upper) + value.shape[1:])
        parts = self.flip(self.flip(parts, 0, self.core), 1, self.side)
        order = (2, 1, 0) + tuple(range(3, parts.ndim))
        return jnp.transpose(parts, order).reshape(value.shape)

    def scatter_upper(self, value):
        return lax.psum_scatter(
            value, "dp", scatter_dimension=0, tiled=True, axis_index_groups=self.upper_groups
        )

    def product_part(self, first_arg, second_arg, part):
        quarter = first_arg.shape[1] // 4
        return rows_product(first_arg[:, part * quarter : (part + 1) * quarter], second_arg)

    def far_part(self, first_arg, second_arg, part):
        send = self.product_part(first_arg, second_arg, part).astype(bf16)
        return self.swap_core(send), send

    def aside_part(self, first_arg, second_arg, far):
        return (self.product_part(first_arg, second_arg, 1) + far.astype(f32)).astype(bf16)

    def near_part(self, first_arg, second_arg, far, aside):
        near = self.product_part(first_arg, second_arg, 0) + far.astype(f32)
        return (near + aside.astype(f32)).astype(bf16)

    def flip(self, value, axis, bit):
        return jnp.where(bit == 1, jnp.flip(value, axis), value)

    def to_relative(self, value):
        lead = value.shape[:-1]
        parts = value.reshape(lead + (self.upper, 2, 2, value.shape[-1] // self.count))
        k = len(lead)
        order = tuple(range(k)) + (k + 2, k + 1, k, k + 3)
        parts = jnp.transpose(parts, order)
        parts = self.flip(self.flip(parts, k, self.core), k + 1, self.side)
        return parts.reshape(value.shape)

    def from_relative(self, value):
        lead = value.shape[:-1]
        parts = value.reshape(lead + (2, 2, self.upper, value.shape[-1] // self.count))
        k = len(lead)
        parts = self.flip(self.flip(parts, k, self.core), k + 1, self.side)
        order = tuple(range(k)) + (k + 2, k + 1, k, k + 3)
        return jnp.transpose(parts, order).reshape(value.shape)

    def relative_blocks(self):
        spot = jnp.arange(self.count, dtype=jnp.int32)
        core = spot // (2 * self.upper)
        side = (spot // self.upper) % 2
        high = spot % self.upper
        return high * 4 + (side ^ self.side) * 2 + (core ^ self.core)

    def own_half(self, rows):
        half = rows.shape[0] // 2
        return lax.dynamic_slice_in_dim(rows, self.tensor * half, half, 0)

    def other_half(self, rows):
        half = rows.shape[0] // 2
        return lax.dynamic_slice_in_dim(rows, (1 - self.tensor) * half, half, 0)

    def in_order(self, own, other):
        return jnp.where(
            self.tensor == 0,
            jnp.concatenate([own, other], axis=0),
            jnp.concatenate([other, own], axis=0),
        )


def dot_nt(first, second):
    return lax.dot_general(first, second, (((1,), (1,)), ((), ())), preferred_element_type=f32)


def dot_nn(first, second):
    return lax.dot_general(first, second, (((1,), (0,)), ((), ())), preferred_element_type=f32)


def dot_tn(first, second):
    return lax.dot_general(first, second, (((0,), (0,)), ((), ())), preferred_element_type=f32)


def forward_kernel(
    prompt_len, top_rows, first_head, lam_ref, q_ref, kv_ref, gain_ref, spot_ref, reach_ref,
    out_ref, vec_ref, lse_ref, one_ref, two_ref, turn_ref,
):
    lam = lam_ref[first_head + pl.program_id(0)]
    rows, keys = q_ref.shape[0], kv_ref.shape[0]
    scale = DK ** (-0.5)
    count = keys // CHUNK
    first_cont = prompt_len // CHUNK
    flipped = rows % 128 == 0

    def span_of(chunk):
        return pl.ds(pl.multiple_of(chunk * CHUNK, CHUNK), CHUNK)

    def eights(values):
        return values.reshape(CHUNK // 8, 8, rows)

    def score(chunk, allowed, columns, tops):
        news = []
        for comp, ref in ((0, one_ref), (1, two_ref)):
            lanes = slice(comp * DK, (comp + 1) * DK)
            scores = dot_nt(kv_ref[span_of(chunk), lanes], q_ref[:, lanes])
            masked = jnp.where(allowed, scores[:, :columns], masked_value)
            if columns < rows:
                masked = jnp.concatenate([masked, scores[:, columns:]], axis=1)
            ref[chunk] = masked
            news.append(jnp.maximum(tops[comp], jnp.max(eights(masked), axis=0)))
        return tuple(news)

    def prompt_chunk(chunk, tops):
        allowed = spot_ref[span_of(chunk), :top_rows] <= reach_ref[0:1, :top_rows]
        return score(chunk, allowed, top_rows, tops)

    def cont_chunk(chunk, tops):
        spot = lax.broadcasted_iota(jnp.int32, (CHUNK, rows), 0) + (chunk * CHUNK - prompt_len)
        allowed = (spot >= reach_ref[1:2, :]) & (spot <= reach_ref[2:3, :])
        return score(chunk, allowed, rows, tops)

    tops = (jnp.full((8, rows), masked_value, f32),) * 2
    tops = lax.fori_loop(0, first_cont, prompt_chunk, tops, unroll=2)
    tops = lax.fori_loop(first_cont, count, cont_chunk, tops, unroll=2)
    tops = [jnp.max(top, axis=0, keepdims=True) * scale for top in tops]

    def weigh(chunk, totals):
        news = []
        for comp, ref in ((0, one_ref), (1, two_ref)):
            terms = jnp.exp(ref[chunk] * scale - tops[comp])
            ref[chunk] = terms
            news.append(totals[comp] + jnp.sum(eights(terms), axis=0))
        return tuple(news)

    totals = lax.fori_loop(0, count, weigh, (jnp.zeros((8, rows), f32),) * 2)
    totals = [jnp.sum(total, axis=0, keepdims=True) for total in totals]
    for comp in range(2):
        lse_ref[0, 8 * comp : 8 * comp + 1, :] = tops[comp] + jnp.log(totals[comp])
    first, second = 1.0 / totals[0], lam / totals[1]
    gather = turn_ref if flipped else out_ref
    gather[...] = jnp.zeros_like(gather)

    def mix(chunk, carry):
        mixed = (one_ref[chunk] * first - two_ref[chunk] * second).astype(bf16)
        value = kv_ref[span_of(chunk), 2 * DK :]
        gather[...] += dot_tn(value, mixed) if flipped else dot_tn(mixed, value)
        return carry

    lax.fori_loop(0, count, mix, 0, unroll=2)
    if flipped:
        out_ref[...] = jnp.transpose(turn_ref[...])
    out = out_ref[...]
    inverse = lax.rsqrt(jnp.mean(out * out, axis=1, keepdims=True) + head_eps)
    vec_ref[...] = (out * inverse * gain_ref[...] * (1.0 - lambda_init)).astype(bf16)


def backward_kernel(
    prompt_len, top_rows, first_head, lam_ref, q_ref, kv_ref, gain_ref, vec_ref, out_ref, lse_ref, spot_ref, reach_ref,
    dq_ref, dkv_ref, sums_ref, one_ref, two_ref, mix_ref, grad_ref, turn_ref,
):
    lam = lam_ref[first_head + pl.program_id(0)]
    rows, keys = q_ref.shape[0], kv_ref.shape[0]
    scale = DK ** (-0.5)
    out = out_ref[...]
    vec = vec_ref[...]
    inverse = lax.rsqrt(jnp.mean(out * out, axis=1, keepdims=True) + head_eps)
    plain = vec * out * inverse * (1.0 - lambda_init)
    scaled = vec * gain_ref[...] * (1.0 - lambda_init)
    grad_ref[...] = (
        inverse * scaled - out * inverse**3 * jnp.mean(out * scaled, axis=1, keepdims=True)
    ).astype(bf16)
    gain_part = jnp.sum(plain, axis=0, keepdims=True)
    grad = grad_ref[...]
    count = keys // CHUNK
    first_cont = prompt_len // CHUNK

    def weigh(chunk):
        span = pl.ds(pl.multiple_of(chunk * CHUNK, CHUNK), CHUNK)
        for comp, ref in ((0, one_ref), (1, two_ref)):
            lanes = slice(comp * DK, (comp + 1) * DK)
            scores = dot_nt(kv_ref[span, lanes], q_ref[:, lanes])
            ref[chunk] = jnp.exp(scores * scale - lse_ref[0, 8 * comp : 8 * comp + 1, :])
        mix_ref[chunk] = dot_nt(kv_ref[span, 2 * DK :], grad)

    def gather_sums(chunk, sums):
        span = pl.ds(pl.multiple_of(chunk * CHUNK, CHUNK), CHUNK)
        one, two, mix = one_ref[chunk], two_ref[chunk], mix_ref[chunk]
        mixed = (one - lam * two).astype(bf16)
        dkv_ref[span, 2 * DK :] = dot_nn(mixed, grad).astype(bf16)
        return (
            sums[0] + jnp.sum((one * mix).reshape(CHUNK // 8, 8, rows), axis=0),
            sums[1] + jnp.sum((two * mix).reshape(CHUNK // 8, 8, rows), axis=0),
        )

    def prompt_chunk(chunk, sums):
        weigh(chunk)
        allowed = spot_ref[pl.ds(chunk * CHUNK, CHUNK), :top_rows] <= reach_ref[0:1, :top_rows]
        for ref in (one_ref, two_ref):
            ref[chunk, :, :top_rows] = jnp.where(allowed, ref[chunk, :, :top_rows], 0.0)
        return gather_sums(chunk, sums)

    def cont_chunk(chunk, sums):
        weigh(chunk)
        spot = lax.broadcasted_iota(jnp.int32, (CHUNK, rows), 0) + (chunk * CHUNK - prompt_len)
        allowed = (spot >= reach_ref[1:2, :]) & (spot <= reach_ref[2:3, :])
        for ref in (one_ref, two_ref):
            ref[chunk] = jnp.where(allowed, ref[chunk], 0.0)
        return gather_sums(chunk, sums)

    sums = (jnp.zeros((8, rows), f32), jnp.zeros((8, rows), f32))
    sums = lax.fori_loop(0, first_cont, prompt_chunk, sums, unroll=2)
    sums = lax.fori_loop(first_cont, count, cont_chunk, sums, unroll=2)
    first = jnp.sum(sums[0], axis=0, keepdims=True)
    second = jnp.sum(sums[1], axis=0, keepdims=True)
    sums_ref[0, 0:1, :] = gain_part
    sums_ref[0, 1:2, :] = jnp.broadcast_to(-jnp.sum(second, axis=1, keepdims=True), (1, DV))
    turn_ref[...] = jnp.zeros_like(turn_ref)

    def back(chunk, carry):
        span = pl.ds(pl.multiple_of(chunk * CHUNK, CHUNK), CHUNK)
        mix = mix_ref[chunk]
        grads = (
            (one_ref[chunk] * (mix - first)).astype(bf16),
            (two_ref[chunk] * ((mix - second) * (-lam))).astype(bf16),
        )
        for comp in range(2):
            lanes = slice(comp * DK, (comp + 1) * DK)
            dkv_ref[span, lanes] = (dot_nn(grads[comp], q_ref[:, lanes]) * scale).astype(bf16)
            turn_ref[lanes, :] += dot_tn(kv_ref[span, lanes], grads[comp])
        return carry

    lax.fori_loop(0, count, back, 0, unroll=2)
    dq_ref[...] = (turn_ref[...] * scale).astype(bf16)


def attend(queries, keys_values, lam_vec, gain_rows, prompt_spots, bounds, prompt_part, span):
    first, heads = span[0], span[1] - span[0]
    rows, keys = queries.shape[0], keys_values.shape[0]
    prompt_len = prompt_spots.shape[0]
    top_rows = min(rows, -(-prompt_part // 128) * 128)
    count = keys // CHUNK
    return pl.pallas_call(
        lambda *refs: forward_kernel(prompt_len, top_rows, first, *refs),
        grid=(heads,),
        in_specs=[
            pl.BlockSpec(memory_space=pltpu.SMEM),
            pl.BlockSpec((rows, 2 * DK), lambda h: (0, h + first)),
            pl.BlockSpec((keys, 2 * DK + DV), lambda h: (0, h + first)),
            pl.BlockSpec((1, DV), lambda h: (0, h + first)),
            pl.BlockSpec((prompt_len, 128), lambda h: (0, 0)),
            pl.BlockSpec((8, rows), lambda h: (0, 0)),
        ],
        out_specs=[
            pl.BlockSpec((rows, DV), lambda h: (0, h)),
            pl.BlockSpec((rows, DV), lambda h: (0, h)),
            pl.BlockSpec((1, 16, rows), lambda h: (h, 0, 0)),
        ],
        out_shape=[
            jax.ShapeDtypeStruct((rows, heads * DV), f32),
            jax.ShapeDtypeStruct((rows, heads * DV), bf16),
            jax.ShapeDtypeStruct((heads, 16, rows), f32),
        ],
        scratch_shapes=[
            pltpu.VMEM((count, CHUNK, rows), f32),
            pltpu.VMEM((count, CHUNK, rows), f32),
            pltpu.VMEM((DV, rows), f32),
        ],
        compiler_params=pltpu.CompilerParams(vmem_limit_bytes=56 * 2**20),
        name="attend",
        cost_estimate=pl.CostEstimate(flops=14_000_000_000, transcendentals=0, bytes_accessed=0),
    )(
        lam_vec,
        queries,
        keys_values,
        gain_rows,
        jnp.broadcast_to(prompt_spots[:, None], (prompt_len, 128)),
        jnp.concatenate([jnp.stack(bounds), jnp.zeros((5, rows), jnp.int32)]),
    )


def attend_back(
    queries, keys_values, lam_vec, gain_rows, vec_grad, out, lse, prompt_spots, bounds, prompt_part, span, done
):
    first, heads, all_heads = span[0], span[1] - span[0], lam_vec.shape[0]
    rows, keys = queries.shape[0], keys_values.shape[0]
    prompt_len = prompt_spots.shape[0]
    top_rows = min(rows, -(-prompt_part // 128) * 128)
    count = keys // CHUNK
    reach = jnp.concatenate([jnp.stack(bounds), jnp.zeros((5, rows), jnp.int32)])
    return pl.pallas_call(
        lambda *refs: backward_kernel(prompt_len, top_rows, first, *refs[:9], *refs[9 + len(done) :]),
        grid=(heads,),
        in_specs=[
            pl.BlockSpec(memory_space=pltpu.SMEM),
            pl.BlockSpec((rows, 2 * DK), lambda h: (0, h + first)),
            pl.BlockSpec((keys, 2 * DK + DV), lambda h: (0, h + first)),
            pl.BlockSpec((1, DV), lambda h: (0, h + first)),
            pl.BlockSpec((rows, DV), lambda h: (0, h + first)),
            pl.BlockSpec((rows, DV), lambda h: (0, h + first)),
            pl.BlockSpec((1, 16, rows), lambda h: (h + first, 0, 0)),
            pl.BlockSpec((prompt_len, 128), lambda h: (0, 0)),
            pl.BlockSpec((8, rows), lambda h: (0, 0)),
        ]
        + [pl.BlockSpec(memory_space=pl.ANY)] * len(done),
        out_specs=[
            pl.BlockSpec((2 * DK, rows), lambda h: (h + first, 0)),
            pl.BlockSpec((keys, 2 * DK + DV), lambda h: (0, h + first)),
            pl.BlockSpec((1, 8, DV), lambda h: (h + first, 0, 0)),
        ],
        out_shape=[
            jax.ShapeDtypeStruct((all_heads * 2 * DK, rows), bf16),
            jax.ShapeDtypeStruct((keys, all_heads * (2 * DK + DV)), bf16),
            jax.ShapeDtypeStruct((all_heads, 8, DV), f32),
        ],
        input_output_aliases={9 + k: k for k in range(len(done))},
        scratch_shapes=[
            pltpu.VMEM((count, CHUNK, rows), f32),
            pltpu.VMEM((count, CHUNK, rows), f32),
            pltpu.VMEM((count, CHUNK, rows), f32),
            pltpu.VMEM((rows, DV), bf16),
            pltpu.VMEM((2 * DK, rows), f32),
        ],
        compiler_params=pltpu.CompilerParams(vmem_limit_bytes=58 * 2**20),
        name="attend_back",
        cost_estimate=pl.CostEstimate(
            flops=0, transcendentals=0, bytes_accessed=0
        ),
    )(
        lam_vec,
        queries,
        keys_values,
        gain_rows,
        vec_grad,
        out,
        lse,
        jnp.broadcast_to(prompt_spots[:, None], (prompt_len, 128)),
        reach,
        *done,
    )


def norm_kernel(count, unit, blocks_ref, swap_ref, *refs):
    *sources, gain_ref, out_ref = refs
    step = pl.program_id(0)
    all_rows, depth = out_ref.shape
    block = depth // count
    upper = count // 4
    rows = all_rows // upper

    def norm_from(pieces, stride):
        for part in range(upper):
            span = slice(part * stride, part * stride + rows)
            total = jnp.zeros((rows, 128), f32)
            for piece in pieces:
                for lane in range(0, piece.shape[1], 128):
                    x = piece[span, lane : lane + 128].astype(f32)
                    total = total + x * x
            total = jnp.sum(total, axis=1, keepdims=True)
            inverse = jnp.broadcast_to(lax.rsqrt(total * (1.0 / depth) + norm_eps), (rows, block))
            size = depth // len(pieces)
            for spot in range(count):
                lanes = slice(spot * block, (spot + 1) * block)
                side = (spot % upper) * 4 * block // size
                start = pl.multiple_of(blocks_ref[spot] * block - side * size, block)
                x = pieces[side][span, pl.ds(start, block)].astype(f32)
                out_ref[part * rows : (part + 1) * rows, lanes] = (
                    x * inverse * gain_ref[:, lanes]
                ).astype(bf16)

    for core in range(2):
        for turn in range(2):

            @pl.when((step >= core * 2) & (step < core * 2 + 2) & (swap_ref[0] == turn))
            def _():
                pair = sources[2 * core : 2 * core + 2]
                norm_from(pair[::-1] if turn else pair, unit)

    @pl.when(step >= 4)
    def _():
        norm_from(sources[4:5], rows)


def norm_keys(at, prompt_groups, cont_tokens, gain_row, prompt_part):
    cont_len, depth = cont_tokens.shape
    count, upper = at.count, at.upper
    unit = prompt_groups[0].shape[0] // (2 * upper)
    group_rows = upper * prompt_part
    if (depth // count) % 128 or cont_len % group_rows or upper % 2:
        cores = []
        for pair in (prompt_groups[:2], prompt_groups[2:]):
            parts = jnp.stack([part.reshape(2 * upper, unit, -1)[:, :prompt_part] for part in pair])
            parts = at.flip(parts.reshape(2, 2 * upper * prompt_part, depth // 2), 0, at.tensor)
            cores.append(jnp.concatenate([parts[0], parts[1]], axis=1))
        rows = at.to_relative(jnp.concatenate(cores + [cont_tokens], axis=0))
        rows = rows.astype(f32)
        return (rows * inv_rms(rows, norm_eps) * gain_row).astype(bf16)

    def spot_of(core):
        return lambda i, blocks, swap: (jnp.clip(i - 2 * core, 0, 1), 0)

    return pl.pallas_call(
        lambda *refs: norm_kernel(count, unit, *refs),
        grid_spec=pltpu.PrefetchScalarGridSpec(
            num_scalar_prefetch=2,
            grid=(4 + cont_len // group_rows,),
            in_specs=[
                pl.BlockSpec((upper * unit, depth // 2), spot_of(core)) for core in (0, 0, 1, 1)
            ]
            + [
                pl.BlockSpec(
                    (group_rows, depth), lambda i, blocks, swap: (jnp.maximum(i - 4, 0), 0)
                ),
                pl.BlockSpec((1, depth), lambda i, blocks, swap: (0, 0)),
            ],
            out_specs=pl.BlockSpec((group_rows, depth), lambda i, blocks, swap: (i, 0)),
        ),
        out_shape=jax.ShapeDtypeStruct((prompt_part * count + cont_len, depth), bf16),
        compiler_params=pltpu.CompilerParams(vmem_limit_bytes=56 * 2**20),
        name="norm_keys",
        cost_estimate=pl.CostEstimate(flops=8_000_000_000, transcendentals=0, bytes_accessed=0),
    )(
        at.relative_blocks(),
        at.tensor.reshape(1).astype(jnp.int32),
        *prompt_groups,
        cont_tokens,
        gain_row.reshape(1, depth),
    )


def per_device(
    tokens,
    cotangent,
    cont_ids,
    q_weight,
    k_weight,
    v_weight,
    out_weight,
    attn_gain,
    head_gain,
    lam_q1,
    lam_k1,
    lam_q2,
    lam_k2,
    gate_weight,
    up_weight,
    down_weight,
    ffn_gain,
):
    at = Places()
    local_rows = tokens.shape[0]
    block_rows = 2 * local_rows
    row_ids = cont_ids[0]
    cont_len = row_ids.shape[0]
    prompt_part = block_rows - cont_len
    prompt_len = prompt_part * at.count
    heads = q_weight.shape[1] // (2 * DK)
    width = heads * 2 * DK
    shard_rows = q_weight.shape[0]

    small_parts = (attn_gain, ffn_gain, head_gain, lam_q1, lam_k1, lam_q2, lam_k2)
    small = jnp.concatenate([part.reshape(-1) for part in small_parts])
    half = D // 2
    small_rows = jnp.zeros((16, half), bf16).at[0, : small.size].set(small)
    prompt_sent = lax.ppermute(tokens[:prompt_part, half:], "tensor", [(0, 1)])
    prompt_own = jnp.where(at.tensor == 0, tokens[:prompt_part, :half], prompt_sent)
    prompt_own = jnp.concatenate([prompt_own, small_rows], axis=0)
    prompt_here = at.gather_upper(prompt_own)

    def by_head(weight):
        return weight.reshape(shard_rows, heads, -1)

    kv_here = at.gather_upper(
        after(
            jnp.concatenate([by_head(k_weight), by_head(v_weight)], axis=2).reshape(
                shard_rows, -1
            ),
            prompt_own,
        )
    )
    q_here = at.gather_upper(after(q_weight, prompt_own))
    out_here = at.gather_upper(after(out_weight, prompt_own))
    gate_here = at.gather_upper(after(gate_weight, prompt_own))
    up_here = at.gather_upper(after(up_weight, prompt_own))
    down_here = at.gather_upper(after(down_weight, prompt_own))

    tokens_rel = at.to_relative(tokens)
    cot_rel = at.to_relative(cotangent)
    tokens_turned = at.swap_tensor(after(tokens, prompt_own))
    prompt_here, tokens_rel, cot_rel, tokens_turned = together(
        prompt_here, tokens_rel, cot_rel, tokens_turned
    )
    prompt_pair = jnp.concatenate([prompt_here, at.swap_side(prompt_here)], axis=0)
    prompt_turned = at.swap_tensor(prompt_pair)
    prompt_far = at.swap_core(prompt_pair)
    kv_here = after(kv_here, prompt_pair)
    kv_side, kv_near = at.swap_side(kv_here), at.swap_core(kv_here)
    prompt_turned, kv_side_early = together(prompt_turned, kv_near)
    kv_near = kv_side_early
    prompt_far_turned = at.swap_core(prompt_turned)
    kv_side, q_here = together(kv_side, q_here)
    kv_far = at.swap_core(kv_side)
    q_side, q_near = at.swap_side(q_here), at.swap_core(q_here)
    prompt_far, prompt_far_turned = together(prompt_far, after(prompt_far_turned, kv_side))
    cont_tokens = at.in_order(tokens, tokens_turned)[prompt_part:]
    cot_turned = at.swap_tensor(after(cot_rel, prompt_far_turned))

    small_all = jnp.concatenate(
        [
            group.reshape(2 * at.upper, -1, half)[:, prompt_part, : small.size]
            for group in (prompt_pair, prompt_far)
        ],
        axis=0,
    ).astype(f32)
    small_full = []
    start = 0
    for part in small_parts:
        small_full.append(
            small_all[:, start : start + part.size].reshape((at.count,) + part.shape)
        )
        start += part.size
    attn_gain_row = small_full[0].reshape(-1)
    ffn_gain_row = small_full[1].reshape(-1)
    head_gain_row = at.block_order(small_full[2]).reshape(DV, heads).T.reshape(1, heads * DV)
    first_exp = jnp.exp(jnp.sum(small_full[3] * small_full[4], axis=(0, 1)))
    second_exp = jnp.exp(jnp.sum(small_full[5] * small_full[6], axis=(0, 1)))
    lam_vec = first_exp - second_exp + lambda_init

    prompt_spots = (
        at.relative_blocks()[:, None] * prompt_part
        + jnp.arange(prompt_part, dtype=jnp.int32)[None]
    ).reshape(-1)
    cont_spot = jnp.arange(cont_len, dtype=jnp.int32)
    earlier = jnp.sum((row_ids[None, :] < row_ids[:, None]).astype(jnp.int32), axis=1)
    far_spot = jnp.full((prompt_part,), prompt_len + cont_len, jnp.int32)
    reach = jnp.concatenate(
        [
            at.index * prompt_part + jnp.arange(prompt_part, dtype=jnp.int32),
            jnp.full((cont_len,), prompt_len, jnp.int32),
        ]
    )
    bounds = (
        reach,
        jnp.concatenate([far_spot, earlier]),
        jnp.concatenate([jnp.full((prompt_part,), -1, jnp.int32), cont_spot]),
    )

    tokens_f32 = tokens_rel.astype(f32)
    prompt_groups = (prompt_pair, prompt_turned, prompt_far, prompt_far_turned)
    normed_keys = norm_keys(at, prompt_groups, cont_tokens, attn_gain_row, prompt_part)
    kv_near, kv_far = after(kv_near, normed_keys), after(kv_far, normed_keys)
    kv_full = jnp.concatenate([kv_here, kv_side, kv_near, kv_far], axis=0)
    kv_full, q_side, out_here = together(kv_full, q_side, out_here)
    q_far = at.swap_core(q_side)
    out_side, out_near = at.swap_side(out_here), at.swap_core(out_here)
    own_block = lax.dynamic_slice_in_dim(
        normed_keys, (at.index // 4) * prompt_part, prompt_part, 0
    )
    normed = jnp.concatenate([own_block, normed_keys[prompt_len:]], axis=0)
    keys_values = plain_product(normed_keys, kv_full).astype(bf16)
    q_near, q_far = after(q_near, keys_values), after(q_far, keys_values)
    q_full = jnp.concatenate([q_here, q_side, q_near, q_far], axis=0)
    queries = plain_product(after(normed, keys_values), q_full).astype(bf16)
    fixed = (lam_vec, head_gain_row, prompt_spots, bounds, prompt_part)
    queries, out_side, gate_here = together(queries, out_side, gate_here)
    out_far = at.swap_core(out_side)
    gate_side, gate_near = at.swap_side(gate_here), at.swap_core(gate_here)
    heads_out, attn_vec, lse = attend(queries, keys_values, *fixed, (0, heads))
    attn_vec, cot_turned = together(attn_vec, cot_turned)
    out_near, out_far = after(out_near, attn_vec), after(out_far, attn_vec)
    out_full = jnp.concatenate([out_here, out_side, out_near, out_far], axis=0)
    attn_own, attn_other = at.own_half(attn_vec), at.other_half(attn_vec)
    out_send = cols_product(attn_other, out_full).astype(bf16)
    out_sent = at.swap_tensor(out_send)
    out_part = cols_product(after(attn_own, out_send), out_full)
    attn_two = jnp.concatenate([attn_own, attn_other], axis=0)
    out_part, attn_two, gate_side, up_here = together(out_part, attn_two, gate_side, up_here)
    up_side, up_near = at.swap_side(up_here), at.swap_core(up_here)
    gate_far = at.swap_core(gate_side)
    out_sent = after(out_sent, gate_side)
    residual = tokens_f32 + (out_part + out_sent.astype(f32))

    inv_second = inv_rms(residual, norm_eps)
    ffn_own = (residual * inv_second * ffn_gain_row).astype(bf16)
    ffn_turned = at.swap_tensor(ffn_own)
    gate_near, gate_far = after(gate_near, ffn_own), after(gate_far, ffn_own)
    gate_full = jnp.concatenate([gate_here, gate_side, gate_near, gate_far], axis=0)
    gate_full, down_here, up_side = together(gate_full, down_here, up_side)
    up_far = at.swap_core(up_side)
    down_side, down_near = at.swap_side(down_here), at.swap_core(down_here)
    ffn_turned = after(ffn_turned, gate_full)
    ffn_in = jnp.concatenate([ffn_own, ffn_turned], axis=0)
    gate_proj = plain_product(ffn_in, gate_full)
    cot_rows = jnp.concatenate([cot_rel, cot_turned], axis=0)
    up_near, up_far = after(up_near, gate_proj), after(up_far, gate_proj)
    up_full = jnp.concatenate([up_here, up_side, up_near, up_far], axis=0)
    up_proj = plain_product(after(ffn_in, gate_proj), up_full)
    gate_sigmoid = jax.nn.sigmoid(gate_proj)
    hidden = (gate_proj * gate_sigmoid * up_proj).astype(bf16)

    down_far_aside, down_send = at.far_part(cot_rows, hidden, 3)
    down_far_keep, down_send = at.far_part(cot_rows, after(hidden, down_send), 2)
    down_send, down_side = together(down_send, down_side)
    down_near = after(down_near, down_side)
    down_far = at.swap_core(down_side)
    down_far_aside = after(down_far_aside, down_side)
    down_grad_side = at.aside_part(cot_rows, hidden, down_far_aside)
    down_grad_aside = at.swap_side(down_grad_side)
    down_near, down_far = after(down_near, down_grad_side), after(down_far, down_grad_side)
    down_full = jnp.concatenate([down_here, down_side, down_near, down_far], axis=0)
    hidden_grad = plain_product(cot_rows, down_full)
    gate_grad = (
        hidden_grad * up_proj * gate_sigmoid * (1.0 + gate_proj * (1.0 - gate_sigmoid))
    ).astype(bf16)
    up_grad = (hidden_grad * gate_proj * gate_sigmoid).astype(bf16)

    def back_ffn(one, two, features=slice(None)):
        return cols_product(one, gate_full[features]) + cols_product(two, up_full[features])

    gate_far_aside, gate_send = at.far_part(ffn_in, gate_grad, 3)
    gate_other, up_other = after(gate_grad[local_rows:], gate_send), up_grad[local_rows:]
    ffn_sends = [back_ffn(gate_other, up_other, slice(0, half)).astype(bf16)]
    gate_other, up_other = after(gate_other, ffn_sends[0]), after(up_other, ffn_sends[0])
    ffn_sends.append(back_ffn(gate_other, up_other, slice(half, D)).astype(bf16))
    ffn_sent = [at.swap_tensor(send) for send in ffn_sends]
    ffn_part = cols_product(after(gate_grad[:local_rows], ffn_sends[1]), gate_full)
    ffn_part, down_grad_aside = together(ffn_part, down_grad_aside)
    ffn_part = ffn_part + cols_product(after(up_grad[:local_rows], down_grad_aside), up_full)
    gate_far_keep, gate_send = at.far_part(ffn_in, after(gate_grad, ffn_part), 2)
    gate_far_aside = after(gate_far_aside, gate_send)
    gate_grad_side = at.aside_part(ffn_in, gate_grad, gate_far_aside)
    gate_grad_aside = at.swap_side(gate_grad_side)
    ffn_sent = together(after(ffn_sent[0], gate_grad_side), ffn_sent[1])
    ffn_in_grad = ffn_part + jnp.concatenate(ffn_sent, axis=1).astype(f32)
    residual_grad = cot_rel.astype(f32) + norm_back(
        residual, inv_second, ffn_gain_row, ffn_in_grad
    )

    branch_own = residual_grad.astype(bf16)
    branch_sent = at.swap_tensor(branch_own)
    down_far_keep = after(down_far_keep, branch_own)
    down_last = at.near_part(cot_rows, hidden, down_far_keep, down_grad_aside)
    grad_down = at.scatter_upper(down_last)
    up_far_aside, up_send = at.far_part(ffn_in, after(up_grad, down_last), 3)
    up_far_keep, up_send = at.far_part(ffn_in, after(up_grad, up_send), 2)
    branch = jnp.concatenate([branch_own, after(branch_sent, up_send)], axis=0)
    vec_two = plain_product(branch, out_full)
    vec_grad = at.in_order(vec_two[:local_rows], vec_two[local_rows:])
    middle = heads // 2
    back_args = (queries, keys_values, lam_vec, head_gain_row)
    back_fixed = (heads_out, lse, prompt_spots, bounds, prompt_part)
    half_back = attend_back(*back_args, vec_grad, *back_fixed, (0, middle), ())
    half_back, gate_grad_aside = together(half_back, gate_grad_aside)
    gate_far_keep = after(gate_far_keep, gate_grad_aside)
    gate_last = at.near_part(ffn_in, gate_grad, gate_far_keep, gate_grad_aside)
    grad_gate = at.scatter_upper(gate_last)
    up_far_aside = after(up_far_aside, gate_last)
    up_grad_side = at.aside_part(ffn_in, up_grad, up_far_aside)
    up_grad_aside = at.swap_side(up_grad_side)
    queries_grad, kv_grad, head_sums = attend_back(
        *back_args, after(vec_grad, up_grad_side), *back_fixed, (middle, heads), half_back
    )
    queries_grad, kv_grad, head_sums, grad_down = together(
        queries_grad, kv_grad, head_sums, grad_down
    )
    queries_grad = queries_grad.T

    quarter = prompt_len // 4

    def prompt_rows(part):
        return kv_grad[part * quarter : (part + 1) * quarter]

    prompt_send = prompt_rows(3)
    prompt_far_aside = at.swap_core(prompt_send)
    prompt_keep = after(prompt_rows(2), prompt_send)
    prompt_far_keep = at.swap_core(prompt_keep)
    kv_far_aside, kv_send = at.far_part(normed_keys, after(kv_grad, prompt_keep), 3)
    kv_send, up_far_keep, up_grad_aside = together(kv_send, up_far_keep, up_grad_aside)
    prompt_far_aside = after(prompt_far_aside, up_grad_aside)
    prompt_side = (prompt_rows(1).astype(f32) + prompt_far_aside.astype(f32)).astype(bf16)
    prompt_aside = at.swap_side(prompt_side)
    up_last = at.near_part(ffn_in, after(up_grad, prompt_side), up_far_keep, up_grad_aside)
    up_last, grad_gate = together(up_last, grad_gate)
    grad_up = at.scatter_upper(up_last)
    kv_far_keep, kv_send = at.far_part(normed_keys, after(kv_grad, up_last), 2)
    kv_far_aside = after(kv_far_aside, kv_send)
    kv_grad_side = at.aside_part(normed_keys, kv_grad, kv_far_aside)
    kv_grad_aside = at.swap_side(kv_grad_side)
    q_far_aside, q_send = at.far_part(normed, after(queries_grad, kv_grad_side), 3)
    q_far_keep, q_send = at.far_part(normed, after(queries_grad, q_send), 2)
    out_far_aside, out_send_grad = at.far_part(branch, after(attn_two, q_send), 3)
    out_far_keep, out_send_grad = at.far_part(branch, after(attn_two, out_send_grad), 2)
    hidden_late = after(hidden, out_send_grad)
    output_part = cols_product(hidden_late[:local_rows], down_full)
    prompt_far_keep, prompt_aside = together(after(prompt_far_keep, output_part), prompt_aside)
    prompt_last = (
        prompt_rows(0).astype(f32) + prompt_far_keep.astype(f32) + prompt_aside.astype(f32)
    ).astype(bf16)
    prompt_grad = at.scatter_upper(prompt_last)
    q_far_aside = after(q_far_aside, prompt_last)
    q_grad_side = at.aside_part(normed, queries_grad, q_far_aside)
    q_grad_aside = at.swap_side(q_grad_side)
    out_far_aside = after(out_far_aside, q_grad_side)
    out_grad_side = at.aside_part(branch, attn_two, out_far_aside)
    out_grad_aside = at.swap_side(out_grad_side)
    output_send = cols_product(after(hidden_late, out_grad_side)[local_rows:], down_full).astype(bf16)
    output_sent = at.swap_tensor(output_send)
    kv_far_keep, kv_grad_aside = together(after(kv_far_keep, output_send), kv_grad_aside)
    kv_last = at.near_part(normed_keys, kv_grad, kv_far_keep, kv_grad_aside)
    grad_kv = at.scatter_upper(kv_last)
    output_sent, grad_up, q_far_keep = together(after(output_sent, kv_last), grad_up, q_far_keep)
    q_far_keep, q_grad_aside = together(q_far_keep, q_grad_aside)
    q_last = at.near_part(normed, queries_grad, q_far_keep, q_grad_aside)
    grad_q = at.scatter_upper(q_last)
    prompt_grad = after(prompt_grad, q_last)
    here_grad = jnp.concatenate([prompt_grad, kv_grad[prompt_len:]], axis=0)

    def back_attn(half_of):
        return cols_product(half_of(queries_grad), q_full) + cols_product(
            half_of(here_grad), kv_full
        )

    normed_send = back_attn(at.other_half).astype(bf16)
    normed_sent = at.swap_tensor(normed_send)
    out_far_keep, out_grad_aside = together(after(out_far_keep, normed_send), out_grad_aside)
    out_last = at.near_part(branch, attn_two, out_far_keep, out_grad_aside)
    grad_out = at.scatter_upper(out_last)
    normed_part = back_attn(lambda rows: at.own_half(after(rows, out_last)))
    normed_grad = normed_part + normed_sent.astype(f32)
    inv_first = inv_rms(tokens_f32, norm_eps)
    tokens_grad = residual_grad + norm_back(tokens_f32, inv_first, attn_gain_row, normed_grad)
    tokens_grad = at.from_relative(tokens_grad.astype(bf16))
    output = at.from_relative((residual + (output_part + output_sent.astype(f32))).astype(bf16))

    def row_sum(grad, weight):
        return jnp.sum(grad.astype(f32) * weight.astype(f32), axis=1)

    head_sums = at.sum_small(jnp.concatenate([head_sums[:, 0], head_sums[:, 1]], axis=1))
    head_gain_sum, lam_sum = head_sums[:, :DV], head_sums[:, DV]
    head_rows = head_gain.shape[0]
    grad_head_gain = lax.dynamic_slice_in_dim(head_gain_sum.T, at.index * head_rows, head_rows, 0)
    one_scale, two_scale = lam_sum * first_exp, -lam_sum * second_exp
    grad_q = grad_q.astype(f32)
    grad_kv = grad_kv.astype(f32).reshape(shard_rows, heads, -1)
    grad_k = grad_kv[:, :, : 2 * DK].reshape(shard_rows, -1)
    grad_v = grad_kv[:, :, 2 * DK :].reshape(shard_rows, -1)
    attn_gain_part = row_sum(grad_q, q_weight) + row_sum(grad_k, k_weight) + row_sum(grad_v, v_weight)
    ffn_gain_part = row_sum(grad_gate, gate_weight) + row_sum(grad_up, up_weight)
    attn_gain_sum = attn_gain_part + at.swap_tensor(attn_gain_part)
    ffn_gain_sum = ffn_gain_part + at.swap_tensor(ffn_gain_part)
    return (
        output,
        tokens_grad,
        grad_q,
        grad_k,
        grad_v,
        after(grad_out, attn_gain_sum).astype(f32),
        attn_gain_sum / attn_gain.astype(f32),
        grad_head_gain,
        one_scale * lam_k1.astype(f32),
        one_scale * lam_q1.astype(f32),
        two_scale * lam_k2.astype(f32),
        two_scale * lam_q2.astype(f32),
        grad_gate.astype(f32),
        grad_up.astype(f32),
        grad_down.astype(f32),
        ffn_gain_sum / ffn_gain.astype(f32),
    )


def solution(mesh):
    rows = P(("dp", "tensor"), None)
    both = P("dp", "tensor")
    placed = (
        (rows, rows, P("dp", None))
        + (both,) * 4
        + (P("dp"),)
        + (both,) * 5
        + (both,) * 3
        + (P("dp"),)
    )
    return jax.shard_map(
        per_device,
        mesh=mesh,
        in_specs=placed,
        out_specs=(rows, rows)
        + (both,) * 4
        + (P("dp"),)
        + (both,) * 5
        + (both,) * 3
        + (P("dp"),),
        check_vma=False,
    )
```

```python
import jax
import jax.numpy as jnp
from jax import lax
from jax.experimental import pallas as pl
from jax.experimental.pallas import tpu as pltpu
from jax.sharding import PartitionSpec as P

D = 2048
DK = 128
DV = 256

norm_eps = 1e-06
head_eps = 1e-05
lambda_init = 0.2
masked_value = -1e30
f32 = jnp.float32
bf16 = jnp.bfloat16
CHUNK = 512


def inv_rms(entries, eps_value):
    return lax.rsqrt(jnp.mean(entries * entries, axis=-1, keepdims=True) + eps_value)


def norm_back(entries, inverse, gain_row, incoming):
    scaled = gain_row * incoming
    return inverse * scaled - entries * inverse**3 * jnp.mean(
        entries * scaled, axis=-1, keepdims=True
    )


def plain_product(first_arg, second_arg):
    return jnp.dot(first_arg, second_arg, preferred_element_type=f32)


def rows_product(first_arg, second_arg):
    return lax.dot_general(
        first_arg, second_arg, (((0,), (0,)), ((), ())), preferred_element_type=f32
    )


def cols_product(first_arg, second_arg):
    return lax.dot_general(
        first_arg, second_arg, (((1,), (1,)), ((), ())), preferred_element_type=f32
    )


def together(*values):
    return lax.optimization_barrier(values)


def after(value, *others):
    if not others:
        return value
    return lax.optimization_barrier((value,) + others)[0]


class Places:
    def __init__(self):
        self.count = lax.axis_size("dp")
        self.upper = self.count // 4
        index = lax.axis_index("dp")
        self.index = index
        self.core = index % 2
        self.side = (index // 2) % 2
        self.tensor = lax.axis_index("tensor")
        self.upper_groups = [
            [low + 4 * high for high in range(self.upper)] for low in range(4)
        ]
        self.core_pairs = [(k, k ^ 1) for k in range(self.count)]
        self.side_pairs = [(k, k ^ 2) for k in range(self.count)]

    def swap_core(self, value):
        return lax.ppermute(value, "dp", self.core_pairs)

    def swap_side(self, value):
        return lax.ppermute(value, "dp", self.side_pairs)

    def swap_tensor(self, value):
        return lax.ppermute(value, "tensor", [(0, 1), (1, 0)])

    def gather_upper(self, shard):
        return lax.all_gather(
            shard, "dp", axis=0, tiled=True, axis_index_groups=self.upper_groups
        )

    def sum_small(self, value):
        step = 1
        while step < self.count:
            value = value + lax.ppermute(
                value, "dp", [(k, k ^ step) for k in range(self.count)]
            )
            step *= 2
        return value

    def block_order(self, value):
        parts = value.reshape((2, 2, self.upper) + value.shape[1:])
        parts = self.flip(self.flip(parts, 0, self.core), 1, self.side)
        order = (2, 1, 0) + tuple(range(3, parts.ndim))
        return jnp.transpose(parts, order).reshape(value.shape)

    def scatter_upper(self, value):
        return lax.psum_scatter(
            value, "dp", scatter_dimension=0, tiled=True, axis_index_groups=self.upper_groups
        )

    def product_part(self, first_arg, second_arg, part):
        quarter = first_arg.shape[1] // 4
        return rows_product(first_arg[:, part * quarter : (part + 1) * quarter], second_arg)

    def far_part(self, first_arg, second_arg, part):
        send = self.product_part(first_arg, second_arg, part).astype(bf16)
        return self.swap_core(send), send

    def far_part_two(self, first_arg, second_arg):
        send = self.product_part(first_arg, second_arg, 3).astype(bf16)
        middle = send.shape[0] // 2
        pieces = [self.swap_core(send[:middle]), self.swap_core(send[middle:])]
        return jnp.concatenate(pieces, axis=0), send

    def aside_part(self, first_arg, second_arg, far):
        return (self.product_part(first_arg, second_arg, 1) + far.astype(f32)).astype(bf16)

    def near_part(self, first_arg, second_arg, far, aside):
        near = self.product_part(first_arg, second_arg, 0) + far.astype(f32)
        return (near + aside.astype(f32)).astype(bf16)

    def flip(self, value, axis, bit):
        return jnp.where(bit == 1, jnp.flip(value, axis), value)

    def to_relative(self, value):
        lead = value.shape[:-1]
        parts = value.reshape(lead + (self.upper, 2, 2, value.shape[-1] // self.count))
        k = len(lead)
        order = tuple(range(k)) + (k + 2, k + 1, k, k + 3)
        parts = jnp.transpose(parts, order)
        parts = self.flip(self.flip(parts, k, self.core), k + 1, self.side)
        return parts.reshape(value.shape)

    def from_relative(self, value):
        lead = value.shape[:-1]
        parts = value.reshape(lead + (2, 2, self.upper, value.shape[-1] // self.count))
        k = len(lead)
        parts = self.flip(self.flip(parts, k, self.core), k + 1, self.side)
        order = tuple(range(k)) + (k + 2, k + 1, k, k + 3)
        return jnp.transpose(parts, order).reshape(value.shape)

    def relative_blocks(self):
        spot = jnp.arange(self.count, dtype=jnp.int32)
        core = spot // (2 * self.upper)
        side = (spot // self.upper) % 2
        high = spot % self.upper
        return high * 4 + (side ^ self.side) * 2 + (core ^ self.core)

    def own_half(self, rows):
        half = rows.shape[0] // 2
        return lax.dynamic_slice_in_dim(rows, self.tensor * half, half, 0)

    def other_half(self, rows):
        half = rows.shape[0] // 2
        return lax.dynamic_slice_in_dim(rows, (1 - self.tensor) * half, half, 0)

    def in_order(self, own, other):
        return jnp.where(
            self.tensor == 0,
            jnp.concatenate([own, other], axis=0),
            jnp.concatenate([other, own], axis=0),
        )


def dot_nt(first, second):
    return lax.dot_general(first, second, (((1,), (1,)), ((), ())), preferred_element_type=f32)


def dot_nn(first, second):
    return lax.dot_general(first, second, (((1,), (0,)), ((), ())), preferred_element_type=f32)


def dot_tn(first, second):
    return lax.dot_general(first, second, (((0,), (0,)), ((), ())), preferred_element_type=f32)


def forward_kernel(
    prompt_len, top_rows, first_head, lam_ref, q_ref, kv_ref, gain_ref, spot_ref, reach_ref,
    out_ref, vec_ref, lse_ref, one_ref, two_ref, turn_ref,
):
    lam = lam_ref[first_head + pl.program_id(0)]
    rows, keys = q_ref.shape[0], kv_ref.shape[0]
    scale = DK ** (-0.5)
    count = keys // CHUNK
    first_cont = prompt_len // CHUNK
    flipped = rows % 128 == 0

    def span_of(chunk):
        return pl.ds(pl.multiple_of(chunk * CHUNK, CHUNK), CHUNK)

    def eights(values):
        return values.reshape(CHUNK // 8, 8, rows)

    def score(chunk, allowed, columns, tops):
        news = []
        for comp, ref in ((0, one_ref), (1, two_ref)):
            lanes = slice(comp * DK, (comp + 1) * DK)
            scores = dot_nt(kv_ref[span_of(chunk), lanes], q_ref[:, lanes])
            masked = jnp.where(allowed, scores[:, :columns], masked_value)
            if columns < rows:
                masked = jnp.concatenate([masked, scores[:, columns:]], axis=1)
            ref[chunk] = masked
            news.append(jnp.maximum(tops[comp], jnp.max(eights(masked), axis=0)))
        return tuple(news)

    def prompt_chunk(chunk, tops):
        allowed = spot_ref[span_of(chunk), :top_rows] <= reach_ref[0:1, :top_rows]
        return score(chunk, allowed, top_rows, tops)

    def cont_chunk(chunk, tops):
        spot = lax.broadcasted_iota(jnp.int32, (CHUNK, rows), 0) + (chunk * CHUNK - prompt_len)
        allowed = (spot >= reach_ref[1:2, :]) & (spot <= reach_ref[2:3, :])
        return score(chunk, allowed, rows, tops)

    tops = (jnp.full((8, rows), masked_value, f32),) * 2
    tops = lax.fori_loop(0, first_cont, prompt_chunk, tops, unroll=2)
    tops = lax.fori_loop(first_cont, count, cont_chunk, tops, unroll=2)
    tops = [jnp.max(top, axis=0, keepdims=True) * scale for top in tops]

    def weigh(chunk, totals):
        news = []
        for comp, ref in ((0, one_ref), (1, two_ref)):
            terms = jnp.exp(ref[chunk] * scale - tops[comp])
            ref[chunk] = terms
            news.append(totals[comp] + jnp.sum(eights(terms), axis=0))
        return tuple(news)

    totals = lax.fori_loop(0, count, weigh, (jnp.zeros((8, rows), f32),) * 2)
    totals = [jnp.sum(total, axis=0, keepdims=True) for total in totals]
    for comp in range(2):
        lse_ref[0, 8 * comp : 8 * comp + 1, :] = tops[comp] + jnp.log(totals[comp])
    first, second = 1.0 / totals[0], lam / totals[1]
    gather = turn_ref if flipped else out_ref
    gather[...] = jnp.zeros_like(gather)

    def mix(chunk, carry):
        mixed = (one_ref[chunk] * first - two_ref[chunk] * second).astype(bf16)
        value = kv_ref[span_of(chunk), 2 * DK :]
        gather[...] += dot_tn(value, mixed) if flipped else dot_tn(mixed, value)
        return carry

    lax.fori_loop(0, count, mix, 0, unroll=2)
    if flipped:
        out_ref[...] = jnp.transpose(turn_ref[...])
    out = out_ref[...]
    inverse = lax.rsqrt(jnp.mean(out * out, axis=1, keepdims=True) + head_eps)
    vec_ref[...] = (out * inverse * gain_ref[...] * (1.0 - lambda_init)).astype(bf16)


def backward_kernel(
    prompt_len, top_rows, first_head, lam_ref, q_ref, kv_ref, gain_ref, vec_ref, out_ref, lse_ref, spot_ref, reach_ref,
    dq_ref, dkv_ref, sums_ref, one_ref, two_ref, mix_ref, grad_ref, turn_ref,
):
    lam = lam_ref[first_head + pl.program_id(0)]
    rows, keys = q_ref.shape[0], kv_ref.shape[0]
    scale = DK ** (-0.5)
    out = out_ref[...]
    vec = vec_ref[...]
    inverse = lax.rsqrt(jnp.mean(out * out, axis=1, keepdims=True) + head_eps)
    plain = vec * out * inverse * (1.0 - lambda_init)
    scaled = vec * gain_ref[...] * (1.0 - lambda_init)
    grad_ref[...] = (
        inverse * scaled - out * inverse**3 * jnp.mean(out * scaled, axis=1, keepdims=True)
    ).astype(bf16)
    gain_part = jnp.sum(plain, axis=0, keepdims=True)
    grad = grad_ref[...]
    count = keys // CHUNK
    first_cont = prompt_len // CHUNK

    def weigh(chunk):
        span = pl.ds(pl.multiple_of(chunk * CHUNK, CHUNK), CHUNK)
        for comp, ref in ((0, one_ref), (1, two_ref)):
            lanes = slice(comp * DK, (comp + 1) * DK)
            scores = dot_nt(kv_ref[span, lanes], q_ref[:, lanes])
            ref[chunk] = jnp.exp(scores * scale - lse_ref[0, 8 * comp : 8 * comp + 1, :])
        mix_ref[chunk] = dot_nt(kv_ref[span, 2 * DK :], grad)

    def gather_sums(chunk, sums):
        span = pl.ds(pl.multiple_of(chunk * CHUNK, CHUNK), CHUNK)
        one, two, mix = one_ref[chunk], two_ref[chunk], mix_ref[chunk]
        mixed = (one - lam * two).astype(bf16)
        dkv_ref[span, 2 * DK :] = dot_nn(mixed, grad).astype(bf16)
        return (
            sums[0] + jnp.sum((one * mix).reshape(CHUNK // 8, 8, rows), axis=0),
            sums[1] + jnp.sum((two * mix).reshape(CHUNK // 8, 8, rows), axis=0),
        )

    def prompt_chunk(chunk, sums):
        weigh(chunk)
        allowed = spot_ref[pl.ds(chunk * CHUNK, CHUNK), :top_rows] <= reach_ref[0:1, :top_rows]
        for ref in (one_ref, two_ref):
            ref[chunk, :, :top_rows] = jnp.where(allowed, ref[chunk, :, :top_rows], 0.0)
        return gather_sums(chunk, sums)

    def cont_chunk(chunk, sums):
        weigh(chunk)
        spot = lax.broadcasted_iota(jnp.int32, (CHUNK, rows), 0) + (chunk * CHUNK - prompt_len)
        allowed = (spot >= reach_ref[1:2, :]) & (spot <= reach_ref[2:3, :])
        for ref in (one_ref, two_ref):
            ref[chunk] = jnp.where(allowed, ref[chunk], 0.0)
        return gather_sums(chunk, sums)

    sums = (jnp.zeros((8, rows), f32), jnp.zeros((8, rows), f32))
    sums = lax.fori_loop(0, first_cont, prompt_chunk, sums, unroll=2)
    sums = lax.fori_loop(first_cont, count, cont_chunk, sums, unroll=2)
    first = jnp.sum(sums[0], axis=0, keepdims=True)
    second = jnp.sum(sums[1], axis=0, keepdims=True)
    sums_ref[0, 0:1, :] = gain_part
    sums_ref[0, 1:2, :] = jnp.broadcast_to(-jnp.sum(second, axis=1, keepdims=True), (1, DV))
    turn_ref[...] = jnp.zeros_like(turn_ref)

    def back(chunk, carry):
        span = pl.ds(pl.multiple_of(chunk * CHUNK, CHUNK), CHUNK)
        mix = mix_ref[chunk]
        grads = (
            (one_ref[chunk] * (mix - first)).astype(bf16),
            (two_ref[chunk] * ((mix - second) * (-lam))).astype(bf16),
        )
        for comp in range(2):
            lanes = slice(comp * DK, (comp + 1) * DK)
            dkv_ref[span, lanes] = (dot_nn(grads[comp], q_ref[:, lanes]) * scale).astype(bf16)
            turn_ref[lanes, :] += dot_tn(kv_ref[span, lanes], grads[comp])
        return carry

    lax.fori_loop(0, count, back, 0, unroll=2)
    dq_ref[...] = (turn_ref[...] * scale).astype(bf16)


def attend(queries, keys_values, lam_vec, gain_rows, prompt_spots, bounds, prompt_part, span):
    first, heads = span[0], span[1] - span[0]
    rows, keys = queries.shape[0], keys_values.shape[0]
    prompt_len = prompt_spots.shape[0]
    top_rows = min(rows, -(-prompt_part // 128) * 128)
    count = keys // CHUNK
    return pl.pallas_call(
        lambda *refs: forward_kernel(prompt_len, top_rows, first, *refs),
        grid=(heads,),
        in_specs=[
            pl.BlockSpec(memory_space=pltpu.SMEM),
            pl.BlockSpec((rows, 2 * DK), lambda h: (0, h + first)),
            pl.BlockSpec((keys, 2 * DK + DV), lambda h: (0, h + first)),
            pl.BlockSpec((1, DV), lambda h: (0, h + first)),
            pl.BlockSpec((prompt_len, 128), lambda h: (0, 0)),
            pl.BlockSpec((8, rows), lambda h: (0, 0)),
        ],
        out_specs=[
            pl.BlockSpec((rows, DV), lambda h: (0, h)),
            pl.BlockSpec((rows, DV), lambda h: (0, h)),
            pl.BlockSpec((1, 16, rows), lambda h: (h, 0, 0)),
        ],
        out_shape=[
            jax.ShapeDtypeStruct((rows, heads * DV), f32),
            jax.ShapeDtypeStruct((rows, heads * DV), bf16),
            jax.ShapeDtypeStruct((heads, 16, rows), f32),
        ],
        scratch_shapes=[
            pltpu.VMEM((count, CHUNK, rows), f32),
            pltpu.VMEM((count, CHUNK, rows), f32),
            pltpu.VMEM((DV, rows), f32),
        ],
        compiler_params=pltpu.CompilerParams(vmem_limit_bytes=56 * 2**20),
        name="attend",
        cost_estimate=pl.CostEstimate(flops=14_000_000_000, transcendentals=0, bytes_accessed=0),
    )(
        lam_vec,
        queries,
        keys_values,
        gain_rows,
        jnp.broadcast_to(prompt_spots[:, None], (prompt_len, 128)),
        jnp.concatenate([jnp.stack(bounds), jnp.zeros((5, rows), jnp.int32)]),
    )


def attend_back(
    queries, keys_values, lam_vec, gain_rows, vec_grad, out, lse, prompt_spots, bounds, prompt_part, span, done
):
    first, heads, all_heads = span[0], span[1] - span[0], lam_vec.shape[0]
    rows, keys = queries.shape[0], keys_values.shape[0]
    prompt_len = prompt_spots.shape[0]
    top_rows = min(rows, -(-prompt_part // 128) * 128)
    count = keys // CHUNK
    reach = jnp.concatenate([jnp.stack(bounds), jnp.zeros((5, rows), jnp.int32)])
    return pl.pallas_call(
        lambda *refs: backward_kernel(prompt_len, top_rows, first, *refs[:9], *refs[9 + len(done) :]),
        grid=(heads,),
        in_specs=[
            pl.BlockSpec(memory_space=pltpu.SMEM),
            pl.BlockSpec((rows, 2 * DK), lambda h: (0, h + first)),
            pl.BlockSpec((keys, 2 * DK + DV), lambda h: (0, h + first)),
            pl.BlockSpec((1, DV), lambda h: (0, h + first)),
            pl.BlockSpec((rows, DV), lambda h: (0, h + first)),
            pl.BlockSpec((rows, DV), lambda h: (0, h + first)),
            pl.BlockSpec((1, 16, rows), lambda h: (h + first, 0, 0)),
            pl.BlockSpec((prompt_len, 128), lambda h: (0, 0)),
            pl.BlockSpec((8, rows), lambda h: (0, 0)),
        ]
        + [pl.BlockSpec(memory_space=pl.ANY)] * len(done),
        out_specs=[
            pl.BlockSpec((2 * DK, rows), lambda h: (h + first, 0)),
            pl.BlockSpec((keys, 2 * DK + DV), lambda h: (0, h + first)),
            pl.BlockSpec((1, 8, DV), lambda h: (h + first, 0, 0)),
        ],
        out_shape=[
            jax.ShapeDtypeStruct((all_heads * 2 * DK, rows), bf16),
            jax.ShapeDtypeStruct((keys, all_heads * (2 * DK + DV)), bf16),
            jax.ShapeDtypeStruct((all_heads, 8, DV), f32),
        ],
        input_output_aliases={9 + k: k for k in range(len(done))},
        scratch_shapes=[
            pltpu.VMEM((count, CHUNK, rows), f32),
            pltpu.VMEM((count, CHUNK, rows), f32),
            pltpu.VMEM((count, CHUNK, rows), f32),
            pltpu.VMEM((rows, DV), bf16),
            pltpu.VMEM((2 * DK, rows), f32),
        ],
        compiler_params=pltpu.CompilerParams(vmem_limit_bytes=58 * 2**20),
        name="attend_back",
        cost_estimate=pl.CostEstimate(
            flops=0, transcendentals=0, bytes_accessed=0
        ),
    )(
        lam_vec,
        queries,
        keys_values,
        gain_rows,
        vec_grad,
        out,
        lse,
        jnp.broadcast_to(prompt_spots[:, None], (prompt_len, 128)),
        reach,
        *done,
    )


def norm_kernel(count, unit, blocks_ref, swap_ref, *refs):
    *sources, gain_ref, out_ref = refs
    step = pl.program_id(0)
    all_rows, depth = out_ref.shape
    block = depth // count
    upper = count // 4
    rows = all_rows // upper

    def norm_from(pieces, stride):
        for part in range(upper):
            span = slice(part * stride, part * stride + rows)
            total = jnp.zeros((rows, 128), f32)
            for piece in pieces:
                for lane in range(0, piece.shape[1], 128):
                    x = piece[span, lane : lane + 128].astype(f32)
                    total = total + x * x
            total = jnp.sum(total, axis=1, keepdims=True)
            inverse = jnp.broadcast_to(lax.rsqrt(total * (1.0 / depth) + norm_eps), (rows, block))
            size = depth // len(pieces)
            for spot in range(count):
                lanes = slice(spot * block, (spot + 1) * block)
                side = (spot % upper) * 4 * block // size
                start = pl.multiple_of(blocks_ref[spot] * block - side * size, block)
                x = pieces[side][span, pl.ds(start, block)].astype(f32)
                out_ref[part * rows : (part + 1) * rows, lanes] = (
                    x * inverse * gain_ref[:, lanes]
                ).astype(bf16)

    for core in range(2):
        for turn in range(2):

            @pl.when((step >= core * 2) & (step < core * 2 + 2) & (swap_ref[0] == turn))
            def _():
                pair = sources[2 * core : 2 * core + 2]
                norm_from(pair[::-1] if turn else pair, unit)

    @pl.when(step >= 4)
    def _():
        norm_from(sources[4:5], rows)


def norm_keys(at, prompt_groups, cont_tokens, gain_row, prompt_part):
    cont_len, depth = cont_tokens.shape
    count, upper = at.count, at.upper
    unit = prompt_groups[0].shape[0] // (2 * upper)
    group_rows = upper * prompt_part
    if (depth // count) % 128 or cont_len % group_rows or upper % 2:
        cores = []
        for pair in (prompt_groups[:2], prompt_groups[2:]):
            parts = jnp.stack([part.reshape(2 * upper, unit, -1)[:, :prompt_part] for part in pair])
            parts = at.flip(parts.reshape(2, 2 * upper * prompt_part, depth // 2), 0, at.tensor)
            cores.append(jnp.concatenate([parts[0], parts[1]], axis=1))
        rows = at.to_relative(jnp.concatenate(cores + [cont_tokens], axis=0))
        rows = rows.astype(f32)
        return (rows * inv_rms(rows, norm_eps) * gain_row).astype(bf16)

    def spot_of(core):
        return lambda i, blocks, swap: (jnp.clip(i - 2 * core, 0, 1), 0)

    return pl.pallas_call(
        lambda *refs: norm_kernel(count, unit, *refs),
        grid_spec=pltpu.PrefetchScalarGridSpec(
            num_scalar_prefetch=2,
            grid=(4 + cont_len // group_rows,),
            in_specs=[
                pl.BlockSpec((upper * unit, depth // 2), spot_of(core)) for core in (0, 0, 1, 1)
            ]
            + [
                pl.BlockSpec(
                    (group_rows, depth), lambda i, blocks, swap: (jnp.maximum(i - 4, 0), 0)
                ),
                pl.BlockSpec((1, depth), lambda i, blocks, swap: (0, 0)),
            ],
            out_specs=pl.BlockSpec((group_rows, depth), lambda i, blocks, swap: (i, 0)),
        ),
        out_shape=jax.ShapeDtypeStruct((prompt_part * count + cont_len, depth), bf16),
        compiler_params=pltpu.CompilerParams(vmem_limit_bytes=56 * 2**20),
        name="norm_keys",
        cost_estimate=pl.CostEstimate(flops=8_000_000_000, transcendentals=0, bytes_accessed=0),
    )(
        at.relative_blocks(),
        at.tensor.reshape(1).astype(jnp.int32),
        *prompt_groups,
        cont_tokens,
        gain_row.reshape(1, depth),
    )


def per_device(
    tokens,
    cotangent,
    cont_ids,
    q_weight,
    k_weight,
    v_weight,
    out_weight,
    attn_gain,
    head_gain,
    lam_q1,
    lam_k1,
    lam_q2,
    lam_k2,
    gate_weight,
    up_weight,
    down_weight,
    ffn_gain,
):
    at = Places()
    local_rows = tokens.shape[0]
    block_rows = 2 * local_rows
    row_ids = cont_ids[0]
    cont_len = row_ids.shape[0]
    prompt_part = block_rows - cont_len
    prompt_len = prompt_part * at.count
    heads = q_weight.shape[1] // (2 * DK)
    width = heads * 2 * DK
    shard_rows = q_weight.shape[0]

    small_parts = (attn_gain, ffn_gain, head_gain, lam_q1, lam_k1, lam_q2, lam_k2)
    small = jnp.concatenate([part.reshape(-1) for part in small_parts])
    half = D // 2
    small_rows = jnp.zeros((16, half), bf16).at[0, : small.size].set(small)
    prompt_sent = lax.ppermute(tokens[:prompt_part, half:], "tensor", [(0, 1)])
    prompt_own = jnp.where(at.tensor == 0, tokens[:prompt_part, :half], prompt_sent)
    prompt_own = jnp.concatenate([prompt_own, small_rows], axis=0)
    prompt_here = at.gather_upper(prompt_own)

    def by_head(weight):
        return weight.reshape(shard_rows, heads, -1)

    kv_here = at.gather_upper(
        after(
            jnp.concatenate([by_head(k_weight), by_head(v_weight)], axis=2).reshape(
                shard_rows, -1
            ),
            prompt_own,
        )
    )
    q_here = at.gather_upper(after(q_weight, prompt_own))
    out_here = at.gather_upper(after(out_weight, prompt_own))
    gate_here = at.gather_upper(after(gate_weight, prompt_own))
    up_here = at.gather_upper(after(up_weight, prompt_own))
    down_here = at.gather_upper(after(down_weight, prompt_own))

    tokens_rel = at.to_relative(tokens)
    cot_rel = at.to_relative(cotangent)
    tokens_turned = at.swap_tensor(after(tokens, prompt_own))
    prompt_here, tokens_rel, cot_rel, tokens_turned = together(
        prompt_here, tokens_rel, cot_rel, tokens_turned
    )
    prompt_pair = jnp.concatenate([prompt_here, at.swap_side(prompt_here)], axis=0)
    prompt_turned = at.swap_tensor(prompt_pair)
    prompt_far = at.swap_core(prompt_pair)
    kv_here = after(kv_here, prompt_pair)
    kv_side, kv_near = at.swap_side(kv_here), at.swap_core(kv_here)
    prompt_turned, kv_side_early = together(prompt_turned, kv_near)
    kv_near = kv_side_early
    prompt_far_turned = at.swap_core(prompt_turned)
    kv_side, q_here = together(kv_side, q_here)
    kv_far = at.swap_core(kv_side)
    q_side, q_near = at.swap_side(q_here), at.swap_core(q_here)
    prompt_far, prompt_far_turned = together(prompt_far, after(prompt_far_turned, kv_side))
    cont_tokens = at.in_order(tokens, tokens_turned)[prompt_part:]
    cot_turned = at.swap_tensor(after(cot_rel, prompt_far_turned))

    small_all = jnp.concatenate(
        [
            group.reshape(2 * at.upper, -1, half)[:, prompt_part, : small.size]
            for group in (prompt_pair, prompt_far)
        ],
        axis=0,
    ).astype(f32)
    small_full = []
    start = 0
    for part in small_parts:
        small_full.append(
            small_all[:, start : start + part.size].reshape((at.count,) + part.shape)
        )
        start += part.size
    attn_gain_row = small_full[0].reshape(-1)
    ffn_gain_row = small_full[1].reshape(-1)
    head_gain_row = at.block_order(small_full[2]).reshape(DV, heads).T.reshape(1, heads * DV)
    first_exp = jnp.exp(jnp.sum(small_full[3] * small_full[4], axis=(0, 1)))
    second_exp = jnp.exp(jnp.sum(small_full[5] * small_full[6], axis=(0, 1)))
    lam_vec = first_exp - second_exp + lambda_init

    prompt_spots = (
        at.relative_blocks()[:, None] * prompt_part
        + jnp.arange(prompt_part, dtype=jnp.int32)[None]
    ).reshape(-1)
    cont_spot = jnp.arange(cont_len, dtype=jnp.int32)
    earlier = jnp.sum((row_ids[None, :] < row_ids[:, None]).astype(jnp.int32), axis=1)
    far_spot = jnp.full((prompt_part,), prompt_len + cont_len, jnp.int32)
    reach = jnp.concatenate(
        [
            at.index * prompt_part + jnp.arange(prompt_part, dtype=jnp.int32),
            jnp.full((cont_len,), prompt_len, jnp.int32),
        ]
    )
    bounds = (
        reach,
        jnp.concatenate([far_spot, earlier]),
        jnp.concatenate([jnp.full((prompt_part,), -1, jnp.int32), cont_spot]),
    )

    tokens_f32 = tokens_rel.astype(f32)
    prompt_groups = (prompt_pair, prompt_turned, prompt_far, prompt_far_turned)
    normed_keys = norm_keys(at, prompt_groups, cont_tokens, attn_gain_row, prompt_part)
    kv_near, kv_far = after(kv_near, normed_keys), after(kv_far, normed_keys)
    kv_full = jnp.concatenate([kv_here, kv_side, kv_near, kv_far], axis=0)
    kv_full, q_side, out_here = together(kv_full, q_side, out_here)
    q_far = at.swap_core(q_side)
    out_side, out_near = at.swap_side(out_here), at.swap_core(out_here)
    own_block = lax.dynamic_slice_in_dim(
        normed_keys, (at.index // 4) * prompt_part, prompt_part, 0
    )
    normed = jnp.concatenate([own_block, normed_keys[prompt_len:]], axis=0)
    keys_values = plain_product(normed_keys, kv_full).astype(bf16)
    keys_values, out_side, gate_here = together(keys_values, out_side, gate_here)
    out_far = at.swap_core(out_side)
    gate_side, gate_near = at.swap_side(gate_here), at.swap_core(gate_here)
    q_parts = [after(part, keys_values) for part in (q_here, q_side, q_near, q_far)]
    q_full = jnp.concatenate(q_parts, axis=0)
    queries = plain_product(after(normed, keys_values), q_full).astype(bf16)
    fixed = (lam_vec, head_gain_row, prompt_spots, bounds, prompt_part)
    heads_out, attn_vec, lse = attend(queries, keys_values, *fixed, (0, heads))
    attn_vec, cot_turned = together(attn_vec, cot_turned)
    out_near, out_far = after(out_near, attn_vec), after(out_far, attn_vec)
    out_full = jnp.concatenate([out_here, out_side, out_near, out_far], axis=0)
    attn_own, attn_other = at.own_half(attn_vec), at.other_half(attn_vec)
    out_send = cols_product(attn_other, out_full).astype(bf16)
    out_sent = at.swap_tensor(out_send)
    out_part = cols_product(after(attn_own, out_send), out_full)
    attn_two = jnp.concatenate([attn_own, attn_other], axis=0)
    out_part, attn_two, gate_side, up_here = together(out_part, attn_two, gate_side, up_here)
    up_side, up_near = at.swap_side(up_here), at.swap_core(up_here)
    gate_far = at.swap_core(gate_side)
    out_sent = after(out_sent, gate_side)
    residual = tokens_f32 + (out_part + out_sent.astype(f32))

    inv_second = inv_rms(residual, norm_eps)
    ffn_own = (residual * inv_second * ffn_gain_row).astype(bf16)
    ffn_turned = at.swap_tensor(ffn_own)
    gate_near, gate_far = after(gate_near, ffn_own), after(gate_far, ffn_own)
    gate_full = jnp.concatenate([gate_here, gate_side, gate_near, gate_far], axis=0)
    gate_full, down_here, up_side = together(gate_full, down_here, up_side)
    up_far = at.swap_core(up_side)
    down_side, down_near = at.swap_side(down_here), at.swap_core(down_here)
    ffn_turned = after(ffn_turned, gate_full)
    ffn_in = jnp.concatenate([ffn_own, ffn_turned], axis=0)
    gate_proj = plain_product(ffn_in, gate_full)
    cot_rows = jnp.concatenate([cot_rel, cot_turned], axis=0)
    up_near, up_far = after(up_near, gate_proj), after(up_far, gate_proj)
    up_full = jnp.concatenate([up_here, up_side, up_near, up_far], axis=0)
    up_proj = plain_product(after(ffn_in, gate_proj), up_full)
    gate_sigmoid = jax.nn.sigmoid(gate_proj)
    hidden = (gate_proj * gate_sigmoid * up_proj).astype(bf16)

    down_far_aside, down_send = at.far_part(cot_rows, hidden, 3)
    down_far_keep, down_send = at.far_part(cot_rows, after(hidden, down_send), 2)
    down_send, down_side = together(down_send, down_side)
    down_near = after(down_near, down_side)
    down_far = at.swap_core(down_side)
    down_far_aside = after(down_far_aside, down_side)
    down_grad_side = at.aside_part(cot_rows, hidden, down_far_aside)
    down_grad_aside = at.swap_side(down_grad_side)
    down_near, down_far = after(down_near, down_grad_side), after(down_far, down_grad_side)
    down_full = jnp.concatenate([down_here, down_side, down_near, down_far], axis=0)
    hidden_grad = plain_product(cot_rows, down_full)
    gate_grad = (
        hidden_grad * up_proj * gate_sigmoid * (1.0 + gate_proj * (1.0 - gate_sigmoid))
    ).astype(bf16)
    up_grad = (hidden_grad * gate_proj * gate_sigmoid).astype(bf16)

    def back_ffn(one, two, features=slice(None)):
        return cols_product(one, gate_full[features]) + cols_product(two, up_full[features])

    gate_far_aside, gate_send = at.far_part_two(ffn_in, gate_grad)
    gate_other, up_other = after(gate_grad[local_rows:], gate_send), up_grad[local_rows:]
    ffn_sends = [back_ffn(gate_other, up_other, slice(0, half)).astype(bf16)]
    gate_other, up_other = after(gate_other, ffn_sends[0]), after(up_other, ffn_sends[0])
    ffn_sends.append(back_ffn(gate_other, up_other, slice(half, D)).astype(bf16))
    ffn_sent = [at.swap_tensor(send) for send in ffn_sends]
    gate_far_aside = after(gate_far_aside, ffn_sends[1])
    gate_grad_side = at.aside_part(ffn_in, gate_grad, gate_far_aside)
    gate_grad_aside = at.swap_side(gate_grad_side)
    ffn_part = cols_product(after(gate_grad[:local_rows], gate_grad_side), gate_full)
    ffn_part, down_grad_aside = together(ffn_part, down_grad_aside)
    down_far_keep = after(down_far_keep, ffn_part)
    down_last = at.near_part(cot_rows, hidden, down_far_keep, down_grad_aside)
    grad_down = at.scatter_upper(down_last)
    ffn_part = ffn_part + cols_product(after(up_grad[:local_rows], down_last), up_full)
    gate_far_keep, gate_send = at.far_part(ffn_in, after(gate_grad, ffn_part), 2)
    ffn_sent = together(after(ffn_sent[0], gate_send), ffn_sent[1])
    ffn_in_grad = ffn_part + jnp.concatenate(ffn_sent, axis=1).astype(f32)
    residual_grad = cot_rel.astype(f32) + norm_back(
        residual, inv_second, ffn_gain_row, ffn_in_grad
    )

    branch_own = residual_grad.astype(bf16)
    branch_sent = at.swap_tensor(branch_own)
    up_far_aside, up_send = at.far_part_two(ffn_in, after(up_grad, branch_own))
    up_far_keep, up_send = at.far_part(ffn_in, after(up_grad, up_send), 2)
    branch = jnp.concatenate([branch_own, after(branch_sent, up_send)], axis=0)
    vec_two = plain_product(branch, out_full)
    vec_grad = at.in_order(vec_two[:local_rows], vec_two[local_rows:])
    vec_grad, gate_grad_aside = together(vec_grad, gate_grad_aside)
    gate_far_keep = after(gate_far_keep, gate_grad_aside)
    gate_last = at.near_part(ffn_in, gate_grad, gate_far_keep, gate_grad_aside)
    grad_gate = at.scatter_upper(gate_last)
    up_far_aside = after(up_far_aside, gate_last)
    up_grad_side = at.aside_part(ffn_in, up_grad, up_far_aside)
    up_grad_aside = at.swap_side(up_grad_side)
    queries_grad, kv_grad, head_sums = attend_back(
        queries,
        keys_values,
        lam_vec,
        head_gain_row,
        after(vec_grad, up_grad_side),
        heads_out,
        lse,
        prompt_spots,
        bounds,
        prompt_part,
        (0, heads),
        (),
    )
    queries_grad, kv_grad, head_sums, grad_down = together(
        queries_grad, kv_grad, head_sums, grad_down
    )
    queries_grad = queries_grad.T

    quarter = prompt_len // 4

    def prompt_rows(part):
        return kv_grad[part * quarter : (part + 1) * quarter]

    prompt_send = prompt_rows(3)
    prompt_far_aside = at.swap_core(prompt_send)
    prompt_keep = after(prompt_rows(2), prompt_send)
    prompt_far_keep = at.swap_core(prompt_keep)
    kv_far_aside, kv_send = at.far_part(normed_keys, after(kv_grad, prompt_keep), 3)
    kv_send, up_far_keep, up_grad_aside = together(kv_send, up_far_keep, up_grad_aside)
    prompt_far_aside = after(prompt_far_aside, up_grad_aside)
    prompt_side = (prompt_rows(1).astype(f32) + prompt_far_aside.astype(f32)).astype(bf16)
    prompt_aside = at.swap_side(prompt_side)
    up_last = at.near_part(ffn_in, after(up_grad, prompt_side), up_far_keep, up_grad_aside)
    up_last, grad_gate = together(up_last, grad_gate)
    grad_up = at.scatter_upper(up_last)
    kv_far_keep, kv_send = at.far_part(normed_keys, after(kv_grad, up_last), 2)
    kv_far_aside = after(kv_far_aside, kv_send)
    kv_grad_side = at.aside_part(normed_keys, kv_grad, kv_far_aside)
    kv_grad_aside = at.swap_side(kv_grad_side)
    q_far_aside, q_send = at.far_part(normed, after(queries_grad, kv_grad_side), 3)
    q_far_keep, q_send = at.far_part(normed, after(queries_grad, q_send), 2)
    out_far_aside, out_send_grad = at.far_part(branch, after(attn_two, q_send), 3)
    out_far_keep, out_send_grad = at.far_part(branch, after(attn_two, out_send_grad), 2)
    hidden_late = after(hidden, out_send_grad)
    output_part = cols_product(hidden_late[:local_rows], down_full)
    prompt_far_keep, prompt_aside = together(after(prompt_far_keep, output_part), prompt_aside)
    prompt_last = (
        prompt_rows(0).astype(f32) + prompt_far_keep.astype(f32) + prompt_aside.astype(f32)
    ).astype(bf16)
    prompt_grad = at.scatter_upper(prompt_last)
    q_far_aside = after(q_far_aside, prompt_last)
    q_grad_side = at.aside_part(normed, queries_grad, q_far_aside)
    q_grad_aside = at.swap_side(q_grad_side)
    out_far_aside = after(out_far_aside, q_grad_side)
    out_grad_side = at.aside_part(branch, attn_two, out_far_aside)
    out_grad_aside = at.swap_side(out_grad_side)
    output_send = cols_product(after(hidden_late, out_grad_side)[local_rows:], down_full).astype(bf16)
    output_sent = at.swap_tensor(output_send)
    kv_far_keep, kv_grad_aside = together(after(kv_far_keep, output_send), kv_grad_aside)
    kv_last = at.near_part(normed_keys, kv_grad, kv_far_keep, kv_grad_aside)
    grad_kv = at.scatter_upper(kv_last)
    output_sent, grad_up, q_far_keep = together(after(output_sent, kv_last), grad_up, q_far_keep)
    q_far_keep, q_grad_aside = together(q_far_keep, q_grad_aside)
    q_last = at.near_part(normed, queries_grad, q_far_keep, q_grad_aside)
    grad_q = at.scatter_upper(q_last)
    prompt_grad = after(prompt_grad, q_last)
    here_grad = jnp.concatenate([prompt_grad, kv_grad[prompt_len:]], axis=0)

    def back_attn(half_of):
        return cols_product(half_of(queries_grad), q_full) + cols_product(
            half_of(here_grad), kv_full
        )

    normed_send = back_attn(at.other_half).astype(bf16)
    normed_sent = at.swap_tensor(normed_send)
    out_far_keep, out_grad_aside = together(after(out_far_keep, normed_send), out_grad_aside)
    out_last = at.near_part(branch, attn_two, out_far_keep, out_grad_aside)
    grad_out = at.scatter_upper(out_last)
    normed_part = back_attn(lambda rows: at.own_half(after(rows, out_last)))
    normed_grad = normed_part + normed_sent.astype(f32)
    inv_first = inv_rms(tokens_f32, norm_eps)
    tokens_grad = residual_grad + norm_back(tokens_f32, inv_first, attn_gain_row, normed_grad)
    tokens_grad = at.from_relative(tokens_grad.astype(bf16))
    output = at.from_relative((residual + (output_part + output_sent.astype(f32))).astype(bf16))

    def row_sum(grad, weight):
        return jnp.sum(grad.astype(f32) * weight.astype(f32), axis=1)

    head_sums = at.sum_small(jnp.concatenate([head_sums[:, 0], head_sums[:, 1]], axis=1))
    head_gain_sum, lam_sum = head_sums[:, :DV], head_sums[:, DV]
    head_rows = head_gain.shape[0]
    grad_head_gain = lax.dynamic_slice_in_dim(head_gain_sum.T, at.index * head_rows, head_rows, 0)
    one_scale, two_scale = lam_sum * first_exp, -lam_sum * second_exp
    grad_q = grad_q.astype(f32)
    grad_kv = grad_kv.astype(f32).reshape(shard_rows, heads, -1)
    grad_k = grad_kv[:, :, : 2 * DK].reshape(shard_rows, -1)
    grad_v = grad_kv[:, :, 2 * DK :].reshape(shard_rows, -1)
    attn_gain_part = row_sum(grad_q, q_weight) + row_sum(grad_k, k_weight) + row_sum(grad_v, v_weight)
    ffn_gain_part = row_sum(grad_gate, gate_weight) + row_sum(grad_up, up_weight)
    attn_gain_sum = attn_gain_part + at.swap_tensor(attn_gain_part)
    ffn_gain_sum = ffn_gain_part + at.swap_tensor(ffn_gain_part)
    return (
        output,
        tokens_grad,
        grad_q,
        grad_k,
        grad_v,
        after(grad_out, attn_gain_sum).astype(f32),
        attn_gain_sum / attn_gain.astype(f32),
        grad_head_gain,
        one_scale * lam_k1.astype(f32),
        one_scale * lam_q1.astype(f32),
        two_scale * lam_k2.astype(f32),
        two_scale * lam_q2.astype(f32),
        grad_gate.astype(f32),
        grad_up.astype(f32),
        grad_down.astype(f32),
        ffn_gain_sum / ffn_gain.astype(f32),
    )


def solution(mesh):
    rows = P(("dp", "tensor"), None)
    both = P("dp", "tensor")
    placed = (
        (rows, rows, P("dp", None))
        + (both,) * 4
        + (P("dp"),)
        + (both,) * 5
        + (both,) * 3
        + (P("dp"),)
    )
    return jax.shard_map(
        per_device,
        mesh=mesh,
        in_specs=placed,
        out_specs=(rows, rows)
        + (both,) * 4
        + (P("dp"),)
        + (both,) * 5
        + (both,) * 3
        + (P("dp"),),
        check_vma=False,
    )
```

```python
import jax
import jax.numpy as jnp
from jax import lax
from jax.experimental import pallas as pl
from jax.experimental.pallas import tpu as pltpu
from jax.sharding import PartitionSpec as P

D = 2048
DK = 128
DV = 256

norm_eps = 1e-06
head_eps = 1e-05
lambda_init = 0.2
masked_value = -1e30
f32 = jnp.float32
bf16 = jnp.bfloat16
CHUNK = 512


def inv_rms(entries, eps_value):
    return lax.rsqrt(jnp.mean(entries * entries, axis=-1, keepdims=True) + eps_value)


def norm_back(entries, inverse, gain_row, incoming):
    scaled = gain_row * incoming
    return inverse * scaled - entries * inverse**3 * jnp.mean(
        entries * scaled, axis=-1, keepdims=True
    )


def plain_product(first_arg, second_arg):
    return jnp.dot(first_arg, second_arg, preferred_element_type=f32)


def rows_product(first_arg, second_arg):
    return lax.dot_general(
        first_arg, second_arg, (((0,), (0,)), ((), ())), preferred_element_type=f32
    )


def cols_product(first_arg, second_arg):
    return lax.dot_general(
        first_arg, second_arg, (((1,), (1,)), ((), ())), preferred_element_type=f32
    )


def together(*values):
    return lax.optimization_barrier(values)


def after(value, *others):
    if not others:
        return value
    return lax.optimization_barrier((value,) + others)[0]


class Places:
    def __init__(self):
        self.count = lax.axis_size("dp")
        self.upper = self.count // 4
        index = lax.axis_index("dp")
        self.index = index
        self.core = index % 2
        self.side = (index // 2) % 2
        self.tensor = lax.axis_index("tensor")
        self.upper_groups = [
            [low + 4 * high for high in range(self.upper)] for low in range(4)
        ]
        self.core_pairs = [(k, k ^ 1) for k in range(self.count)]
        self.side_pairs = [(k, k ^ 2) for k in range(self.count)]

    def swap_core(self, value):
        return lax.ppermute(value, "dp", self.core_pairs)

    def swap_side(self, value):
        return lax.ppermute(value, "dp", self.side_pairs)

    def swap_tensor(self, value):
        return lax.ppermute(value, "tensor", [(0, 1), (1, 0)])

    def gather_upper(self, shard):
        return lax.all_gather(
            shard, "dp", axis=0, tiled=True, axis_index_groups=self.upper_groups
        )

    def sum_small(self, value):
        step = 1
        while step < self.count:
            value = value + lax.ppermute(
                value, "dp", [(k, k ^ step) for k in range(self.count)]
            )
            step *= 2
        return value

    def block_order(self, value):
        parts = value.reshape((2, 2, self.upper) + value.shape[1:])
        parts = self.flip(self.flip(parts, 0, self.core), 1, self.side)
        order = (2, 1, 0) + tuple(range(3, parts.ndim))
        return jnp.transpose(parts, order).reshape(value.shape)

    def scatter_upper(self, value):
        return lax.psum_scatter(
            value, "dp", scatter_dimension=0, tiled=True, axis_index_groups=self.upper_groups
        )

    def product_part(self, first_arg, second_arg, part):
        quarter = first_arg.shape[1] // 4
        return rows_product(first_arg[:, part * quarter : (part + 1) * quarter], second_arg)

    def far_part(self, first_arg, second_arg, part):
        send = self.product_part(first_arg, second_arg, part).astype(bf16)
        return self.swap_core(send), send

    def far_part_two(self, first_arg, second_arg):
        send = self.product_part(first_arg, second_arg, 3).astype(bf16)
        middle = send.shape[0] // 2
        pieces = [self.swap_core(send[:middle]), self.swap_core(send[middle:])]
        return jnp.concatenate(pieces, axis=0), send

    def aside_part(self, first_arg, second_arg, far):
        return (self.product_part(first_arg, second_arg, 1) + far.astype(f32)).astype(bf16)

    def near_part(self, first_arg, second_arg, far, aside):
        near = self.product_part(first_arg, second_arg, 0) + far.astype(f32)
        return (near + aside.astype(f32)).astype(bf16)

    def flip(self, value, axis, bit):
        return jnp.where(bit == 1, jnp.flip(value, axis), value)

    def to_relative(self, value):
        lead = value.shape[:-1]
        parts = value.reshape(lead + (self.upper, 2, 2, value.shape[-1] // self.count))
        k = len(lead)
        order = tuple(range(k)) + (k + 2, k + 1, k, k + 3)
        parts = jnp.transpose(parts, order)
        parts = self.flip(self.flip(parts, k, self.core), k + 1, self.side)
        return parts.reshape(value.shape)

    def from_relative(self, value):
        lead = value.shape[:-1]
        parts = value.reshape(lead + (2, 2, self.upper, value.shape[-1] // self.count))
        k = len(lead)
        parts = self.flip(self.flip(parts, k, self.core), k + 1, self.side)
        order = tuple(range(k)) + (k + 2, k + 1, k, k + 3)
        return jnp.transpose(parts, order).reshape(value.shape)

    def relative_blocks(self):
        spot = jnp.arange(self.count, dtype=jnp.int32)
        core = spot // (2 * self.upper)
        side = (spot // self.upper) % 2
        high = spot % self.upper
        return high * 4 + (side ^ self.side) * 2 + (core ^ self.core)

    def own_half(self, rows):
        half = rows.shape[0] // 2
        return lax.dynamic_slice_in_dim(rows, self.tensor * half, half, 0)

    def other_half(self, rows):
        half = rows.shape[0] // 2
        return lax.dynamic_slice_in_dim(rows, (1 - self.tensor) * half, half, 0)

    def in_order(self, own, other):
        return jnp.where(
            self.tensor == 0,
            jnp.concatenate([own, other], axis=0),
            jnp.concatenate([other, own], axis=0),
        )


def dot_nt(first, second):
    return lax.dot_general(first, second, (((1,), (1,)), ((), ())), preferred_element_type=f32)


def dot_nn(first, second):
    return lax.dot_general(first, second, (((1,), (0,)), ((), ())), preferred_element_type=f32)


def dot_tn(first, second):
    return lax.dot_general(first, second, (((0,), (0,)), ((), ())), preferred_element_type=f32)


def forward_kernel(
    prompt_len, top_rows, first_head, lam_ref, q_ref, kv_ref, gain_ref, spot_ref, reach_ref,
    out_ref, vec_ref, lse_ref, one_ref, two_ref, turn_ref,
):
    lam = lam_ref[first_head + pl.program_id(0)]
    rows, keys = q_ref.shape[0], kv_ref.shape[0]
    scale = DK ** (-0.5)
    count = keys // CHUNK
    first_cont = prompt_len // CHUNK
    flipped = rows % 128 == 0

    def span_of(chunk):
        return pl.ds(pl.multiple_of(chunk * CHUNK, CHUNK), CHUNK)

    def eights(values):
        return values.reshape(CHUNK // 8, 8, rows)

    def score(chunk, allowed, columns, tops):
        news = []
        for comp, ref in ((0, one_ref), (1, two_ref)):
            lanes = slice(comp * DK, (comp + 1) * DK)
            scores = dot_nt(kv_ref[span_of(chunk), lanes], q_ref[:, lanes])
            masked = jnp.where(allowed, scores[:, :columns], masked_value)
            if columns < rows:
                masked = jnp.concatenate([masked, scores[:, columns:]], axis=1)
            ref[chunk] = masked
            news.append(jnp.maximum(tops[comp], jnp.max(eights(masked), axis=0)))
        return tuple(news)

    def prompt_chunk(chunk, tops):
        allowed = spot_ref[span_of(chunk), :top_rows] <= reach_ref[0:1, :top_rows]
        return score(chunk, allowed, top_rows, tops)

    def cont_chunk(chunk, tops):
        spot = lax.broadcasted_iota(jnp.int32, (CHUNK, rows), 0) + (chunk * CHUNK - prompt_len)
        allowed = (spot >= reach_ref[1:2, :]) & (spot <= reach_ref[2:3, :])
        return score(chunk, allowed, rows, tops)

    tops = (jnp.full((8, rows), masked_value, f32),) * 2
    tops = lax.fori_loop(0, first_cont, prompt_chunk, tops, unroll=2)
    tops = lax.fori_loop(first_cont, count, cont_chunk, tops, unroll=2)
    tops = [jnp.max(top, axis=0, keepdims=True) * scale for top in tops]

    def weigh(chunk, totals):
        news = []
        for comp, ref in ((0, one_ref), (1, two_ref)):
            terms = jnp.exp(ref[chunk] * scale - tops[comp])
            ref[chunk] = terms
            news.append(totals[comp] + jnp.sum(eights(terms), axis=0))
        return tuple(news)

    totals = lax.fori_loop(0, count, weigh, (jnp.zeros((8, rows), f32),) * 2)
    totals = [jnp.sum(total, axis=0, keepdims=True) for total in totals]
    for comp in range(2):
        lse_ref[0, 8 * comp : 8 * comp + 1, :] = tops[comp] + jnp.log(totals[comp])
    first, second = 1.0 / totals[0], lam / totals[1]
    gather = turn_ref if flipped else out_ref
    gather[...] = jnp.zeros_like(gather)

    def mix(chunk, carry):
        mixed = (one_ref[chunk] * first - two_ref[chunk] * second).astype(bf16)
        value = kv_ref[span_of(chunk), 2 * DK :]
        gather[...] += dot_tn(value, mixed) if flipped else dot_tn(mixed, value)
        return carry

    lax.fori_loop(0, count, mix, 0, unroll=2)
    if flipped:
        out_ref[...] = jnp.transpose(turn_ref[...])
    out = out_ref[...]
    inverse = lax.rsqrt(jnp.mean(out * out, axis=1, keepdims=True) + head_eps)
    vec_ref[...] = (out * inverse * gain_ref[...] * (1.0 - lambda_init)).astype(bf16)


def backward_kernel(
    prompt_len, top_rows, first_head, lam_ref, q_ref, kv_ref, gain_ref, vec_ref, out_ref, lse_ref, spot_ref, reach_ref,
    dq_ref, dkv_ref, sums_ref, one_ref, two_ref, mix_ref, grad_ref, turn_ref,
):
    lam = lam_ref[first_head + pl.program_id(0)]
    rows, keys = q_ref.shape[0], kv_ref.shape[0]
    scale = DK ** (-0.5)
    out = out_ref[...]
    vec = vec_ref[...]
    inverse = lax.rsqrt(jnp.mean(out * out, axis=1, keepdims=True) + head_eps)
    plain = vec * out * inverse * (1.0 - lambda_init)
    scaled = vec * gain_ref[...] * (1.0 - lambda_init)
    grad_ref[...] = (
        inverse * scaled - out * inverse**3 * jnp.mean(out * scaled, axis=1, keepdims=True)
    ).astype(bf16)
    gain_part = jnp.sum(plain, axis=0, keepdims=True)
    grad = grad_ref[...]
    count = keys // CHUNK
    first_cont = prompt_len // CHUNK

    def weigh(chunk):
        span = pl.ds(pl.multiple_of(chunk * CHUNK, CHUNK), CHUNK)
        for comp, ref in ((0, one_ref), (1, two_ref)):
            lanes = slice(comp * DK, (comp + 1) * DK)
            scores = dot_nt(kv_ref[span, lanes], q_ref[:, lanes])
            ref[chunk] = jnp.exp(scores * scale - lse_ref[0, 8 * comp : 8 * comp + 1, :])
        mix_ref[chunk] = dot_nt(kv_ref[span, 2 * DK :], grad)

    def gather_sums(chunk, sums):
        span = pl.ds(pl.multiple_of(chunk * CHUNK, CHUNK), CHUNK)
        one, two, mix = one_ref[chunk], two_ref[chunk], mix_ref[chunk]
        mixed = (one - lam * two).astype(bf16)
        dkv_ref[span, 2 * DK :] = dot_nn(mixed, grad).astype(bf16)
        return (
            sums[0] + jnp.sum((one * mix).reshape(CHUNK // 8, 8, rows), axis=0),
            sums[1] + jnp.sum((two * mix).reshape(CHUNK // 8, 8, rows), axis=0),
        )

    def prompt_chunk(chunk, sums):
        weigh(chunk)
        allowed = spot_ref[pl.ds(chunk * CHUNK, CHUNK), :top_rows] <= reach_ref[0:1, :top_rows]
        for ref in (one_ref, two_ref):
            ref[chunk, :, :top_rows] = jnp.where(allowed, ref[chunk, :, :top_rows], 0.0)
        return gather_sums(chunk, sums)

    def cont_chunk(chunk, sums):
        weigh(chunk)
        spot = lax.broadcasted_iota(jnp.int32, (CHUNK, rows), 0) + (chunk * CHUNK - prompt_len)
        allowed = (spot >= reach_ref[1:2, :]) & (spot <= reach_ref[2:3, :])
        for ref in (one_ref, two_ref):
            ref[chunk] = jnp.where(allowed, ref[chunk], 0.0)
        return gather_sums(chunk, sums)

    sums = (jnp.zeros((8, rows), f32), jnp.zeros((8, rows), f32))
    sums = lax.fori_loop(0, first_cont, prompt_chunk, sums, unroll=2)
    sums = lax.fori_loop(first_cont, count, cont_chunk, sums, unroll=2)
    first = jnp.sum(sums[0], axis=0, keepdims=True)
    second = jnp.sum(sums[1], axis=0, keepdims=True)
    sums_ref[0, 0:1, :] = gain_part
    sums_ref[0, 1:2, :] = jnp.broadcast_to(-jnp.sum(second, axis=1, keepdims=True), (1, DV))
    turn_ref[...] = jnp.zeros_like(turn_ref)

    def back(chunk, carry):
        span = pl.ds(pl.multiple_of(chunk * CHUNK, CHUNK), CHUNK)
        mix = mix_ref[chunk]
        grads = (
            (one_ref[chunk] * (mix - first)).astype(bf16),
            (two_ref[chunk] * ((mix - second) * (-lam))).astype(bf16),
        )
        for comp in range(2):
            lanes = slice(comp * DK, (comp + 1) * DK)
            dkv_ref[span, lanes] = (dot_nn(grads[comp], q_ref[:, lanes]) * scale).astype(bf16)
            turn_ref[lanes, :] += dot_tn(kv_ref[span, lanes], grads[comp])
        return carry

    lax.fori_loop(0, count, back, 0, unroll=2)
    dq_ref[...] = (turn_ref[...] * scale).astype(bf16)


def attend(queries, keys_values, lam_vec, gain_rows, prompt_spots, bounds, prompt_part, span):
    first, heads = span[0], span[1] - span[0]
    rows, keys = queries.shape[0], keys_values.shape[0]
    prompt_len = prompt_spots.shape[0]
    top_rows = min(rows, -(-prompt_part // 128) * 128)
    count = keys // CHUNK
    return pl.pallas_call(
        lambda *refs: forward_kernel(prompt_len, top_rows, first, *refs),
        grid=(heads,),
        in_specs=[
            pl.BlockSpec(memory_space=pltpu.SMEM),
            pl.BlockSpec((rows, 2 * DK), lambda h: (0, h + first)),
            pl.BlockSpec((keys, 2 * DK + DV), lambda h: (0, h + first)),
            pl.BlockSpec((1, DV), lambda h: (0, h + first)),
            pl.BlockSpec((prompt_len, 128), lambda h: (0, 0)),
            pl.BlockSpec((8, rows), lambda h: (0, 0)),
        ],
        out_specs=[
            pl.BlockSpec((rows, DV), lambda h: (0, h)),
            pl.BlockSpec((rows, DV), lambda h: (0, h)),
            pl.BlockSpec((1, 16, rows), lambda h: (h, 0, 0)),
        ],
        out_shape=[
            jax.ShapeDtypeStruct((rows, heads * DV), f32),
            jax.ShapeDtypeStruct((rows, heads * DV), bf16),
            jax.ShapeDtypeStruct((heads, 16, rows), f32),
        ],
        scratch_shapes=[
            pltpu.VMEM((count, CHUNK, rows), f32),
            pltpu.VMEM((count, CHUNK, rows), f32),
            pltpu.VMEM((DV, rows), f32),
        ],
        compiler_params=pltpu.CompilerParams(vmem_limit_bytes=56 * 2**20),
        name="attend",
        cost_estimate=pl.CostEstimate(flops=0, transcendentals=0, bytes_accessed=0),
    )(
        lam_vec,
        queries,
        keys_values,
        gain_rows,
        jnp.broadcast_to(prompt_spots[:, None], (prompt_len, 128)),
        jnp.concatenate([jnp.stack(bounds), jnp.zeros((5, rows), jnp.int32)]),
    )


def attend_back(
    queries, keys_values, lam_vec, gain_rows, vec_grad, out, lse, prompt_spots, bounds, prompt_part, span, done
):
    first, heads, all_heads = span[0], span[1] - span[0], lam_vec.shape[0]
    rows, keys = queries.shape[0], keys_values.shape[0]
    prompt_len = prompt_spots.shape[0]
    top_rows = min(rows, -(-prompt_part // 128) * 128)
    count = keys // CHUNK
    reach = jnp.concatenate([jnp.stack(bounds), jnp.zeros((5, rows), jnp.int32)])
    return pl.pallas_call(
        lambda *refs: backward_kernel(prompt_len, top_rows, first, *refs[:9], *refs[9 + len(done) :]),
        grid=(heads,),
        in_specs=[
            pl.BlockSpec(memory_space=pltpu.SMEM),
            pl.BlockSpec((rows, 2 * DK), lambda h: (0, h + first)),
            pl.BlockSpec((keys, 2 * DK + DV), lambda h: (0, h + first)),
            pl.BlockSpec((1, DV), lambda h: (0, h + first)),
            pl.BlockSpec((rows, DV), lambda h: (0, h + first)),
            pl.BlockSpec((rows, DV), lambda h: (0, h + first)),
            pl.BlockSpec((1, 16, rows), lambda h: (h + first, 0, 0)),
            pl.BlockSpec((prompt_len, 128), lambda h: (0, 0)),
            pl.BlockSpec((8, rows), lambda h: (0, 0)),
        ]
        + [pl.BlockSpec(memory_space=pl.ANY)] * len(done),
        out_specs=[
            pl.BlockSpec((2 * DK, rows), lambda h: (h + first, 0)),
            pl.BlockSpec((keys, 2 * DK + DV), lambda h: (0, h + first)),
            pl.BlockSpec((1, 8, DV), lambda h: (h + first, 0, 0)),
        ],
        out_shape=[
            jax.ShapeDtypeStruct((all_heads * 2 * DK, rows), bf16),
            jax.ShapeDtypeStruct((keys, all_heads * (2 * DK + DV)), bf16),
            jax.ShapeDtypeStruct((all_heads, 8, DV), f32),
        ],
        input_output_aliases={9 + k: k for k in range(len(done))},
        scratch_shapes=[
            pltpu.VMEM((count, CHUNK, rows), f32),
            pltpu.VMEM((count, CHUNK, rows), f32),
            pltpu.VMEM((count, CHUNK, rows), f32),
            pltpu.VMEM((rows, DV), bf16),
            pltpu.VMEM((2 * DK, rows), f32),
        ],
        compiler_params=pltpu.CompilerParams(vmem_limit_bytes=58 * 2**20),
        name="attend_back",
        cost_estimate=pl.CostEstimate(
            flops=0, transcendentals=0, bytes_accessed=0
        ),
    )(
        lam_vec,
        queries,
        keys_values,
        gain_rows,
        vec_grad,
        out,
        lse,
        jnp.broadcast_to(prompt_spots[:, None], (prompt_len, 128)),
        reach,
        *done,
    )


def norm_kernel(count, unit, blocks_ref, swap_ref, *refs):
    *sources, gain_ref, out_ref = refs
    step = pl.program_id(0)
    all_rows, depth = out_ref.shape
    block = depth // count
    upper = count // 4
    rows = all_rows // upper

    def norm_from(pieces, stride):
        for part in range(upper):
            span = slice(part * stride, part * stride + rows)
            total = jnp.zeros((rows, 128), f32)
            for piece in pieces:
                for lane in range(0, piece.shape[1], 128):
                    x = piece[span, lane : lane + 128].astype(f32)
                    total = total + x * x
            total = jnp.sum(total, axis=1, keepdims=True)
            inverse = jnp.broadcast_to(lax.rsqrt(total * (1.0 / depth) + norm_eps), (rows, block))
            size = depth // len(pieces)
            for spot in range(count):
                lanes = slice(spot * block, (spot + 1) * block)
                side = (spot % upper) * 4 * block // size
                start = pl.multiple_of(blocks_ref[spot] * block - side * size, block)
                x = pieces[side][span, pl.ds(start, block)].astype(f32)
                out_ref[part * rows : (part + 1) * rows, lanes] = (
                    x * inverse * gain_ref[:, lanes]
                ).astype(bf16)

    for group in range(4):
        for turn in range(2):

            @pl.when((step == group) & (swap_ref[0] == turn))
            def _():
                pair = sources[2 * group : 2 * group + 2]
                norm_from(pair[::-1] if turn else pair, unit)

    @pl.when(step >= 4)
    def _():
        norm_from(sources[8:9], rows)


def norm_keys(at, prompt_groups, cont_tokens, gain_row, prompt_part):
    cont_len, depth = cont_tokens.shape
    count, upper = at.count, at.upper
    unit = prompt_groups[0][0].shape[0] // upper
    group_rows = upper * prompt_part
    if (depth // count) % 128 or cont_len % group_rows or upper % 2:
        groups = []
        for pair in prompt_groups:
            parts = jnp.stack([part.reshape(upper, unit, -1)[:, :prompt_part] for part in pair])
            parts = at.flip(parts.reshape(2, group_rows, depth // 2), 0, at.tensor)
            groups.append(jnp.concatenate([parts[0], parts[1]], axis=1))
        rows = at.to_relative(jnp.concatenate(groups + [cont_tokens], axis=0))
        rows = rows.astype(f32)
        return (rows * inv_rms(rows, norm_eps) * gain_row).astype(bf16)

    return pl.pallas_call(
        lambda *refs: norm_kernel(count, unit, *refs),
        grid_spec=pltpu.PrefetchScalarGridSpec(
            num_scalar_prefetch=2,
            grid=(4 + cont_len // group_rows,),
            in_specs=[
                pl.BlockSpec((upper * unit, depth // 2), lambda i, blocks, swap: (0, 0))
                for _ in range(8)
            ]
            + [
                pl.BlockSpec(
                    (group_rows, depth), lambda i, blocks, swap: (jnp.maximum(i - 4, 0), 0)
                ),
                pl.BlockSpec((1, depth), lambda i, blocks, swap: (0, 0)),
            ],
            out_specs=pl.BlockSpec((group_rows, depth), lambda i, blocks, swap: (i, 0)),
        ),
        out_shape=jax.ShapeDtypeStruct((prompt_part * count + cont_len, depth), bf16),
        compiler_params=pltpu.CompilerParams(vmem_limit_bytes=56 * 2**20),
        name="norm_keys",
        cost_estimate=pl.CostEstimate(flops=0, transcendentals=0, bytes_accessed=0),
    )(
        at.relative_blocks(),
        at.tensor.reshape(1).astype(jnp.int32),
        *[part for pair in prompt_groups for part in pair],
        cont_tokens,
        gain_row.reshape(1, depth),
    )


def per_device(
    tokens,
    cotangent,
    cont_ids,
    q_weight,
    k_weight,
    v_weight,
    out_weight,
    attn_gain,
    head_gain,
    lam_q1,
    lam_k1,
    lam_q2,
    lam_k2,
    gate_weight,
    up_weight,
    down_weight,
    ffn_gain,
):
    at = Places()
    local_rows = tokens.shape[0]
    block_rows = 2 * local_rows
    row_ids = cont_ids[0]
    cont_len = row_ids.shape[0]
    prompt_part = block_rows - cont_len
    prompt_len = prompt_part * at.count
    heads = q_weight.shape[1] // (2 * DK)
    width = heads * 2 * DK
    shard_rows = q_weight.shape[0]

    small_parts = (attn_gain, ffn_gain, head_gain, lam_q1, lam_k1, lam_q2, lam_k2)
    small = jnp.concatenate([part.reshape(-1) for part in small_parts])
    half = D // 2
    small_rows = jnp.zeros((16, half), bf16).at[0, : small.size].set(small)
    prompt_sent = lax.ppermute(tokens[:prompt_part, half:], "tensor", [(0, 1)])
    prompt_own = jnp.where(at.tensor == 0, tokens[:prompt_part, :half], prompt_sent)
    prompt_own = jnp.concatenate([prompt_own, small_rows], axis=0)
    prompt_here = at.gather_upper(prompt_own)

    def by_head(weight):
        return weight.reshape(shard_rows, heads, -1)

    kv_here = at.gather_upper(
        after(
            jnp.concatenate([by_head(k_weight), by_head(v_weight)], axis=2).reshape(
                shard_rows, -1
            ),
            prompt_own,
        )
    )
    q_here = at.gather_upper(after(q_weight, prompt_own))
    out_here = at.gather_upper(after(out_weight, prompt_own))
    gate_here = at.gather_upper(after(gate_weight, prompt_own))
    up_here = at.gather_upper(after(up_weight, prompt_own))
    down_here = at.gather_upper(after(down_weight, prompt_own))

    tokens_rel = at.to_relative(tokens)
    cot_rel = at.to_relative(cotangent)
    tokens_turned = at.swap_tensor(after(tokens, prompt_own))
    prompt_here, tokens_rel, cot_rel, tokens_turned = together(
        prompt_here, tokens_rel, cot_rel, tokens_turned
    )
    cont_tokens = at.in_order(tokens, tokens_turned)[prompt_part:]
    here_turned, here_far = at.swap_tensor(prompt_here), at.swap_core(prompt_here)
    prompt_side = at.swap_side(prompt_here)
    here_turned, prompt_side, cont_tokens = together(here_turned, prompt_side, cont_tokens)
    side_turned, side_far = at.swap_tensor(prompt_side), at.swap_core(prompt_side)
    here_turned_far = at.swap_core(here_turned)
    kv_here = after(kv_here, prompt_side)
    kv_side, kv_near = at.swap_side(kv_here), at.swap_core(kv_here)
    side_turned = after(side_turned, kv_here)
    side_turned_far = at.swap_core(side_turned)
    prompt_groups = (
        (prompt_here, here_turned),
        (prompt_side, side_turned),
        (here_far, here_turned_far),
        (side_far, side_turned_far),
    )

    small_all = jnp.concatenate(
        [
            group[0].reshape(at.upper, -1, half)[:, prompt_part, : small.size]
            for group in prompt_groups
        ],
        axis=0,
    ).astype(f32)
    small_full = []
    start = 0
    for part in small_parts:
        small_full.append(
            small_all[:, start : start + part.size].reshape((at.count,) + part.shape)
        )
        start += part.size
    attn_gain_row = small_full[0].reshape(-1)
    ffn_gain_row = small_full[1].reshape(-1)
    head_gain_row = at.block_order(small_full[2]).reshape(DV, heads).T.reshape(1, heads * DV)
    first_exp = jnp.exp(jnp.sum(small_full[3] * small_full[4], axis=(0, 1)))
    second_exp = jnp.exp(jnp.sum(small_full[5] * small_full[6], axis=(0, 1)))
    lam_vec = first_exp - second_exp + lambda_init

    prompt_spots = (
        at.relative_blocks()[:, None] * prompt_part
        + jnp.arange(prompt_part, dtype=jnp.int32)[None]
    ).reshape(-1)
    cont_spot = jnp.arange(cont_len, dtype=jnp.int32)
    earlier = jnp.sum((row_ids[None, :] < row_ids[:, None]).astype(jnp.int32), axis=1)
    far_spot = jnp.full((prompt_part,), prompt_len + cont_len, jnp.int32)
    reach = jnp.concatenate(
        [
            at.index * prompt_part + jnp.arange(prompt_part, dtype=jnp.int32),
            jnp.full((cont_len,), prompt_len, jnp.int32),
        ]
    )
    bounds = (
        reach,
        jnp.concatenate([far_spot, earlier]),
        jnp.concatenate([jnp.full((prompt_part,), -1, jnp.int32), cont_spot]),
    )

    tokens_f32 = tokens_rel.astype(f32)
    normed_keys = norm_keys(at, prompt_groups, cont_tokens, attn_gain_row, prompt_part)
    normed_keys, kv_side, q_here = together(normed_keys, kv_side, q_here)
    kv_far = at.swap_core(kv_side)
    q_side, q_near = at.swap_side(q_here), at.swap_core(q_here)
    cot_turned = at.swap_tensor(after(cot_rel, normed_keys))
    kv_near = after(kv_near, kv_side)
    kv_full = jnp.concatenate([kv_here, kv_side, kv_near, kv_far], axis=0)
    keys_values = plain_product(normed_keys, kv_full).astype(bf16)
    keys_values, q_side, out_here, normed_late = together(
        keys_values, q_side, out_here, normed_keys
    )
    q_far = at.swap_core(q_side)
    out_side, out_near = at.swap_side(out_here), at.swap_core(out_here)
    own_block = lax.dynamic_slice_in_dim(
        normed_late, (at.index // 4) * prompt_part, prompt_part, 0
    )
    normed = jnp.concatenate([own_block, normed_late[prompt_len:]], axis=0)
    q_parts = [after(part, keys_values) for part in (q_here, q_side, q_near, q_far)]
    q_full = jnp.concatenate(q_parts, axis=0)
    queries = plain_product(after(normed, keys_values), q_full).astype(bf16)
    queries, out_side, gate_here = together(queries, out_side, gate_here)
    out_far = at.swap_core(out_side)
    gate_side, gate_near = at.swap_side(gate_here), at.swap_core(gate_here)
    fixed = (lam_vec, head_gain_row, prompt_spots, bounds, prompt_part)
    heads_out, attn_vec, lse = attend(queries, keys_values, *fixed, (0, heads))
    attn_vec, cot_turned = together(attn_vec, cot_turned)
    out_near, out_far = after(out_near, attn_vec), after(out_far, attn_vec)
    out_full = jnp.concatenate([out_here, out_side, out_near, out_far], axis=0)
    attn_own, attn_other = at.own_half(attn_vec), at.other_half(attn_vec)
    out_send = cols_product(attn_other, out_full).astype(bf16)
    out_sent = at.swap_tensor(out_send)
    out_part = cols_product(after(attn_own, out_send), out_full)
    attn_two = jnp.concatenate([attn_own, attn_other], axis=0)
    out_part, attn_two, gate_side, up_here = together(out_part, attn_two, gate_side, up_here)
    up_side, up_near = at.swap_side(up_here), at.swap_core(up_here)
    gate_far = at.swap_core(gate_side)
    out_sent = after(out_sent, gate_side)
    residual = tokens_f32 + (out_part + out_sent.astype(f32))

    inv_second = inv_rms(residual, norm_eps)
    ffn_own = (residual * inv_second * ffn_gain_row).astype(bf16)
    ffn_turned = at.swap_tensor(ffn_own)
    gate_near, gate_far = after(gate_near, ffn_own), after(gate_far, ffn_own)
    gate_full = jnp.concatenate([gate_here, gate_side, gate_near, gate_far], axis=0)
    gate_full, down_here, up_side = together(gate_full, down_here, up_side)
    up_far = at.swap_core(up_side)
    down_side, down_near = at.swap_side(down_here), at.swap_core(down_here)
    ffn_turned = after(ffn_turned, gate_full)
    ffn_in = jnp.concatenate([ffn_own, ffn_turned], axis=0)
    gate_proj = plain_product(ffn_in, gate_full)
    cot_rows = jnp.concatenate([cot_rel, cot_turned], axis=0)
    up_near, up_far = after(up_near, gate_proj), after(up_far, gate_proj)
    up_full = jnp.concatenate([up_here, up_side, up_near, up_far], axis=0)
    up_proj = plain_product(after(ffn_in, gate_proj), up_full)
    gate_sigmoid = jax.nn.sigmoid(gate_proj)
    hidden = (gate_proj * gate_sigmoid * up_proj).astype(bf16)

    down_far_aside, down_send = at.far_part(cot_rows, hidden, 3)
    down_far_keep, down_send = at.far_part(cot_rows, after(hidden, down_send), 2)
    down_send, down_side = together(down_send, down_side)
    down_near = after(down_near, down_side)
    down_far = at.swap_core(down_side)
    down_far_aside = after(down_far_aside, down_side)
    down_grad_side = at.aside_part(cot_rows, hidden, down_far_aside)
    down_grad_aside = at.swap_side(down_grad_side)
    down_near, down_far = after(down_near, down_grad_side), after(down_far, down_grad_side)
    down_full = jnp.concatenate([down_here, down_side, down_near, down_far], axis=0)
    hidden_grad = plain_product(cot_rows, down_full)
    gate_grad = (
        hidden_grad * up_proj * gate_sigmoid * (1.0 + gate_proj * (1.0 - gate_sigmoid))
    ).astype(bf16)
    up_grad = (hidden_grad * gate_proj * gate_sigmoid).astype(bf16)

    def back_ffn(one, two, features=slice(None)):
        return cols_product(one, gate_full[features]) + cols_product(two, up_full[features])

    gate_far_aside, gate_send = at.far_part_two(ffn_in, gate_grad)
    gate_other, up_other = after(gate_grad[local_rows:], gate_send), up_grad[local_rows:]
    ffn_sends = [back_ffn(gate_other, up_other, slice(0, half)).astype(bf16)]
    gate_other, up_other = after(gate_other, ffn_sends[0]), after(up_other, ffn_sends[0])
    ffn_sends.append(back_ffn(gate_other, up_other, slice(half, D)).astype(bf16))
    ffn_sent = [at.swap_tensor(send) for send in ffn_sends]
    gate_far_aside = after(gate_far_aside, ffn_sends[1])
    gate_grad_side = at.aside_part(ffn_in, gate_grad, gate_far_aside)
    gate_grad_aside = at.swap_side(gate_grad_side)
    ffn_part = cols_product(after(gate_grad[:local_rows], gate_grad_side), gate_full)
    ffn_part, down_grad_aside = together(ffn_part, down_grad_aside)
    down_far_keep = after(down_far_keep, ffn_part)
    down_last = at.near_part(cot_rows, hidden, down_far_keep, down_grad_aside)
    grad_down = at.scatter_upper(down_last)
    ffn_part = ffn_part + cols_product(after(up_grad[:local_rows], down_last), up_full)
    gate_far_keep, gate_send = at.far_part(ffn_in, after(gate_grad, ffn_part), 2)
    ffn_sent = together(after(ffn_sent[0], gate_send), ffn_sent[1])
    ffn_in_grad = ffn_part + jnp.concatenate(ffn_sent, axis=1).astype(f32)
    residual_grad = cot_rel.astype(f32) + norm_back(
        residual, inv_second, ffn_gain_row, ffn_in_grad
    )

    branch_own = residual_grad.astype(bf16)
    branch_sent = at.swap_tensor(branch_own)
    up_far_aside, up_send = at.far_part_two(ffn_in, after(up_grad, branch_own))
    up_far_keep, up_send = at.far_part(ffn_in, after(up_grad, up_send), 2)
    branch = jnp.concatenate([branch_own, after(branch_sent, up_send)], axis=0)
    vec_two = plain_product(branch, out_full)
    vec_grad = at.in_order(vec_two[:local_rows], vec_two[local_rows:])
    vec_grad, gate_grad_aside = together(vec_grad, gate_grad_aside)
    gate_far_keep = after(gate_far_keep, gate_grad_aside)
    gate_last = at.near_part(ffn_in, gate_grad, gate_far_keep, gate_grad_aside)
    grad_gate = at.scatter_upper(gate_last)
    up_far_aside = after(up_far_aside, gate_last)
    up_grad_side = at.aside_part(ffn_in, up_grad, up_far_aside)
    up_grad_aside = at.swap_side(up_grad_side)
    queries_grad, kv_grad, head_sums = attend_back(
        queries,
        keys_values,
        lam_vec,
        head_gain_row,
        after(vec_grad, up_grad_side),
        heads_out,
        lse,
        prompt_spots,
        bounds,
        prompt_part,
        (0, heads),
        (),
    )
    queries_grad, kv_grad, head_sums, grad_down = together(
        queries_grad, kv_grad, head_sums, grad_down
    )
    queries_grad = queries_grad.T

    quarter = prompt_len // 4

    def prompt_rows(part):
        return kv_grad[part * quarter : (part + 1) * quarter]

    prompt_send = prompt_rows(3)
    prompt_far_aside = at.swap_core(prompt_send)
    prompt_keep = after(prompt_rows(2), prompt_send)
    prompt_far_keep = at.swap_core(prompt_keep)
    kv_far_aside, kv_send = at.far_part(normed_keys, after(kv_grad, prompt_keep), 3)
    kv_send, up_far_keep, up_grad_aside = together(kv_send, up_far_keep, up_grad_aside)
    prompt_far_aside = after(prompt_far_aside, up_grad_aside)
    prompt_side = (prompt_rows(1).astype(f32) + prompt_far_aside.astype(f32)).astype(bf16)
    prompt_aside = at.swap_side(prompt_side)
    up_last = at.near_part(ffn_in, after(up_grad, prompt_side), up_far_keep, up_grad_aside)
    up_last, grad_gate = together(up_last, grad_gate)
    grad_up = at.scatter_upper(up_last)
    kv_far_keep, kv_send = at.far_part(normed_keys, after(kv_grad, up_last), 2)
    kv_far_aside = after(kv_far_aside, kv_send)
    kv_grad_side = at.aside_part(normed_keys, kv_grad, kv_far_aside)
    kv_grad_aside = at.swap_side(kv_grad_side)
    q_far_aside, q_send = at.far_part(normed, after(queries_grad, kv_grad_side), 3)
    q_far_keep, q_send = at.far_part(normed, after(queries_grad, q_send), 2)
    out_far_aside, out_send_grad = at.far_part(branch, after(attn_two, q_send), 3)
    out_far_keep, out_send_grad = at.far_part(branch, after(attn_two, out_send_grad), 2)
    hidden_late = after(hidden, out_send_grad)
    output_part = cols_product(hidden_late[:local_rows], down_full)
    prompt_far_keep, prompt_aside = together(after(prompt_far_keep, output_part), prompt_aside)
    prompt_last = (
        prompt_rows(0).astype(f32) + prompt_far_keep.astype(f32) + prompt_aside.astype(f32)
    ).astype(bf16)
    prompt_grad = at.scatter_upper(prompt_last)
    q_far_aside = after(q_far_aside, prompt_last)
    q_grad_side = at.aside_part(normed, queries_grad, q_far_aside)
    q_grad_aside = at.swap_side(q_grad_side)
    out_far_aside = after(out_far_aside, q_grad_side)
    out_grad_side = at.aside_part(branch, attn_two, out_far_aside)
    out_grad_aside = at.swap_side(out_grad_side)
    output_send = cols_product(after(hidden_late, out_grad_side)[local_rows:], down_full).astype(bf16)
    output_sent = at.swap_tensor(output_send)
    kv_far_keep, kv_grad_aside = together(after(kv_far_keep, output_send), kv_grad_aside)
    kv_last = at.near_part(normed_keys, kv_grad, kv_far_keep, kv_grad_aside)
    grad_kv = at.scatter_upper(kv_last)
    output_sent, grad_up, q_far_keep = together(after(output_sent, kv_last), grad_up, q_far_keep)
    q_far_keep, q_grad_aside = together(q_far_keep, q_grad_aside)
    q_last = at.near_part(normed, queries_grad, q_far_keep, q_grad_aside)
    grad_q = at.scatter_upper(q_last)
    prompt_grad = after(prompt_grad, q_last)
    here_grad = jnp.concatenate([prompt_grad, kv_grad[prompt_len:]], axis=0)

    def back_attn(half_of):
        return cols_product(half_of(queries_grad), q_full) + cols_product(
            half_of(here_grad), kv_full
        )

    normed_send = back_attn(at.other_half).astype(bf16)
    normed_sent = at.swap_tensor(normed_send)
    out_far_keep, out_grad_aside = together(after(out_far_keep, normed_send), out_grad_aside)
    out_last = at.near_part(branch, attn_two, out_far_keep, out_grad_aside)
    grad_out = at.scatter_upper(out_last)
    normed_part = back_attn(lambda rows: at.own_half(after(rows, out_last)))
    normed_grad = normed_part + normed_sent.astype(f32)
    inv_first = inv_rms(tokens_f32, norm_eps)
    tokens_grad = residual_grad + norm_back(tokens_f32, inv_first, attn_gain_row, normed_grad)
    tokens_grad = at.from_relative(tokens_grad.astype(bf16))
    output = at.from_relative((residual + (output_part + output_sent.astype(f32))).astype(bf16))

    def row_sum(grad, weight):
        return jnp.sum(grad.astype(f32) * weight.astype(f32), axis=1)

    head_sums = at.sum_small(jnp.concatenate([head_sums[:, 0], head_sums[:, 1]], axis=1))
    head_gain_sum, lam_sum = head_sums[:, :DV], head_sums[:, DV]
    head_rows = head_gain.shape[0]
    grad_head_gain = lax.dynamic_slice_in_dim(head_gain_sum.T, at.index * head_rows, head_rows, 0)
    one_scale, two_scale = lam_sum * first_exp, -lam_sum * second_exp
    grad_q = grad_q.astype(f32)
    grad_kv = grad_kv.astype(f32).reshape(shard_rows, heads, -1)
    grad_k = grad_kv[:, :, : 2 * DK].reshape(shard_rows, -1)
    grad_v = grad_kv[:, :, 2 * DK :].reshape(shard_rows, -1)
    attn_gain_part = row_sum(grad_q, q_weight) + row_sum(grad_k, k_weight) + row_sum(grad_v, v_weight)
    ffn_gain_part = row_sum(grad_gate, gate_weight) + row_sum(grad_up, up_weight)
    attn_gain_sum = attn_gain_part + at.swap_tensor(attn_gain_part)
    ffn_gain_sum = ffn_gain_part + at.swap_tensor(ffn_gain_part)
    return (
        output,
        tokens_grad,
        grad_q,
        grad_k,
        grad_v,
        after(grad_out, attn_gain_sum).astype(f32),
        attn_gain_sum / attn_gain.astype(f32),
        grad_head_gain,
        one_scale * lam_k1.astype(f32),
        one_scale * lam_q1.astype(f32),
        two_scale * lam_k2.astype(f32),
        two_scale * lam_q2.astype(f32),
        grad_gate.astype(f32),
        grad_up.astype(f32),
        grad_down.astype(f32),
        ffn_gain_sum / ffn_gain.astype(f32),
    )


def solution(mesh):
    rows = P(("dp", "tensor"), None)
    both = P("dp", "tensor")
    placed = (
        (rows, rows, P("dp", None))
        + (both,) * 4
        + (P("dp"),)
        + (both,) * 5
        + (both,) * 3
        + (P("dp"),)
    )
    return jax.shard_map(
        per_device,
        mesh=mesh,
        in_specs=placed,
        out_specs=(rows, rows)
        + (both,) * 4
        + (P("dp"),)
        + (both,) * 5
        + (both,) * 3
        + (P("dp"),),
        check_vma=False,
    )
```

```python
import jax
import jax.numpy as jnp
from jax import lax
from jax.experimental import pallas as pl
from jax.experimental.pallas import tpu as pltpu
from jax.sharding import PartitionSpec as P

D = 2048
DK = 128
DV = 256

norm_eps = 1e-06
head_eps = 1e-05
lambda_init = 0.2
masked_value = -1e30
f32 = jnp.float32
bf16 = jnp.bfloat16
CHUNK = 512


def inv_rms(entries, eps_value):
    return lax.rsqrt(jnp.mean(entries * entries, axis=-1, keepdims=True) + eps_value)


def norm_back(entries, inverse, gain_row, incoming):
    scaled = gain_row * incoming
    return inverse * scaled - entries * inverse**3 * jnp.mean(
        entries * scaled, axis=-1, keepdims=True
    )


def plain_product(first_arg, second_arg):
    return jnp.dot(first_arg, second_arg, preferred_element_type=f32)


def rows_product(first_arg, second_arg):
    return lax.dot_general(
        first_arg, second_arg, (((0,), (0,)), ((), ())), preferred_element_type=f32
    )


def cols_product(first_arg, second_arg):
    return lax.dot_general(
        first_arg, second_arg, (((1,), (1,)), ((), ())), preferred_element_type=f32
    )


def together(*values):
    return lax.optimization_barrier(values)


def after(value, *others):
    if not others:
        return value
    return lax.optimization_barrier((value,) + others)[0]


class Places:
    def __init__(self):
        self.count = lax.axis_size("dp")
        self.upper = self.count // 4
        index = lax.axis_index("dp")
        self.index = index
        self.core = index % 2
        self.side = (index // 2) % 2
        self.tensor = lax.axis_index("tensor")
        self.upper_groups = [
            [low + 4 * high for high in range(self.upper)] for low in range(4)
        ]
        self.core_pairs = [(k, k ^ 1) for k in range(self.count)]
        self.side_pairs = [(k, k ^ 2) for k in range(self.count)]

    def swap_core(self, value):
        return lax.ppermute(value, "dp", self.core_pairs)

    def swap_side(self, value):
        return lax.ppermute(value, "dp", self.side_pairs)

    def swap_tensor(self, value):
        return lax.ppermute(value, "tensor", [(0, 1), (1, 0)])

    def gather_upper(self, shard):
        return lax.all_gather(
            shard, "dp", axis=0, tiled=True, axis_index_groups=self.upper_groups
        )

    def sum_small(self, value):
        step = 1
        while step < self.count:
            value = value + lax.ppermute(
                value, "dp", [(k, k ^ step) for k in range(self.count)]
            )
            step *= 2
        return value

    def block_order(self, value):
        parts = value.reshape((2, 2, self.upper) + value.shape[1:])
        parts = self.flip(self.flip(parts, 0, self.core), 1, self.side)
        order = (2, 1, 0) + tuple(range(3, parts.ndim))
        return jnp.transpose(parts, order).reshape(value.shape)

    def scatter_upper(self, value):
        return lax.psum_scatter(
            value, "dp", scatter_dimension=0, tiled=True, axis_index_groups=self.upper_groups
        )

    def product_part(self, first_arg, second_arg, part):
        quarter = first_arg.shape[1] // 4
        return rows_product(first_arg[:, part * quarter : (part + 1) * quarter], second_arg)

    def far_part(self, first_arg, second_arg, part):
        send = self.product_part(first_arg, second_arg, part).astype(bf16)
        return self.swap_core(send), send

    def far_part_two(self, first_arg, second_arg):
        send = self.product_part(first_arg, second_arg, 3).astype(bf16)
        middle = send.shape[0] // 2
        pieces = [self.swap_core(send[:middle]), self.swap_core(send[middle:])]
        return jnp.concatenate(pieces, axis=0), send

    def aside_part(self, first_arg, second_arg, far):
        return (self.product_part(first_arg, second_arg, 1) + far.astype(f32)).astype(bf16)

    def near_part(self, first_arg, second_arg, far, aside):
        near = self.product_part(first_arg, second_arg, 0) + far.astype(f32)
        return (near + aside.astype(f32)).astype(bf16)

    def flip(self, value, axis, bit):
        return jnp.where(bit == 1, jnp.flip(value, axis), value)

    def to_relative(self, value):
        lead = value.shape[:-1]
        parts = value.reshape(lead + (self.upper, 2, 2, value.shape[-1] // self.count))
        k = len(lead)
        order = tuple(range(k)) + (k + 2, k + 1, k, k + 3)
        parts = jnp.transpose(parts, order)
        parts = self.flip(self.flip(parts, k, self.core), k + 1, self.side)
        return parts.reshape(value.shape)

    def from_relative(self, value):
        lead = value.shape[:-1]
        parts = value.reshape(lead + (2, 2, self.upper, value.shape[-1] // self.count))
        k = len(lead)
        parts = self.flip(self.flip(parts, k, self.core), k + 1, self.side)
        order = tuple(range(k)) + (k + 2, k + 1, k, k + 3)
        return jnp.transpose(parts, order).reshape(value.shape)

    def relative_blocks(self):
        spot = jnp.arange(self.count, dtype=jnp.int32)
        core = spot // (2 * self.upper)
        side = (spot // self.upper) % 2
        high = spot % self.upper
        return high * 4 + (side ^ self.side) * 2 + (core ^ self.core)

    def own_half(self, rows):
        half = rows.shape[0] // 2
        return lax.dynamic_slice_in_dim(rows, self.tensor * half, half, 0)

    def other_half(self, rows):
        half = rows.shape[0] // 2
        return lax.dynamic_slice_in_dim(rows, (1 - self.tensor) * half, half, 0)

    def in_order(self, own, other):
        return jnp.where(
            self.tensor == 0,
            jnp.concatenate([own, other], axis=0),
            jnp.concatenate([other, own], axis=0),
        )


def dot_nt(first, second):
    return lax.dot_general(first, second, (((1,), (1,)), ((), ())), preferred_element_type=f32)


def dot_nn(first, second):
    return lax.dot_general(first, second, (((1,), (0,)), ((), ())), preferred_element_type=f32)


def dot_tn(first, second):
    return lax.dot_general(first, second, (((0,), (0,)), ((), ())), preferred_element_type=f32)


def forward_kernel(
    prompt_len, top_rows, first_head, lam_ref, q_ref, kv_ref, gain_ref, spot_ref, reach_ref,
    out_ref, vec_ref, lse_ref, one_ref, two_ref, turn_ref,
):
    lam = lam_ref[first_head + pl.program_id(0)]
    rows, keys = q_ref.shape[0], kv_ref.shape[0]
    scale = DK ** (-0.5)
    count = keys // CHUNK
    first_cont = prompt_len // CHUNK
    flipped = rows % 128 == 0

    def span_of(chunk):
        return pl.ds(pl.multiple_of(chunk * CHUNK, CHUNK), CHUNK)

    def eights(values):
        return values.reshape(CHUNK // 8, 8, rows)

    def score(chunk, allowed, columns, tops):
        news = []
        for comp, ref in ((0, one_ref), (1, two_ref)):
            lanes = slice(comp * DK, (comp + 1) * DK)
            scores = dot_nt(kv_ref[span_of(chunk), lanes], q_ref[:, lanes])
            masked = jnp.where(allowed, scores[:, :columns], masked_value)
            if columns < rows:
                masked = jnp.concatenate([masked, scores[:, columns:]], axis=1)
            ref[chunk] = masked
            news.append(jnp.maximum(tops[comp], jnp.max(eights(masked), axis=0)))
        return tuple(news)

    def prompt_chunk(chunk, tops):
        allowed = spot_ref[span_of(chunk), :top_rows] <= reach_ref[0:1, :top_rows]
        return score(chunk, allowed, top_rows, tops)

    def cont_chunk(chunk, tops):
        spot = lax.broadcasted_iota(jnp.int32, (CHUNK, rows), 0) + (chunk * CHUNK - prompt_len)
        allowed = (spot >= reach_ref[1:2, :]) & (spot <= reach_ref[2:3, :])
        return score(chunk, allowed, rows, tops)

    tops = (jnp.full((8, rows), masked_value, f32),) * 2
    tops = lax.fori_loop(0, first_cont, prompt_chunk, tops, unroll=2)
    tops = lax.fori_loop(first_cont, count, cont_chunk, tops, unroll=2)
    tops = [jnp.max(top, axis=0, keepdims=True) * scale for top in tops]

    def weigh(chunk, totals):
        news = []
        for comp, ref in ((0, one_ref), (1, two_ref)):
            terms = jnp.exp(ref[chunk] * scale - tops[comp])
            ref[chunk] = terms
            news.append(totals[comp] + jnp.sum(eights(terms), axis=0))
        return tuple(news)

    totals = lax.fori_loop(0, count, weigh, (jnp.zeros((8, rows), f32),) * 2)
    totals = [jnp.sum(total, axis=0, keepdims=True) for total in totals]
    for comp in range(2):
        lse_ref[0, 8 * comp : 8 * comp + 1, :] = tops[comp] + jnp.log(totals[comp])
    first, second = 1.0 / totals[0], lam / totals[1]
    gather = turn_ref if flipped else out_ref
    gather[...] = jnp.zeros_like(gather)

    def mix(chunk, carry):
        mixed = (one_ref[chunk] * first - two_ref[chunk] * second).astype(bf16)
        value = kv_ref[span_of(chunk), 2 * DK :]
        gather[...] += dot_tn(value, mixed) if flipped else dot_tn(mixed, value)
        return carry

    lax.fori_loop(0, count, mix, 0, unroll=2)
    if flipped:
        out_ref[...] = jnp.transpose(turn_ref[...])
    out = out_ref[...]
    inverse = lax.rsqrt(jnp.mean(out * out, axis=1, keepdims=True) + head_eps)
    vec_ref[...] = (out * inverse * gain_ref[...] * (1.0 - lambda_init)).astype(bf16)


def backward_kernel(
    prompt_len, top_rows, first_head, lam_ref, q_ref, kv_ref, gain_ref, vec_ref, out_ref, lse_ref, spot_ref, reach_ref,
    dq_ref, dkv_ref, sums_ref, one_ref, two_ref, mix_ref, grad_ref, turn_ref,
):
    lam = lam_ref[first_head + pl.program_id(0)]
    rows, keys = q_ref.shape[0], kv_ref.shape[0]
    scale = DK ** (-0.5)
    out = out_ref[...]
    vec = vec_ref[...]
    inverse = lax.rsqrt(jnp.mean(out * out, axis=1, keepdims=True) + head_eps)
    plain = vec * out * inverse * (1.0 - lambda_init)
    scaled = vec * gain_ref[...] * (1.0 - lambda_init)
    grad_ref[...] = (
        inverse * scaled - out * inverse**3 * jnp.mean(out * scaled, axis=1, keepdims=True)
    ).astype(bf16)
    gain_part = jnp.sum(plain, axis=0, keepdims=True)
    grad = grad_ref[...]
    count = keys // CHUNK
    first_cont = prompt_len // CHUNK

    def weigh(chunk):
        span = pl.ds(pl.multiple_of(chunk * CHUNK, CHUNK), CHUNK)
        for comp, ref in ((0, one_ref), (1, two_ref)):
            lanes = slice(comp * DK, (comp + 1) * DK)
            scores = dot_nt(kv_ref[span, lanes], q_ref[:, lanes])
            ref[chunk] = jnp.exp(scores * scale - lse_ref[0, 8 * comp : 8 * comp + 1, :])
        mix_ref[chunk] = dot_nt(kv_ref[span, 2 * DK :], grad)

    def gather_sums(chunk, sums):
        span = pl.ds(pl.multiple_of(chunk * CHUNK, CHUNK), CHUNK)
        one, two, mix = one_ref[chunk], two_ref[chunk], mix_ref[chunk]
        mixed = (one - lam * two).astype(bf16)
        dkv_ref[span, 2 * DK :] = dot_nn(mixed, grad).astype(bf16)
        return (
            sums[0] + jnp.sum((one * mix).reshape(CHUNK // 8, 8, rows), axis=0),
            sums[1] + jnp.sum((two * mix).reshape(CHUNK // 8, 8, rows), axis=0),
        )

    def prompt_chunk(chunk, sums):
        weigh(chunk)
        allowed = spot_ref[pl.ds(chunk * CHUNK, CHUNK), :top_rows] <= reach_ref[0:1, :top_rows]
        for ref in (one_ref, two_ref):
            ref[chunk, :, :top_rows] = jnp.where(allowed, ref[chunk, :, :top_rows], 0.0)
        return gather_sums(chunk, sums)

    def cont_chunk(chunk, sums):
        weigh(chunk)
        spot = lax.broadcasted_iota(jnp.int32, (CHUNK, rows), 0) + (chunk * CHUNK - prompt_len)
        allowed = (spot >= reach_ref[1:2, :]) & (spot <= reach_ref[2:3, :])
        for ref in (one_ref, two_ref):
            ref[chunk] = jnp.where(allowed, ref[chunk], 0.0)
        return gather_sums(chunk, sums)

    sums = (jnp.zeros((8, rows), f32), jnp.zeros((8, rows), f32))
    sums = lax.fori_loop(0, first_cont, prompt_chunk, sums, unroll=2)
    sums = lax.fori_loop(first_cont, count, cont_chunk, sums, unroll=2)
    first = jnp.sum(sums[0], axis=0, keepdims=True)
    second = jnp.sum(sums[1], axis=0, keepdims=True)
    sums_ref[0, 0:1, :] = gain_part
    sums_ref[0, 1:2, :] = jnp.broadcast_to(-jnp.sum(second, axis=1, keepdims=True), (1, DV))
    turn_ref[...] = jnp.zeros_like(turn_ref)

    def back(chunk, carry):
        span = pl.ds(pl.multiple_of(chunk * CHUNK, CHUNK), CHUNK)
        mix = mix_ref[chunk]
        grads = (
            (one_ref[chunk] * (mix - first)).astype(bf16),
            (two_ref[chunk] * ((mix - second) * (-lam))).astype(bf16),
        )
        for comp in range(2):
            lanes = slice(comp * DK, (comp + 1) * DK)
            dkv_ref[span, lanes] = (dot_nn(grads[comp], q_ref[:, lanes]) * scale).astype(bf16)
            turn_ref[lanes, :] += dot_tn(kv_ref[span, lanes], grads[comp])
        return carry

    lax.fori_loop(0, count, back, 0, unroll=2)
    dq_ref[...] = (turn_ref[...] * scale).astype(bf16)


def attend(queries, keys_values, lam_vec, gain_rows, prompt_spots, bounds, prompt_part, span):
    first, heads = span[0], span[1] - span[0]
    rows, keys = queries.shape[0], keys_values.shape[0]
    prompt_len = prompt_spots.shape[0]
    top_rows = min(rows, -(-prompt_part // 128) * 128)
    count = keys // CHUNK
    return pl.pallas_call(
        lambda *refs: forward_kernel(prompt_len, top_rows, first, *refs),
        grid=(heads,),
        in_specs=[
            pl.BlockSpec(memory_space=pltpu.SMEM),
            pl.BlockSpec((rows, 2 * DK), lambda h: (0, h + first)),
            pl.BlockSpec((keys, 2 * DK + DV), lambda h: (0, h + first)),
            pl.BlockSpec((1, DV), lambda h: (0, h + first)),
            pl.BlockSpec((prompt_len, 128), lambda h: (0, 0)),
            pl.BlockSpec((8, rows), lambda h: (0, 0)),
        ],
        out_specs=[
            pl.BlockSpec((rows, DV), lambda h: (0, h)),
            pl.BlockSpec((rows, DV), lambda h: (0, h)),
            pl.BlockSpec((1, 16, rows), lambda h: (h, 0, 0)),
        ],
        out_shape=[
            jax.ShapeDtypeStruct((rows, heads * DV), f32),
            jax.ShapeDtypeStruct((rows, heads * DV), bf16),
            jax.ShapeDtypeStruct((heads, 16, rows), f32),
        ],
        scratch_shapes=[
            pltpu.VMEM((count, CHUNK, rows), f32),
            pltpu.VMEM((count, CHUNK, rows), f32),
            pltpu.VMEM((DV, rows), f32),
        ],
        compiler_params=pltpu.CompilerParams(vmem_limit_bytes=56 * 2**20),
        name="attend",
        cost_estimate=pl.CostEstimate(flops=0, transcendentals=0, bytes_accessed=0),
    )(
        lam_vec,
        queries,
        keys_values,
        gain_rows,
        jnp.broadcast_to(prompt_spots[:, None], (prompt_len, 128)),
        jnp.concatenate([jnp.stack(bounds), jnp.zeros((5, rows), jnp.int32)]),
    )


def attend_back(
    queries, keys_values, lam_vec, gain_rows, vec_grad, out, lse, prompt_spots, bounds, prompt_part, span, done
):
    first, heads, all_heads = span[0], span[1] - span[0], lam_vec.shape[0]
    rows, keys = queries.shape[0], keys_values.shape[0]
    prompt_len = prompt_spots.shape[0]
    top_rows = min(rows, -(-prompt_part // 128) * 128)
    count = keys // CHUNK
    reach = jnp.concatenate([jnp.stack(bounds), jnp.zeros((5, rows), jnp.int32)])
    return pl.pallas_call(
        lambda *refs: backward_kernel(prompt_len, top_rows, first, *refs[:9], *refs[9 + len(done) :]),
        grid=(heads,),
        in_specs=[
            pl.BlockSpec(memory_space=pltpu.SMEM),
            pl.BlockSpec((rows, 2 * DK), lambda h: (0, h + first)),
            pl.BlockSpec((keys, 2 * DK + DV), lambda h: (0, h + first)),
            pl.BlockSpec((1, DV), lambda h: (0, h + first)),
            pl.BlockSpec((rows, DV), lambda h: (0, h + first)),
            pl.BlockSpec((rows, DV), lambda h: (0, h + first)),
            pl.BlockSpec((1, 16, rows), lambda h: (h + first, 0, 0)),
            pl.BlockSpec((prompt_len, 128), lambda h: (0, 0)),
            pl.BlockSpec((8, rows), lambda h: (0, 0)),
        ]
        + [pl.BlockSpec(memory_space=pl.ANY)] * len(done),
        out_specs=[
            pl.BlockSpec((2 * DK, rows), lambda h: (h + first, 0)),
            pl.BlockSpec((keys, 2 * DK + DV), lambda h: (0, h + first)),
            pl.BlockSpec((1, 8, DV), lambda h: (h + first, 0, 0)),
        ],
        out_shape=[
            jax.ShapeDtypeStruct((all_heads * 2 * DK, rows), bf16),
            jax.ShapeDtypeStruct((keys, all_heads * (2 * DK + DV)), bf16),
            jax.ShapeDtypeStruct((all_heads, 8, DV), f32),
        ],
        input_output_aliases={9 + k: k for k in range(len(done))},
        scratch_shapes=[
            pltpu.VMEM((count, CHUNK, rows), f32),
            pltpu.VMEM((count, CHUNK, rows), f32),
            pltpu.VMEM((count, CHUNK, rows), f32),
            pltpu.VMEM((rows, DV), bf16),
            pltpu.VMEM((2 * DK, rows), f32),
        ],
        compiler_params=pltpu.CompilerParams(vmem_limit_bytes=58 * 2**20),
        name="attend_back",
        cost_estimate=pl.CostEstimate(
            flops=0, transcendentals=0, bytes_accessed=0
        ),
    )(
        lam_vec,
        queries,
        keys_values,
        gain_rows,
        vec_grad,
        out,
        lse,
        jnp.broadcast_to(prompt_spots[:, None], (prompt_len, 128)),
        reach,
        *done,
    )


def norm_kernel(count, unit, blocks_ref, swap_ref, *refs):
    *sources, gain_ref, out_ref = refs
    step = pl.program_id(0)
    all_rows, depth = out_ref.shape
    block = depth // count
    upper = count // 4
    rows = all_rows // upper

    def norm_from(pieces, stride):
        for part in range(upper):
            span = slice(part * stride, part * stride + rows)
            total = jnp.zeros((rows, 128), f32)
            for piece in pieces:
                for lane in range(0, piece.shape[1], 128):
                    x = piece[span, lane : lane + 128].astype(f32)
                    total = total + x * x
            total = jnp.sum(total, axis=1, keepdims=True)
            inverse = jnp.broadcast_to(lax.rsqrt(total * (1.0 / depth) + norm_eps), (rows, block))
            size = depth // len(pieces)
            for spot in range(count):
                lanes = slice(spot * block, (spot + 1) * block)
                side = (spot % upper) * 4 * block // size
                start = pl.multiple_of(blocks_ref[spot] * block - side * size, block)
                x = pieces[side][span, pl.ds(start, block)].astype(f32)
                out_ref[part * rows : (part + 1) * rows, lanes] = (
                    x * inverse * gain_ref[:, lanes]
                ).astype(bf16)

    for group in range(4):
        for turn in range(2):

            @pl.when((step == group) & (swap_ref[0] == turn))
            def _():
                pair = sources[2 * group : 2 * group + 2]
                norm_from(pair[::-1] if turn else pair, unit)

    @pl.when(step >= 4)
    def _():
        norm_from(sources[8:9], rows)


def norm_keys(at, prompt_groups, cont_tokens, gain_row, prompt_part):
    cont_len, depth = cont_tokens.shape
    count, upper = at.count, at.upper
    unit = prompt_groups[0][0].shape[0] // upper
    group_rows = upper * prompt_part
    if (depth // count) % 128 or cont_len % group_rows or upper % 2:
        groups = []
        for pair in prompt_groups:
            parts = jnp.stack([part.reshape(upper, unit, -1)[:, :prompt_part] for part in pair])
            parts = at.flip(parts.reshape(2, group_rows, depth // 2), 0, at.tensor)
            groups.append(jnp.concatenate([parts[0], parts[1]], axis=1))
        rows = at.to_relative(jnp.concatenate(groups + [cont_tokens], axis=0))
        rows = rows.astype(f32)
        return (rows * inv_rms(rows, norm_eps) * gain_row).astype(bf16)

    return pl.pallas_call(
        lambda *refs: norm_kernel(count, unit, *refs),
        grid_spec=pltpu.PrefetchScalarGridSpec(
            num_scalar_prefetch=2,
            grid=(4 + cont_len // group_rows,),
            in_specs=[
                pl.BlockSpec((upper * unit, depth // 2), lambda i, blocks, swap: (0, 0))
                for _ in range(8)
            ]
            + [
                pl.BlockSpec(
                    (group_rows, depth), lambda i, blocks, swap: (jnp.maximum(i - 4, 0), 0)
                ),
                pl.BlockSpec((1, depth), lambda i, blocks, swap: (0, 0)),
            ],
            out_specs=pl.BlockSpec((group_rows, depth), lambda i, blocks, swap: (i, 0)),
        ),
        out_shape=jax.ShapeDtypeStruct((prompt_part * count + cont_len, depth), bf16),
        compiler_params=pltpu.CompilerParams(vmem_limit_bytes=56 * 2**20),
        name="norm_keys",
        cost_estimate=pl.CostEstimate(flops=0, transcendentals=0, bytes_accessed=0),
    )(
        at.relative_blocks(),
        at.tensor.reshape(1).astype(jnp.int32),
        *[part for pair in prompt_groups for part in pair],
        cont_tokens,
        gain_row.reshape(1, depth),
    )


def per_device(
    tokens,
    cotangent,
    cont_ids,
    q_weight,
    k_weight,
    v_weight,
    out_weight,
    attn_gain,
    head_gain,
    lam_q1,
    lam_k1,
    lam_q2,
    lam_k2,
    gate_weight,
    up_weight,
    down_weight,
    ffn_gain,
):
    at = Places()
    local_rows = tokens.shape[0]
    block_rows = 2 * local_rows
    row_ids = cont_ids[0]
    cont_len = row_ids.shape[0]
    prompt_part = block_rows - cont_len
    prompt_len = prompt_part * at.count
    heads = q_weight.shape[1] // (2 * DK)
    width = heads * 2 * DK
    shard_rows = q_weight.shape[0]

    small_parts = (attn_gain, ffn_gain, head_gain, lam_q1, lam_k1, lam_q2, lam_k2)
    small = jnp.concatenate([part.reshape(-1) for part in small_parts])
    half = D // 2
    small_rows = jnp.zeros((16, half), bf16).at[0, : small.size].set(small)
    prompt_sent = lax.ppermute(tokens[:prompt_part, half:], "tensor", [(0, 1)])
    prompt_own = jnp.where(at.tensor == 0, tokens[:prompt_part, :half], prompt_sent)
    prompt_own = jnp.concatenate([prompt_own, small_rows], axis=0)
    prompt_here = at.gather_upper(prompt_own)

    def by_head(weight):
        return weight.reshape(shard_rows, heads, -1)

    kv_here = at.gather_upper(
        after(
            jnp.concatenate([by_head(k_weight), by_head(v_weight)], axis=2).reshape(
                shard_rows, -1
            ),
            prompt_own,
        )
    )
    joint_here = at.gather_upper(
        after(jnp.concatenate([q_weight, out_weight], axis=1), prompt_own)
    )
    gate_here = at.gather_upper(after(gate_weight, prompt_own))
    up_here = at.gather_upper(after(up_weight, prompt_own))
    down_here = at.gather_upper(after(down_weight, prompt_own))

    tokens_rel = at.to_relative(tokens)
    cot_rel = at.to_relative(cotangent)
    tokens_turned = at.swap_tensor(after(tokens, prompt_own))
    prompt_here, tokens_rel, cot_rel, tokens_turned = together(
        prompt_here, tokens_rel, cot_rel, tokens_turned
    )
    cont_tokens = at.in_order(tokens, tokens_turned)[prompt_part:]
    here_turned, here_far = at.swap_tensor(prompt_here), at.swap_core(prompt_here)
    prompt_side = at.swap_side(prompt_here)
    here_turned, prompt_side, cont_tokens = together(here_turned, prompt_side, cont_tokens)
    side_turned, side_far = at.swap_tensor(prompt_side), at.swap_core(prompt_side)
    here_turned_far = at.swap_core(here_turned)
    kv_here = after(kv_here, prompt_side)
    kv_side, kv_near = at.swap_side(kv_here), at.swap_core(kv_here)
    side_turned = after(side_turned, kv_here)
    side_turned_far = at.swap_core(side_turned)
    prompt_groups = (
        (prompt_here, here_turned),
        (prompt_side, side_turned),
        (here_far, here_turned_far),
        (side_far, side_turned_far),
    )

    small_all = jnp.concatenate(
        [
            group[0].reshape(at.upper, -1, half)[:, prompt_part, : small.size]
            for group in prompt_groups
        ],
        axis=0,
    ).astype(f32)
    small_full = []
    start = 0
    for part in small_parts:
        small_full.append(
            small_all[:, start : start + part.size].reshape((at.count,) + part.shape)
        )
        start += part.size
    attn_gain_row = small_full[0].reshape(-1)
    ffn_gain_row = small_full[1].reshape(-1)
    head_gain_row = at.block_order(small_full[2]).reshape(DV, heads).T.reshape(1, heads * DV)
    first_exp = jnp.exp(jnp.sum(small_full[3] * small_full[4], axis=(0, 1)))
    second_exp = jnp.exp(jnp.sum(small_full[5] * small_full[6], axis=(0, 1)))
    lam_vec = first_exp - second_exp + lambda_init

    prompt_spots = (
        at.relative_blocks()[:, None] * prompt_part
        + jnp.arange(prompt_part, dtype=jnp.int32)[None]
    ).reshape(-1)
    cont_spot = jnp.arange(cont_len, dtype=jnp.int32)
    earlier = jnp.sum((row_ids[None, :] < row_ids[:, None]).astype(jnp.int32), axis=1)
    far_spot = jnp.full((prompt_part,), prompt_len + cont_len, jnp.int32)
    reach = jnp.concatenate(
        [
            at.index * prompt_part + jnp.arange(prompt_part, dtype=jnp.int32),
            jnp.full((cont_len,), prompt_len, jnp.int32),
        ]
    )
    bounds = (
        reach,
        jnp.concatenate([far_spot, earlier]),
        jnp.concatenate([jnp.full((prompt_part,), -1, jnp.int32), cont_spot]),
    )

    tokens_f32 = tokens_rel.astype(f32)
    normed_keys = norm_keys(at, prompt_groups, cont_tokens, attn_gain_row, prompt_part)
    normed_keys, kv_side, joint_here = together(normed_keys, kv_side, joint_here)
    kv_far = at.swap_core(kv_side)
    joint_side, joint_near = at.swap_side(joint_here), at.swap_core(joint_here)
    cot_turned = at.swap_tensor(after(cot_rel, normed_keys))
    kv_near = after(kv_near, kv_side)
    kv_full = jnp.concatenate([kv_here, kv_side, kv_near, kv_far], axis=0)
    keys_values = plain_product(normed_keys, kv_full).astype(bf16)
    keys_values, joint_side, normed_late = together(keys_values, joint_side, normed_keys)
    joint_far = at.swap_core(joint_side)
    joint_far, gate_here = together(joint_far, gate_here)
    gate_side, gate_near = at.swap_side(gate_here), at.swap_core(gate_here)
    joint = (joint_here, joint_side, joint_near, joint_far)
    own_block = lax.dynamic_slice_in_dim(
        normed_late, (at.index // 4) * prompt_part, prompt_part, 0
    )
    normed = jnp.concatenate([own_block, normed_late[prompt_len:]], axis=0)
    q_full = jnp.concatenate([after(part, gate_here)[:, :width] for part in joint], axis=0)
    q_full = lax.optimization_barrier(q_full)
    queries = plain_product(after(normed, keys_values), q_full).astype(bf16)
    fixed = (lam_vec, head_gain_row, prompt_spots, bounds, prompt_part)
    heads_out, attn_vec, lse = attend(queries, keys_values, *fixed, (0, heads))
    attn_vec, cot_turned = together(attn_vec, cot_turned)
    out_full = jnp.concatenate([after(part, attn_vec)[:, width:] for part in joint], axis=0)
    out_full = lax.optimization_barrier(out_full)
    attn_own, attn_other = at.own_half(attn_vec), at.other_half(attn_vec)
    out_send = cols_product(attn_other, out_full).astype(bf16)
    out_sent = at.swap_tensor(out_send)
    out_part = cols_product(after(attn_own, out_send), out_full)
    attn_two = jnp.concatenate([attn_own, attn_other], axis=0)
    out_part, attn_two, gate_side, up_here = together(out_part, attn_two, gate_side, up_here)
    up_side, up_near = at.swap_side(up_here), at.swap_core(up_here)
    gate_far = at.swap_core(gate_side)
    out_sent = after(out_sent, gate_side)
    residual = tokens_f32 + (out_part + out_sent.astype(f32))

    inv_second = inv_rms(residual, norm_eps)
    ffn_own = (residual * inv_second * ffn_gain_row).astype(bf16)
    ffn_turned = at.swap_tensor(ffn_own)
    gate_near, gate_far = after(gate_near, ffn_own), after(gate_far, ffn_own)
    gate_full = jnp.concatenate([gate_here, gate_side, gate_near, gate_far], axis=0)
    gate_full, down_here, up_side = together(gate_full, down_here, up_side)
    up_far = at.swap_core(up_side)
    down_side, down_near = at.swap_side(down_here), at.swap_core(down_here)
    ffn_turned = after(ffn_turned, gate_full)
    ffn_in = jnp.concatenate([ffn_own, ffn_turned], axis=0)
    gate_proj = plain_product(ffn_in, gate_full)
    cot_rows = jnp.concatenate([cot_rel, cot_turned], axis=0)
    up_near, up_far = after(up_near, gate_proj), after(up_far, gate_proj)
    up_full = jnp.concatenate([up_here, up_side, up_near, up_far], axis=0)
    up_proj = plain_product(after(ffn_in, gate_proj), up_full)
    gate_sigmoid = jax.nn.sigmoid(gate_proj)
    hidden = (gate_proj * gate_sigmoid * up_proj).astype(bf16)

    down_far_aside, down_send = at.far_part(cot_rows, hidden, 3)
    down_far_keep, down_send = at.far_part(cot_rows, after(hidden, down_send), 2)
    down_send, down_side = together(down_send, down_side)
    down_near = after(down_near, down_side)
    down_far = at.swap_core(down_side)
    down_far_aside = after(down_far_aside, down_side)
    down_grad_side = at.aside_part(cot_rows, hidden, down_far_aside)
    down_grad_aside = at.swap_side(down_grad_side)
    down_near, down_far = after(down_near, down_grad_side), after(down_far, down_grad_side)
    down_full = jnp.concatenate([down_here, down_side, down_near, down_far], axis=0)
    hidden_grad = plain_product(cot_rows, down_full)
    gate_grad = (
        hidden_grad * up_proj * gate_sigmoid * (1.0 + gate_proj * (1.0 - gate_sigmoid))
    ).astype(bf16)
    up_grad = (hidden_grad * gate_proj * gate_sigmoid).astype(bf16)

    def back_ffn(one, two, features=slice(None)):
        return cols_product(one, gate_full[features]) + cols_product(two, up_full[features])

    gate_far_aside, gate_send = at.far_part_two(ffn_in, gate_grad)
    gate_other, up_other = after(gate_grad[local_rows:], gate_send), up_grad[local_rows:]
    ffn_sends = [back_ffn(gate_other, up_other, slice(0, half)).astype(bf16)]
    gate_other, up_other = after(gate_other, ffn_sends[0]), after(up_other, ffn_sends[0])
    ffn_sends.append(back_ffn(gate_other, up_other, slice(half, D)).astype(bf16))
    ffn_sent = [at.swap_tensor(send) for send in ffn_sends]
    gate_far_aside = after(gate_far_aside, ffn_sends[1])
    gate_grad_side = at.aside_part(ffn_in, gate_grad, gate_far_aside)
    gate_grad_aside = at.swap_side(gate_grad_side)
    ffn_part = cols_product(after(gate_grad[:local_rows], gate_grad_side), gate_full)
    ffn_part, down_grad_aside = together(ffn_part, down_grad_aside)
    down_far_keep = after(down_far_keep, ffn_part)
    down_last = at.near_part(cot_rows, hidden, down_far_keep, down_grad_aside)
    grad_down = at.scatter_upper(down_last)
    ffn_part = ffn_part + cols_product(after(up_grad[:local_rows], down_last), up_full)
    gate_far_keep, gate_send = at.far_part(ffn_in, after(gate_grad, ffn_part), 2)
    ffn_sent = together(after(ffn_sent[0], gate_send), ffn_sent[1])
    ffn_in_grad = ffn_part + jnp.concatenate(ffn_sent, axis=1).astype(f32)
    residual_grad = cot_rel.astype(f32) + norm_back(
        residual, inv_second, ffn_gain_row, ffn_in_grad
    )

    branch_own = residual_grad.astype(bf16)
    branch_sent = at.swap_tensor(branch_own)
    up_far_aside, up_send = at.far_part_two(ffn_in, after(up_grad, branch_own))
    up_far_keep, up_send = at.far_part(ffn_in, after(up_grad, up_send), 2)
    branch = jnp.concatenate([branch_own, after(branch_sent, up_send)], axis=0)
    vec_two = plain_product(branch, out_full)
    vec_grad = at.in_order(vec_two[:local_rows], vec_two[local_rows:])
    vec_grad, gate_grad_aside = together(vec_grad, gate_grad_aside)
    up_far_aside = after(up_far_aside, gate_grad_aside)
    up_grad_side = at.aside_part(ffn_in, up_grad, up_far_aside)
    up_grad_aside = at.swap_side(up_grad_side)
    gate_far_keep = after(gate_far_keep, up_grad_side)
    gate_last = at.near_part(ffn_in, gate_grad, gate_far_keep, gate_grad_aside)
    grad_gate = at.scatter_upper(gate_last)
    queries_grad, kv_grad, head_sums = attend_back(
        queries,
        keys_values,
        lam_vec,
        head_gain_row,
        after(vec_grad, gate_last),
        heads_out,
        lse,
        prompt_spots,
        bounds,
        prompt_part,
        (0, heads),
        (),
    )
    queries_grad, kv_grad, head_sums, grad_down = together(
        queries_grad, kv_grad, head_sums, grad_down
    )
    queries_grad = queries_grad.T

    quarter = prompt_len // 4

    def prompt_rows(part):
        return kv_grad[part * quarter : (part + 1) * quarter]

    prompt_send = prompt_rows(3)
    prompt_far_aside = at.swap_core(prompt_send)
    prompt_keep = after(prompt_rows(2), prompt_send)
    prompt_far_keep = at.swap_core(prompt_keep)
    kv_far_aside, kv_send = at.far_part(normed_keys, after(kv_grad, prompt_keep), 3)
    kv_send, up_far_keep, up_grad_aside = together(kv_send, up_far_keep, up_grad_aside)
    prompt_far_aside = after(prompt_far_aside, up_grad_aside)
    prompt_side = (prompt_rows(1).astype(f32) + prompt_far_aside.astype(f32)).astype(bf16)
    prompt_aside = at.swap_side(prompt_side)
    up_last = at.near_part(ffn_in, after(up_grad, prompt_side), up_far_keep, up_grad_aside)
    up_last, grad_gate = together(up_last, grad_gate)
    grad_up = at.scatter_upper(up_last)
    kv_far_keep, kv_send = at.far_part(normed_keys, after(kv_grad, up_last), 2)
    kv_far_aside = after(kv_far_aside, kv_send)
    kv_grad_side = at.aside_part(normed_keys, kv_grad, kv_far_aside)
    kv_grad_aside = at.swap_side(kv_grad_side)
    q_far_aside, q_send = at.far_part(normed, after(queries_grad, kv_grad_side), 3)
    q_far_keep, q_send = at.far_part(normed, after(queries_grad, q_send), 2)
    out_far_aside, out_send_grad = at.far_part(branch, after(attn_two, q_send), 3)
    out_far_keep, out_send_grad = at.far_part(branch, after(attn_two, out_send_grad), 2)
    hidden_late = after(hidden, out_send_grad)
    output_part = cols_product(hidden_late[:local_rows], down_full)
    prompt_far_keep, prompt_aside = together(after(prompt_far_keep, output_part), prompt_aside)
    prompt_last = (
        prompt_rows(0).astype(f32) + prompt_far_keep.astype(f32) + prompt_aside.astype(f32)
    ).astype(bf16)
    prompt_grad = at.scatter_upper(prompt_last)
    q_far_aside = after(q_far_aside, prompt_last)
    q_grad_side = at.aside_part(normed, queries_grad, q_far_aside)
    q_grad_aside = at.swap_side(q_grad_side)
    out_far_aside = after(out_far_aside, q_grad_side)
    out_grad_side = at.aside_part(branch, attn_two, out_far_aside)
    out_grad_aside = at.swap_side(out_grad_side)
    output_send = cols_product(after(hidden_late, out_grad_side)[local_rows:], down_full).astype(bf16)
    output_sent = at.swap_tensor(output_send)
    kv_far_keep, kv_grad_aside = together(after(kv_far_keep, output_send), kv_grad_aside)
    kv_last = at.near_part(normed_keys, kv_grad, kv_far_keep, kv_grad_aside)
    grad_kv = at.scatter_upper(kv_last)
    output_sent, grad_up, q_far_keep = together(after(output_sent, kv_last), grad_up, q_far_keep)
    q_far_keep, q_grad_aside = together(q_far_keep, q_grad_aside)
    q_last = at.near_part(normed, queries_grad, q_far_keep, q_grad_aside)
    grad_q = at.scatter_upper(q_last)
    prompt_grad = after(prompt_grad, q_last)
    here_grad = jnp.concatenate([prompt_grad, kv_grad[prompt_len:]], axis=0)

    def back_attn(half_of):
        return cols_product(half_of(queries_grad), q_full) + cols_product(
            half_of(here_grad), kv_full
        )

    normed_send = back_attn(at.other_half).astype(bf16)
    normed_sent = at.swap_tensor(normed_send)
    out_far_keep, out_grad_aside = together(after(out_far_keep, normed_send), out_grad_aside)
    out_last = at.near_part(branch, attn_two, out_far_keep, out_grad_aside)
    grad_out = at.scatter_upper(out_last)
    normed_part = back_attn(lambda rows: at.own_half(after(rows, out_last)))
    normed_grad = normed_part + normed_sent.astype(f32)
    inv_first = inv_rms(tokens_f32, norm_eps)
    tokens_grad = residual_grad + norm_back(tokens_f32, inv_first, attn_gain_row, normed_grad)
    tokens_grad = at.from_relative(tokens_grad.astype(bf16))
    output = at.from_relative((residual + (output_part + output_sent.astype(f32))).astype(bf16))

    def row_sum(grad, weight):
        return jnp.sum(grad.astype(f32) * weight.astype(f32), axis=1)

    head_sums = at.sum_small(jnp.concatenate([head_sums[:, 0], head_sums[:, 1]], axis=1))
    head_gain_sum, lam_sum = head_sums[:, :DV], head_sums[:, DV]
    head_rows = head_gain.shape[0]
    grad_head_gain = lax.dynamic_slice_in_dim(head_gain_sum.T, at.index * head_rows, head_rows, 0)
    one_scale, two_scale = lam_sum * first_exp, -lam_sum * second_exp
    grad_q = grad_q.astype(f32)
    grad_kv = grad_kv.astype(f32).reshape(shard_rows, heads, -1)
    grad_k = grad_kv[:, :, : 2 * DK].reshape(shard_rows, -1)
    grad_v = grad_kv[:, :, 2 * DK :].reshape(shard_rows, -1)
    attn_gain_part = row_sum(grad_q, q_weight) + row_sum(grad_k, k_weight) + row_sum(grad_v, v_weight)
    ffn_gain_part = row_sum(grad_gate, gate_weight) + row_sum(grad_up, up_weight)
    attn_gain_sum = attn_gain_part + at.swap_tensor(attn_gain_part)
    ffn_gain_sum = ffn_gain_part + at.swap_tensor(ffn_gain_part)
    return (
        output,
        tokens_grad,
        grad_q,
        grad_k,
        grad_v,
        after(grad_out, attn_gain_sum).astype(f32),
        attn_gain_sum / attn_gain.astype(f32),
        grad_head_gain,
        one_scale * lam_k1.astype(f32),
        one_scale * lam_q1.astype(f32),
        two_scale * lam_k2.astype(f32),
        two_scale * lam_q2.astype(f32),
        grad_gate.astype(f32),
        grad_up.astype(f32),
        grad_down.astype(f32),
        ffn_gain_sum / ffn_gain.astype(f32),
    )


def solution(mesh):
    rows = P(("dp", "tensor"), None)
    both = P("dp", "tensor")
    placed = (
        (rows, rows, P("dp", None))
        + (both,) * 4
        + (P("dp"),)
        + (both,) * 5
        + (both,) * 3
        + (P("dp"),)
    )
    return jax.shard_map(
        per_device,
        mesh=mesh,
        in_specs=placed,
        out_specs=(rows, rows)
        + (both,) * 4
        + (P("dp"),)
        + (both,) * 5
        + (both,) * 3
        + (P("dp"),),
        check_vma=False,
    )
```
